32 devices in a mesh: rep: 4 (over y, core), fsdp: 8 (over z, x).
Axes of the slice: x: 2, y: 2, z: 4, core: 2. Of those that a mesh axis runs over, the one named last changes fastest.
Arguments:
- layer_input: bfloat16 [64, 512, 768], P(('rep', 'fsdp')), may hold values from -6 to 6
- masked: int32 [64, 512], P(('rep', 'fsdp')), may hold values 0 or 1
- replaced: int32 [64, 512], P(('rep', 'fsdp')), may hold values 0 or 1
- lengths: int32 [64], P(('rep', 'fsdp')), may hold values from 256 to 512
- w_qkv: bfloat16 [768, 2304], P('fsdp'), may hold values from -0.21875 to 0.21875
- b_q: bfloat16 [768], P('fsdp'), may hold values from -3 to 3
- b_v: bfloat16 [768], P('fsdp'), may hold values from -3 to 3
- w_out: bfloat16 [768, 768], P('fsdp'), may hold values from -0.875 to 0.875
- b_out: bfloat16 [768], P('fsdp'), may hold values from -3 to 3
- gain1: bfloat16 [768], P('fsdp'), may hold values from 0.25 to 1.75
- shift1: bfloat16 [768], P('fsdp'), may hold values from -3 to 3
- mask_vec: bfloat16 [768], P('fsdp'), may hold values from -4 to 4
- repl_vec: bfloat16 [768], P('fsdp'), may hold values from -4 to 4
- w_in: bfloat16 [768, 3072], P('fsdp'), may hold values from -0.21875 to 0.21875
- b_in: bfloat16 [3072], P('fsdp'), may hold values from -3 to 3
- w_down: bfloat16 [3072, 768], P('fsdp'), may hold values from -0.109375 to 0.109375
- b_down: bfloat16 [768], P('fsdp'), may hold values from -3 to 3
- gain2: bfloat16 [768], P('fsdp'), may hold values from 0.25 to 1.75
- shift2: bfloat16 [768], P('fsdp'), may hold values from -3 to 3
- cotangent: bfloat16 [64, 512, 768], P(('rep', 'fsdp')), may hold values from -6 to 6
Outputs:
- layer_output: bfloat16 [64, 512, 768], P(('rep', 'fsdp'))
- grad_input: bfloat16 [64, 512, 768], P(('rep', 'fsdp'))
- grad_w_qkv: float32 [768, 2304], P('fsdp')
- grad_b_q: float32 [768], P('fsdp')
- grad_b_v: float32 [768], P('fsdp')
- grad_w_out: float32 [768, 768], P('fsdp')
- grad_b_out: float32 [768], P('fsdp')
- grad_gain1: float32 [768], P('fsdp')
- grad_shift1: float32 [768], P('fsdp')
- grad_mask_vec: float32 [768], P('fsdp')
- grad_repl_vec: float32 [768], P('fsdp')
- grad_w_in: float32 [768, 3072], P('fsdp')
- grad_b_in: float32 [3072], P('fsdp')
- grad_w_down: float32 [3072, 768], P('fsdp')
- grad_b_down: float32 [768], P('fsdp')
- grad_gain2: float32 [768], P('fsdp')
- grad_shift2: float32 [768], P('fsdp')
The draws below stay inside these ranges and needn't reach their ends.
All inputs are finite; a program needn't handle non-finite values. No bound on the sum of `masked` or of `replaced` on one device may be relied on, other than what follows from the above.
Results may differ from the reference program's by a relative error of at most 0.018.
Values may be sent and summed in bfloat16 or wider, within the bound.
No kernel may reach another device: no remote copies, remote signals or barrier semaphores. Data moves between devices by JAX's collectives and lax.ppermute only.
A program may use at most 192 MiB of HBM per device.

```python
import jax
import jax.numpy as jnp
from jax import lax

D = 768
HEADS = 12
HEAD = 64
FF = 3072
SEQ = 512
DOCS = 64


def set_ends(values, own_key, smallest, largest):
    dims = values.shape
    spot = [jax.random.randint(jax.random.fold_in(own_key, axis), (), 0, dims[axis]) for axis in range(len(dims))]
    values = values.at[tuple(spot)].set(smallest)
    longest = dims.index(max(dims))
    spot[longest] = (spot[longest] + 1) % dims[longest]
    return values.at[tuple(spot)].set(largest)


def block_scale(key, dims, split, least, high):
    def one(dim, parts):
        heights = jax.random.uniform(jax.random.fold_in(jax.random.fold_in(key, 6), dim), (parts,), jnp.float32, least / len(split), high / len(split))
        return jnp.repeat(jnp.exp(heights), dims[dim] // parts).reshape((-1,) + (1,) * (len(dims) - dim - 1))

    level = one(*split[0])
    for cut in split[1:]:
        level = level * one(*cut)
    return level


def bell_draw(key, extent, width, bound, pieces=(), held_as=jnp.bfloat16):
    entries = width * jax.random.normal(key, extent, jnp.float32)
    if pieces:
        entries = entries * block_scale(key, extent, pieces, -0.22, 0.18)
    return jnp.clip(entries, -bound, bound).astype(held_as)


def setup_inputs(seed: int = 0) -> dict:
    seeds = jax.random.split(jax.random.key(seed), 21)
    layer_input = bell_draw(seeds[0], (DOCS, SEQ, D), 1.0, 6.0, ((0, 32),))
    masked = set_ends((jax.random.randint(seeds[1], (DOCS, SEQ), 0, 20) < 3).astype(jnp.int32), jax.random.fold_in(seeds[1], 1), 0, 1)
    replaced = set_ends((jax.random.randint(seeds[2], (DOCS, SEQ), 0, 20) < 3).astype(jnp.int32), jax.random.fold_in(seeds[2], 1), 0, 1)
    lengths = set_ends(jax.random.randint(seeds[3], (DOCS,), SEQ // 2, SEQ + 1), jax.random.fold_in(seeds[3], 1), SEQ // 2, SEQ).astype(jnp.int32)
    w_qkv = bell_draw(seeds[4], (D, 3 * D), D ** -0.5, 0.21875, ((0, 8),))
    b_q = bell_draw(seeds[5], (D,), 0.5, 3.0, ((0, 8),))
    b_v = bell_draw(seeds[6], (D,), 0.5, 3.0, ((0, 8),))
    w_out = bell_draw(seeds[7], (D, D), (D // 16) ** -0.5, 0.875, ((0, 8),))
    b_out = bell_draw(seeds[8], (D,), 0.5, 3.0, ((0, 8),))
    gain1 = jnp.clip(1.0 + 0.15 * jax.random.normal(seeds[9], (D,), jnp.float32), 0.25, 1.75).astype(jnp.bfloat16)
    shift1 = bell_draw(seeds[10], (D,), 0.5, 3.0, ((0, 8),))
    mask_vec = bell_draw(seeds[11], (D,), 1.0, 4.0, ((0, 8),))
    repl_vec = bell_draw(seeds[12], (D,), 1.0, 4.0, ((0, 8),))
    w_in = bell_draw(seeds[13], (D, FF), D ** -0.5, 0.21875, ((0, 8),))
    b_in = bell_draw(seeds[14], (FF,), 0.5, 3.0, ((0, 8),))
    w_down = bell_draw(seeds[15], (FF, D), FF ** -0.5, 0.109375, ((0, 8),))
    b_down = bell_draw(seeds[16], (D,), 0.5, 3.0, ((0, 8),))
    gain2 = jnp.clip(1.0 + 0.15 * jax.random.normal(seeds[17], (D,), jnp.float32), 0.25, 1.75).astype(jnp.bfloat16)
    shift2 = bell_draw(seeds[18], (D,), 0.5, 3.0, ((0, 8),))
    cotangent = bell_draw(seeds[19], (DOCS, SEQ, D), 1.0, 6.0, ((0, 32),))
    return dict(layer_input=layer_input, masked=masked, replaced=replaced, lengths=lengths, w_qkv=w_qkv, b_q=b_q, b_v=b_v, w_out=w_out, b_out=b_out, gain1=gain1, shift1=shift1, mask_vec=mask_vec, repl_vec=repl_vec, w_in=w_in, b_in=b_in, w_down=w_down, b_down=b_down, gain2=gain2, shift2=shift2, cotangent=cotangent)


@jax.custom_vjp
def low(v):
    return lax.optimization_barrier(v.astype(jnp.bfloat16)).astype(jnp.float32)

@jax.custom_vjp
def low_back(v):
    return v

def low_keep(v):
    return (low(v), None)

def low_pass(kept, grad):
    return (grad,)

def back_keep(v):
    return (v, None)

def back_low(kept, grad):
    return (low(grad),)
low.defvjp(low_keep, low_pass)
low_back.defvjp(back_keep, back_low)
epsilon = 1e-05
highest = lax.Precision.HIGHEST

def layer_norm(resid, gain, shift):
    center = resid - lax.optimization_barrier(jnp.mean(resid, axis=-1, keepdims=True))
    inv_std = lax.rsqrt(lax.optimization_barrier(jnp.mean(center * center, axis=-1, keepdims=True)) + epsilon)
    return center * inv_std * gain + shift

def doc_layer(param_set, tokens, mask_flag, repl_flag, length):
    w_qkv, b_q, b_v, w_out, b_out, gain1, shift1, mask_vec, repl_vec, w_in, b_in, w_down, b_down, gain2, shift2 = param_set
    embed = tokens + mask_flag[:, None] * mask_vec + repl_flag[:, None] * repl_vec
    embed_low = low(embed)
    projected = jnp.dot(embed_low, w_qkv, precision=highest) + jnp.concatenate([b_q, jnp.zeros_like(b_q), b_v])
    query = low_back(low(projected[:, :D])).reshape(SEQ, HEADS, HEAD)
    keys = low_back(low(projected[:, D:2 * D])).reshape(SEQ, HEADS, HEAD)
    values = low_back(low(projected[:, 2 * D:])).reshape(SEQ, HEADS, HEAD)
    scores = low_back(jnp.einsum('qhd,khd->hqk', query, keys, precision=highest) * HEAD ** (-0.5))
    allowed = jnp.arange(SEQ) < length
    probs = low(jax.nn.softmax(jnp.where(allowed[None, None, :], scores, -1e+30), axis=-1))
    context = low_back(low(jnp.einsum('hqk,khd->qhd', probs, values, precision=highest).reshape(SEQ, D)))
    attended = low_back(jnp.dot(context, w_out, precision=highest) + b_out)
    normed = layer_norm(embed + attended, gain1, shift1)
    hidden = low_back(jnp.dot(low(normed), w_in, precision=highest) + b_in)
    activated = low(jax.nn.gelu(hidden, approximate=False))
    branch = low_back(jnp.dot(activated, w_down, precision=highest) + b_down)
    return layer_norm(normed + branch, gain2, shift2)

def reference(layer_input, masked, replaced, lengths, w_qkv, b_q, b_v, w_out, b_out, gain1, shift1, mask_vec, repl_vec, w_in, b_in, w_down, b_down, gain2, shift2, cotangent):
    param_set = tuple((weight.astype(jnp.float32) for weight in (w_qkv, b_q, b_v, w_out, b_out, gain1, shift1, mask_vec, repl_vec, w_in, b_in, w_down, b_down, gain2, shift2)))

    def per_doc(running, operands):
        tokens, mask_row, repl_row, length, cot_row = operands
        output, pullback = jax.vjp(lambda params_in, inputs: doc_layer(params_in, inputs, mask_row.astype(jnp.float32), repl_row.astype(jnp.float32), length), param_set, tokens)
        grad_params, grad_tokens = pullback(cot_row)
        running = jax.tree.map(lambda left, right: left + right, running, grad_params)
        return (running, (output.astype(jnp.bfloat16), grad_tokens.astype(jnp.bfloat16)))
    initial = jax.tree.map(jnp.zeros_like, param_set)
    totals, (layer_output, grad_input) = lax.scan(per_doc, initial, (layer_input.astype(jnp.float32), masked, replaced, lengths, cotangent.astype(jnp.float32)))
    return (layer_output, grad_input, totals[0], totals[1], totals[2], totals[3], totals[4], totals[5], totals[6], totals[7], totals[8], totals[9], totals[10], totals[11], totals[12], totals[13], totals[14])
```

```python
import functools

import jax
import jax.numpy as jnp
from jax import lax
from jax.experimental import pallas as pl
from jax.experimental.pallas import tpu as pltpu
from jax.sharding import PartitionSpec as P

HEADS = 12
AXES = ("rep", "fsdp")
EPSILON = 1e-05
TILE = 256
VMEM_BYTES = 60 * 1024 * 1024
STEEP = 0.28
TAIL = (0.11652066258099363, 0.06749752053058514, 0.2689081593014359, -0.23699088133158833, 0.38987234732742354, -0.10580781763400933)


def wiring(n_fsdp):
    n_z = n_fsdp // 2

    def pairs(move):
        out = []
        for i in range(4 * n_fsdp):
            y, c, z, x = i // (2 * n_fsdp), i // n_fsdp % 2, i % n_fsdp // 2, i % 2
            y2, c2, z2, x2 = move(y, c, z, x)
            out.append((i, ((y2 * 2 + c2) * n_z + z2) * 2 + x2))
        return out

    return {
        "core": pairs(lambda y, c, z, x: (y, 1 - c, z, x)),
        "first": pairs(lambda y, c, z, x: (1 - y, c, z, x) if c == 0 else (y, c, z, 1 - x)),
        "second": pairs(lambda y, c, z, x: (y, c, z, 1 - x) if c == 0 else (1 - y, c, z, x)),
        "z": [pairs(lambda y, c, z, x, m=m: (y, c, z ^ m, x)) for m in range(1, n_z)],
        "rep": [pairs(lambda y, c, z, x, m=m: (y ^ (m // 2), c ^ (m % 2), z, x)) for m in (1, 2, 3)],
        "fsdp_bits": [
            [(i, i ^ (1 << b)) for i in range(4 * n_fsdp)] for b in range(n_fsdp.bit_length() - 1)
        ],
        "rep_bits": [[(i, i ^ (n_fsdp << b)) for i in range(4 * n_fsdp)] for b in (0, 1)],
    }


def send(value, pairs):
    return lax.ppermute(value, AXES, pairs)


def tie(*values):
    return lax.optimization_barrier(values)


def pick(value, axis, index):
    return lax.dynamic_index_in_dim(value, index, axis, keepdims=False)


def add_low(left, right):
    return (left.astype(jnp.float32) + right.astype(jnp.float32)).astype(jnp.bfloat16)


def flip_by(value, axis, mask):
    for bit in range(value.shape[axis].bit_length() - 1):
        shape = value.shape
        cut = value.reshape(shape[:axis] + (-1, 2, 1 << bit) + shape[axis + 1 :])
        value = jnp.where(mask >> bit & 1 == 1, jnp.flip(cut, axis + 1), cut).reshape(shape)
    return value


def gather_z(piece, wires):
    return jnp.concatenate([piece] + [send(piece, pairs) for pairs in wires["z"]])


def grow(value, got):
    return jnp.concatenate([value, got])


def sides_of(half, other, at, n_z):
    rows = half.shape[0] // (4 * n_z)
    if in_blocks(rows):
        return half, other
    y, z, x = at[0], at[2], at[3]
    out = []
    for side, source in ((0, half), (1, other)):
        blocks = source.reshape(2, 2, n_z, rows, -1)
        blocks = jnp.where(at[1] ^ side == 0, blocks, blocks.swapaxes(0, 1))
        blocks = flip_by(flip_by(flip_by(blocks, 0, x), 1, y), 2, z)
        out.append(blocks.transpose(2, 0, 1, 3, 4).reshape(half.shape))
    return tuple(out)


def in_blocks(rows):
    return rows % 16 == 0


def arrival_of(slot, at, side, n_z):
    y, c, z, x = at[0], at[1] ^ side, at[2], at[3]
    by_y, by_x, by_z = slot % 2 ^ y, slot // 2 % 2 ^ x, slot // 4 ^ z
    return jnp.where(c == 0, by_x * 2 + by_y, by_y * 2 + by_x) * n_z + by_z


def sum_core(keep, got, at, n_z):
    y, c, x = at[0], at[1], at[3]
    summed = add_low(keep, got).reshape(n_z, 2, 2, -1, keep.shape[1])
    away = jnp.where(c == 0, pick(summed, 1, 1 - x), pick(summed, 2, 1 - y))
    return jnp.where(c == 0, pick(summed, 1, x), pick(summed, 2, y)), away


def sum_second(keep, got, at):
    spot = jnp.where(at[1] == 0, at[0], at[3])
    summed = add_low(keep, got)
    return pick(summed, 1, spot), pick(summed, 1, 1 - spot)


def sum_first(keep, got, at):
    summed = add_low(keep, got)
    return pick(summed, 0, at[2]), [pick(summed, 0, at[2] ^ m) for m in range(1, summed.shape[0])]


def sum_z(keep, gots):
    total = keep.astype(jnp.float32)
    for got in gots:
        total = total + got.astype(jnp.float32)
    return total.astype(jnp.bfloat16)


def blocks_of(owned, gots, at):
    quarters = jnp.stack([owned] + list(gots))
    return [
        [pick(quarters, 0, (at[0] ^ row) * 2 + (at[1] ^ col)).astype(jnp.float32) for col in (0, 1)] for row in (0, 1)
    ]


def send_all(values, wires):
    return [send(value, pairs) for value, pairs in zip(values, wires, strict=True)]


def dot(left, right):
    return lax.dot_general(left, right, (((1,), (0,)), ((), ())), preferred_element_type=jnp.float32)


def dot_cols(left, right):
    return lax.dot_general(left, right, (((1,), (1,)), ((), ())), preferred_element_type=jnp.float32)


def dot_rows(left, right):
    return lax.dot_general(left, right, (((0,), (0,)), ((), ())), preferred_element_type=jnp.float32)


def call(kernel, grid, in_specs, out_specs, out_shape, scratch=(), flops=0, prefetch=0, aliases=None, name=None):
    sizes = [s.size * s.dtype.itemsize for s in jax.tree.leaves(out_shape)]
    return pl.pallas_call(
        kernel,
        grid_spec=pltpu.PrefetchScalarGridSpec(
            num_scalar_prefetch=prefetch, grid=grid, in_specs=in_specs, out_specs=out_specs, scratch_shapes=scratch
        ),
        out_shape=out_shape,
        compiler_params=pltpu.CompilerParams(
            dimension_semantics=("arbitrary",) * len(grid), vmem_limit_bytes=VMEM_BYTES
        ),
        cost_estimate=pl.CostEstimate(flops=flops, bytes_accessed=2 * sum(sizes), transcendentals=0),
        input_output_aliases=aliases or {},
        name=name,
    )


def whole(shape):
    return pl.BlockSpec(shape, lambda i, *_: (0,) * len(shape))


def tiles(width):
    return pl.BlockSpec((TILE, width), lambda i, *_: (i, 0))


ANY = pl.BlockSpec(memory_space=pl.ANY)


def load(at_ref, sides, n_z, targets, relative=False):
    for side, ref in enumerate(sides):
        half = side if relative else jnp.bitwise_xor(at_ref[1], side)
        rows = ref.shape[0] // (4 * n_z)
        for first, cols, into, sem in targets:
            lanes = pl.ds(pl.multiple_of(half * cols, 128), cols)
            if not in_blocks(rows):
                pltpu.make_async_copy(ref.at[:, pl.ds(first, cols)], into.at[:, lanes], sem).start()
                continue
            for slot in range(4 * n_z):
                block = arrival_of(slot, at_ref, side, n_z)
                pltpu.make_async_copy(
                    ref.at[pl.ds(pl.multiple_of(block * rows, rows), rows), pl.ds(first, cols)],
                    into.at[pl.ds(slot * rows, rows), lanes],
                    sem,
                ).start()


def loaded(array, sem):
    pltpu.make_async_copy(array, array, sem).wait()


def qkv_kernel(n_z, at_ref, flag_ref, x_ref, row_ref, bias_ref, scale_ref, own_ref, other_ref, qkv_ref, low_ref, w_ref, sem):
    @pl.when(pl.program_id(0) == 0)
    def _():
        load(at_ref, (own_ref, other_ref), n_z, [(0, own_ref.shape[1], w_ref, sem)])
        loaded(w_ref, sem)

    embed_low = (x_ref[...].astype(jnp.float32) + dot_rows(flag_ref[...], row_ref[...])).astype(jnp.bfloat16)
    low_ref[...] = embed_low
    out = ((dot(embed_low, w_ref[...]) + bias_ref[...]) * scale_ref[...]).astype(jnp.bfloat16)
    cols = out.shape[1] // 2
    qkv_ref[0] = out[:, :cols]
    qkv_ref[1] = out[:, cols:]


def project(at, flags, x, rows, bias, scale, sides, n_z):
    count, width = x.shape
    cols = sides[0].shape[1]
    return call(
        functools.partial(qkv_kernel, n_z),
        (count // TILE,),
        [
            pl.BlockSpec((16, TILE), lambda i, *_: (0, i)),
            tiles(width),
            whole((16, width)),
            whole((1, 2 * cols)),
            whole((1, 2 * cols)),
            ANY,
            ANY,
        ],
        [pl.BlockSpec((2, TILE, cols), lambda i, *_: (0, i, 0)), tiles(width)],
        [jax.ShapeDtypeStruct((2, count, cols), jnp.bfloat16), jax.ShapeDtypeStruct((count, width), jnp.bfloat16)],
        [pltpu.VMEM((width, 2 * cols), jnp.bfloat16), pltpu.SemaphoreType.DMA],
        4 * count * width * cols,
        1,
        name="project",
    )(at, flags, x, rows, bias, scale, *sides)


def attend_kernel(n_pair, len_ref, q_ref, k_ref, v_ref, *refs):
    ctx_ref, inv_ref, p_ref = refs[-3:]
    length = len_ref[pl.program_id(0) // n_pair]
    query, keys, values = q_ref[...], k_ref[...], v_ref[...]
    lane = lax.broadcasted_iota(jnp.int32, query.shape, 1)
    row = lax.broadcasted_iota(jnp.int32, query.shape, 0)
    unused = jnp.where(row >= length, -1e30, 0.0).astype(jnp.bfloat16)
    zero, one = jnp.zeros_like(query), jnp.ones_like(query)
    low = lane < 64
    parts = []
    for head in (0, 1):
        mine = low if head == 0 else ~low
        spare = lane == 64 - 64 * head
        scores = dot_cols(
            jnp.where(mine, query, jnp.where(spare, one, zero)), jnp.where(mine, keys, jnp.where(spare, unused, zero))
        )
        expo = jnp.exp(scores - jnp.max(scores, axis=1, keepdims=True)).astype(jnp.bfloat16)
        p_ref[head] = expo
        parts.append(dot(expo, jnp.where(mine, values, one)))
    inv = 1.0 / pltpu.roll(jnp.where(low, parts[1], parts[0]), 64, axis=1)
    inv_ref[...] = inv
    ctx_ref[...] = (jnp.where(low, parts[0], parts[1]) * inv).astype(jnp.bfloat16)


def attend(half, lengths, qkv, before):
    docs = lengths.shape[0]
    count, cols = qkv.shape[1:]
    seq, n_pair = count // docs, cols // 384

    def part(which):
        return pl.BlockSpec((None, seq, 128), lambda i, *_: (half, i // n_pair, which * n_pair + i % n_pair))

    def out():
        return pl.BlockSpec((seq, 128), lambda i, *_: (i // n_pair, half * n_pair + i % n_pair))

    return call(
        functools.partial(attend_kernel, n_pair),
        (docs * n_pair,),
        [part(0), part(1), part(2)] + [ANY] * len(before),
        [out(), out(), pl.BlockSpec((None, None, 2, seq, seq), lambda i, *_: (half, i, 0, 0, 0))],
        [
            jax.ShapeDtypeStruct((count, 2 * cols // 3), jnp.bfloat16),
            jax.ShapeDtypeStruct((count, 2 * cols // 3), jnp.float32),
            jax.ShapeDtypeStruct((2, docs * n_pair, 2, seq, seq), jnp.bfloat16),
        ],
        flops=docs * n_pair * 2 * seq * seq * 256 * 4,
        prefetch=1,
        aliases={4 + i: i for i in range(len(before))},
        name="attend",
    )(lengths, qkv, qkv, qkv, *before)


def norm(resid):
    center = resid - jnp.mean(resid, axis=1, keepdims=True)
    inv = lax.rsqrt(jnp.mean(center * center, axis=1, keepdims=True) + EPSILON)
    return center * inv, inv


def norm_back(grad, normal, inv, gain):
    scaled = grad * gain
    return inv * (
        scaled
        - jnp.mean(scaled, axis=1, keepdims=True)
        - normal * jnp.mean(scaled * normal, axis=1, keepdims=True)
    )


def gelu_parts(u):
    expo = jnp.exp(u * u * -0.5)
    t = 1.0 / (1.0 + STEEP * jnp.abs(u))
    poly = TAIL[5]
    for coef in TAIL[4::-1]:
        poly = poly * t + coef
    tail = expo * (t * poly)
    phi = jnp.where(u >= 0, 1.0 - tail, tail)
    return phi, phi + u * (expo * 0.3989422804014327)


def sum_rows(value):
    return jnp.sum(value, axis=0, keepdims=True)


def ffn_kernel(
    n_z,
    at_ref,
    flag_ref,
    x_ref,
    ctx_ref,
    cot_ref,
    row_ref,
    b_in_ref,
    mid_own,
    mid_other,
    down_own,
    down_other,
    out_ref,
    low_ref,
    act_ref,
    dbranch_ref,
    dhidden_ref,
    dattn_ref,
    dresid_ref,
    dctx_ref,
    sums_ref,
    in_sums_ref,
    wo_ref,
    wi_ref,
    wd_ref,
    slope_ref,
    sems,
):
    first = pl.program_id(0) == 0
    width = x_ref.shape[1]
    chunks = range(0, wi_ref.shape[1], width)

    @pl.when(first)
    def _():
        sums_ref[...] = jnp.zeros_like(sums_ref)
        in_sums_ref[...] = jnp.zeros_like(in_sums_ref)
        mid = (mid_own, mid_other)
        load(at_ref, mid, n_z, [(0, width // 2, wo_ref, sems.at[0])])
        load(at_ref, mid, n_z, [(width // 2, mid_own.shape[1] - width // 2, wi_ref, sems.at[1])])
        load(at_ref, (down_own, down_other), n_z, [(0, width // 2, wd_ref, sems.at[2])])
        loaded(wo_ref, sems.at[0])
        loaded(wi_ref, sems.at[1])
        loaded(wd_ref, sems.at[2])

    rows = row_ref[...].astype(jnp.float32)
    b_out, gain1, shift1, b_down, gain2, shift2 = (rows[i : i + 1] for i in range(2, 8))
    embed = x_ref[...].astype(jnp.float32) + dot_rows(flag_ref[...], row_ref[...])
    normal1, inv1 = norm(embed + dot(ctx_ref[...], wo_ref[...]) + b_out)
    normed = normal1 * gain1 + shift1
    normed_low = normed.astype(jnp.bfloat16)
    low_ref[...] = normed_low
    branch = normed + b_down
    for at in chunks:
        cols = slice(at, at + width)
        hidden = dot(normed_low, wi_ref[:, cols]) + b_in_ref[:, cols]
        phi, slope = gelu_parts(hidden)
        slope_ref[:, cols] = slope
        activated = (hidden * phi).astype(jnp.bfloat16)
        act_ref[:, cols] = activated
        branch = branch + dot(activated, wd_ref[cols, :])
    normal2, inv2 = norm(branch)
    out_ref[...] = (normal2 * gain2 + shift2).astype(jnp.bfloat16)
    grad = cot_ref[...].astype(jnp.float32)
    dresid2 = norm_back(grad, normal2, inv2, gain2)
    dbranch = dresid2.astype(jnp.bfloat16)
    dbranch_ref[...] = dbranch
    sums_ref[0:1] += sum_rows(grad * normal2)
    sums_ref[1:2] += sum_rows(grad)
    sums_ref[2:3] += sum_rows(dbranch.astype(jnp.float32))
    dnormed = dresid2
    for at in chunks:
        cols = slice(at, at + width)
        dhidden = (dot_cols(dbranch, wd_ref[cols, :]) * slope_ref[:, cols]).astype(jnp.bfloat16)
        dhidden_ref[:, cols] = dhidden
        in_sums_ref[0:1, cols] += sum_rows(dhidden.astype(jnp.float32))
        dnormed = dnormed + dot_cols(dhidden, wi_ref[:, cols])
    dresid1 = norm_back(dnormed, normal1, inv1, gain1)
    dattn = dresid1.astype(jnp.bfloat16)
    dresid_ref[...] = dresid1
    dattn_ref[...] = dattn
    sums_ref[3:4] += sum_rows(dnormed * normal1)
    sums_ref[4:5] += sum_rows(dnormed)
    sums_ref[5:6] += sum_rows(dattn.astype(jnp.float32))
    dctx_ref[...] = dot_cols(dattn, wo_ref[...]).astype(jnp.bfloat16)


def ffn(at, flags, x, ctx, cot, rows, b_in, mid, down, n_z):
    count, width = x.shape
    ff_width = b_in.shape[1]
    low = jax.ShapeDtypeStruct((count, width), jnp.bfloat16)
    wide = jax.ShapeDtypeStruct((count, ff_width), jnp.bfloat16)
    return call(
        functools.partial(ffn_kernel, n_z),
        (count // TILE,),
        [pl.BlockSpec((16, TILE), lambda i, *_: (0, i))]
        + [tiles(width)] * 3
        + [whole((16, width)), whole((1, ff_width))]
        + [ANY] * 4,
        [tiles(width)] * 2
        + [tiles(ff_width), tiles(width), tiles(ff_width)]
        + [tiles(width)] * 3
        + [whole((8, width)), whole((8, ff_width))],
        [low, low, wide, low, wide, low, jax.ShapeDtypeStruct((count, width), jnp.float32), low]
        + [jax.ShapeDtypeStruct((8, width), jnp.float32), jax.ShapeDtypeStruct((8, ff_width), jnp.float32)],
        [
            pltpu.VMEM((width, width), jnp.bfloat16),
            pltpu.VMEM((width, ff_width), jnp.bfloat16),
            pltpu.VMEM((ff_width, width), jnp.bfloat16),
            pltpu.VMEM((TILE, ff_width), jnp.float32),
            pltpu.SemaphoreType.DMA((3,)),
        ],
        4 * count * width * (width + 2 * ff_width),
        1,
        name="ffn",
    )(at, flags, x, ctx, cot, rows, b_in, *mid, *down)


def down_grad_kernel(at_ref, a_ref, b_ref, keep_ref, give_ref):
    cols = b_ref.shape[1] // 2
    mine, theirs = at_ref[1], 1 - at_ref[1]
    right = jnp.concatenate(
        [b_ref[:, pl.ds(pl.multiple_of(half * cols, 128), cols)] for half in (mine, theirs)], axis=1
    )
    grad = dot_rows(a_ref[...], right).astype(jnp.bfloat16)
    keep_ref[...] = grad[:, :cols]
    give_ref[...] = grad[:, cols:]


def down_grad(at, left, right):
    count, width = right.shape
    rows = left.shape[1]
    return call(
        down_grad_kernel,
        (rows // width,),
        [pl.BlockSpec((count, width), lambda i, *_: (0, i)), whole((count, width))],
        [pl.BlockSpec((width, width // 2), lambda i, *_: (i, 0))] * 2,
        [jax.ShapeDtypeStruct((rows, width // 2), jnp.bfloat16)] * 2,
        flops=2 * count * width * rows,
        prefetch=1,
        name="down_grad",
    )(at, left, right)


def in_grad_kernel(at_ref, a_ref, b_ref, give_ref, keep_ref):
    grad = dot_rows(a_ref[...], b_ref[...]).astype(jnp.bfloat16)

    @pl.when(pl.program_id(0) < 2)
    def _():
        give_ref[...] = grad

    @pl.when(pl.program_id(0) >= 2)
    def _():
        keep_ref[...] = grad


def in_grad(at, left, right):
    count, width = left.shape
    cols = right.shape[1] // 4
    return call(
        in_grad_kernel,
        (4,),
        [
            whole((count, width)),
            pl.BlockSpec((count, cols), lambda i, at_ref: (0, jnp.where(i < 2, 1 - at_ref[1], at_ref[1]) * 2 + i % 2)),
        ],
        [
            pl.BlockSpec((width, cols), lambda i, at_ref: (0, jnp.minimum(i, 1))),
            pl.BlockSpec((width, cols), lambda i, at_ref: (0, jnp.maximum(i - 2, 0))),
        ],
        [jax.ShapeDtypeStruct((width, 2 * cols), jnp.bfloat16)] * 2,
        flops=8 * count * width * cols,
        prefetch=1,
        name="in_grad",
    )(at, left, right)


def attend_back_kernel(n_pair, half_ref, q_ref, k_ref, v_ref, ctx_ref, inv_ref, p_ref, dctx_ref, out_ref):
    pair = pl.program_id(0) % n_pair
    query, keys, values = q_ref[...], k_ref[...], v_ref[...]
    lane = lax.broadcasted_iota(jnp.int32, query.shape, 1)
    low = lane < 64
    zero, one = jnp.zeros_like(query), jnp.ones_like(query)
    dctx = (dctx_ref[...].astype(jnp.float32) * inv_ref[...]).astype(jnp.bfloat16)
    product = dctx.astype(jnp.float32) * ctx_ref[...].astype(jnp.float32)
    grads = []
    for head in (0, 1):
        mine = low if head == 0 else ~low
        spare = lane == 64 - 64 * head
        fine = lane == 65 - 64 * head
        delta = jnp.sum(jnp.where(mine, product, 0.0), axis=1, keepdims=True)
        coarse = delta.astype(jnp.bfloat16)
        rest = (delta - coarse.astype(jnp.float32)).astype(jnp.bfloat16)
        left = jnp.where(mine, dctx, jnp.where(spare, -coarse, jnp.where(fine, -rest, zero)))
        expo = p_ref[head]
        dprobs = dot_cols(left, jnp.where(mine, values, jnp.where(spare | fine, one, zero)))
        dscores = (expo.astype(jnp.float32) * dprobs).astype(jnp.bfloat16)
        grads.append((dot(dscores, keys) * 0.125, dot_rows(dscores, query), dot_rows(expo, dctx)))
    third = out_ref.shape[1] // 3
    for which in range(3):
        grad = jnp.where(low, grads[0][which], grads[1][which]).astype(jnp.bfloat16)
        out_ref[:, pl.ds(pl.multiple_of(which * third + pair * 128, 128), 128)] = grad


def attend_back(half, docs, qkv, ctx, inv, expo, dctx):
    count, cols = qkv.shape[1:]
    seq, n_pair = count // docs, cols // 384

    def part(which):
        return pl.BlockSpec((None, seq, 128), lambda i, h: (h[0], i // n_pair, which * n_pair + i % n_pair))

    one = pl.BlockSpec((seq, 128), lambda i, h: (i // n_pair, h[0] * n_pair + i % n_pair))
    return call(
        functools.partial(attend_back_kernel, n_pair),
        (docs * n_pair,),
        [part(0), part(1), part(2), one, one]
        + [pl.BlockSpec((None, None, 2, seq, seq), lambda i, h: (h[0], i, 0, 0, 0)), one],
        pl.BlockSpec((seq, cols), lambda i, h: (i // n_pair, 0)),
        jax.ShapeDtypeStruct((count, cols), jnp.bfloat16),
        flops=docs * n_pair * 2 * seq * seq * 256 * 10,
        prefetch=1,
        name="attend_back",
    )(half, qkv, qkv, qkv, ctx, inv, expo, dctx)


def attn_grad_kernel(half_ref, ctx_ref, dattn_ref, low_ref, dqkv_ref, out_ref):
    cols = dattn_ref.shape[1]
    out_ref[:, :cols] = dot_rows(ctx_ref[...], dattn_ref[...]).astype(jnp.bfloat16)
    out_ref[:, cols:] = dot_rows(low_ref[...], dqkv_ref[...]).astype(jnp.bfloat16)


def attn_grad(half, ctx, dattn, low, dqkv):
    count, width = ctx.shape
    cols = width // 2 + dqkv.shape[1]
    return call(
        attn_grad_kernel,
        (1,),
        [
            whole((count, width)),
            pl.BlockSpec((count, width // 2), lambda i, h: (0, h[0])),
            whole((count, width)),
            whole(dqkv.shape),
        ],
        whole((width, cols)),
        jax.ShapeDtypeStruct((width, cols), jnp.bfloat16),
        flops=2 * count * width * cols,
        prefetch=1,
        name="attn_grad",
    )(half, ctx, dattn, low, dqkv)


def embed_grad_kernel(n_z, at_ref, flag_ref, dresid_ref, mine_ref, theirs_ref, own_ref, other_ref, grad_ref, sums_ref, bias_ref, w_ref, sem):
    cols = own_ref.shape[1]

    @pl.when(pl.program_id(0) == 0)
    def _():
        sums_ref[...] = jnp.zeros_like(sums_ref)
        bias_ref[...] = jnp.zeros_like(bias_ref)
        load(at_ref, (own_ref, other_ref), n_z, [(0, cols, w_ref, sem)], relative=True)
        loaded(w_ref, sem)

    mine, theirs = mine_ref[...], theirs_ref[...]
    dembed = dresid_ref[...] + dot_cols(mine, w_ref[:, :cols]) + dot_cols(theirs, w_ref[:, cols:])
    coarse = dembed.astype(jnp.bfloat16)
    grad_ref[...] = coarse
    rest = (dembed - coarse.astype(jnp.float32)).astype(jnp.bfloat16)
    sums_ref[...] += dot(flag_ref[...], coarse) + dot(flag_ref[...], rest)
    bias_ref[0:1] += sum_rows(mine.astype(jnp.float32))
    bias_ref[1:2] += sum_rows(theirs.astype(jnp.float32))


def embed_grad(at, flags, dresid, mine, theirs, sides, n_z):
    count, width = dresid.shape
    cols = mine.shape[1]
    return call(
        functools.partial(embed_grad_kernel, n_z),
        (count // TILE,),
        [pl.BlockSpec((16, TILE), lambda i, *_: (0, i)), tiles(width), tiles(cols), tiles(cols), ANY, ANY],
        [tiles(width), whole((16, width)), whole((8, cols))],
        [
            jax.ShapeDtypeStruct((count, width), jnp.bfloat16),
            jax.ShapeDtypeStruct((16, width), jnp.float32),
            jax.ShapeDtypeStruct((8, cols), jnp.float32),
        ],
        [pltpu.VMEM((width, 2 * cols), jnp.bfloat16), pltpu.SemaphoreType.DMA],
        4 * count * width * cols,
        1,
        name="embed_grad",
    )(at, flags, dresid, mine, theirs, *sides)


def body(
    layer_input,
    masked,
    replaced,
    lengths,
    w_qkv,
    b_q,
    b_v,
    w_out,
    b_out,
    gain1,
    shift1,
    mask_vec,
    repl_vec,
    w_in,
    b_in,
    w_down,
    b_down,
    gain2,
    shift2,
    cotangent,
):
    doc_count, seq_len, width = layer_input.shape
    tok_count = doc_count * seq_len
    n_fsdp = lax.axis_size("fsdp")
    n_z = n_fsdp // 2
    wires = wiring(n_fsdp)
    rep, own = lax.axis_index("rep"), lax.axis_index("fsdp")
    at = jnp.stack([rep // 2, rep % 2, own // 2, own % 2]).astype(jnp.int32)
    y, c = at[0], at[1]
    ff_width = w_in.shape[1]
    split = width // 2
    step = width // n_fsdp

    def quarter(weight):
        rows, cols = weight.shape[0] // 2, weight.shape[1] // 2
        return lax.dynamic_slice(weight, (y * rows, c * cols), (rows, cols))

    vectors = (mask_vec, repl_vec, b_out, gain1, shift1, b_down, gain2, shift2, b_q, b_v, b_in)
    packed = jnp.concatenate(vectors)[None]
    for pairs in wires["fsdp_bits"]:
        packed = jnp.concatenate([packed, send(packed, pairs)])
    packed = flip_by(packed, 0, own)
    rows = packed[:, : 10 * step].reshape(n_fsdp, 10, step).transpose(1, 0, 2).reshape(10, width)
    b_in = packed[:, 10 * step :].reshape(1, ff_width).astype(jnp.float32)
    b_qv = rows[8:].astype(jnp.float32)
    bias = jnp.concatenate(
        [piece for h in (0, split) for piece in (b_qv[0, h : h + split], jnp.zeros((split,)), b_qv[1, h : h + split])]
    )[None]
    scale = jnp.where(jnp.arange(6 * split) // split % 3 == 0, (width // HEADS) ** -0.5, 1.0).astype(jnp.float32)[None]
    rows = jnp.concatenate([rows, jnp.zeros((6, width), rows.dtype)])
    first_attn = jnp.concatenate([quarter(w_qkv[:, i * width : (i + 1) * width]) for i in range(3)], axis=1)
    first_mid = jnp.concatenate([quarter(w_out), quarter(w_in)], axis=1)
    first_down = quarter(w_down)

    flags = jnp.stack([masked.reshape(tok_count), replaced.reshape(tok_count)]).astype(jnp.bfloat16)
    flags = jnp.concatenate([flags, jnp.zeros((14, tok_count), jnp.bfloat16)])
    x = layer_input.reshape(tok_count, width)
    cot = cotangent.reshape(tok_count, width)
    attn = gather_z(first_attn, wires)
    first_mid, attn = tie(first_mid, attn)
    attn = grow(attn, send(attn, wires["first"]))
    mid = gather_z(first_mid, wires)
    first_down, mid = tie(first_down, mid)
    got_mid = send(mid, wires["first"])
    got_down = send_all([first_down] * (n_z - 1), wires["z"])
    attn = grow(attn, send(attn, wires["second"]))
    w_attn = sides_of(attn, send(attn, wires["core"]), at, n_z)

    qkv, embed_low = project(at, flags, x, rows, bias, scale, w_attn, n_z)
    qkv, got_mid, got_down = tie(qkv, got_mid, got_down)
    mid = grow(mid, got_mid)
    down = jnp.concatenate([first_down] + got_down)
    qkv, mid, down = tie(qkv, mid, down)
    got_mid = send(mid, wires["second"])
    got_down = send(down, wires["first"])
    part = attend(0, lengths, qkv, ())
    part, got_mid, got_down = tie(part, got_mid, got_down)
    mid = grow(mid, got_mid)
    down = grow(down, got_down)
    part, mid, down = tie(part, mid, down)
    got_mid = send(mid, wires["core"])
    got_down = send(down, wires["second"])
    ctx, inv, expo = attend(1, lengths, qkv, part)
    ctx, got_down = tie(ctx, got_down)
    down = grow(down, got_down)
    w_mid = sides_of(mid, got_mid, at, n_z)
    w_back = sides_of(down, send(down, wires["core"]), at, n_z)
    out, normed_low, activated, dbranch, dhidden, dattn, dresid1, dctx, sums, in_sums = ffn(
        at, flags, x, ctx, cot, rows, b_in, w_mid, w_back, n_z
    )

    mine, theirs = c[None], 1 - c[None]
    keep_d, give_d = down_grad(at, activated, dbranch)
    dhidden, give_d = tie(dhidden, give_d)
    got_d = send(give_d, wires["core"])
    give_i, keep_i = in_grad(at, normed_low, dhidden)
    got_d, give_i = tie(got_d, give_i)
    keep_d, give_d = sum_core(keep_d, got_d, at, n_z)
    dctx, give_d, give_i = tie(dctx, give_d, give_i)
    got_d = send(give_d, wires["second"])
    got_i = send(give_i, wires["core"])
    dqkv_theirs = attend_back(theirs, doc_count, qkv, ctx, inv, expo, dctx)
    got_d, got_i, dqkv_theirs = tie(got_d, got_i, dqkv_theirs)
    keep_d, give_d = sum_second(keep_d, got_d, at)
    keep_i, give_i = sum_core(keep_i, got_i, at, n_z)
    dqkv_theirs, give_d, give_i = tie(dqkv_theirs, give_d, give_i)
    got_d = send(give_d, wires["first"])
    got_i = send(give_i, wires["second"])
    give_a = attn_grad(theirs, ctx, dattn, embed_low, dqkv_theirs)
    dctx, give_a = tie(dctx, give_a)
    got_a = send(give_a, wires["core"])
    dqkv_mine = attend_back(mine, doc_count, qkv, ctx, inv, expo, dctx)
    got_d, got_i, dqkv_mine = tie(got_d, got_i, dqkv_mine)
    keep_d, give_d = sum_first(keep_d, got_d, at)
    keep_i, give_i = sum_second(keep_i, got_i, at)
    dqkv_mine, give_d, give_i = tie(dqkv_mine, give_d, give_i)
    got_d = send_all(give_d, wires["z"])
    got_i = send(give_i, wires["first"])
    keep_a = attn_grad(mine, ctx, dattn, embed_low, dqkv_mine)
    got_a, keep_a = tie(got_a, keep_a)
    keep_a, give_a = sum_core(keep_a, got_a, at, n_z)
    dqkv_mine, give_a = tie(dqkv_mine, give_a)
    got_a = send(give_a, wires["second"])
    grad_input, flag_sums, bias_sums = embed_grad(at, flags, dresid1, dqkv_mine, dqkv_theirs, w_attn, n_z)
    got_d, got_i, got_a, flag_sums = tie(got_d, got_i, got_a, flag_sums)
    keep_i, give_i = sum_first(keep_i, got_i, at)
    keep_a, give_a = sum_second(keep_a, got_a, at)
    got_a = send(give_a, wires["first"])
    got_i = send_all(give_i, wires["z"])
    owned_d = sum_z(keep_d, got_d)
    got_d = send_all([owned_d] * 3, wires["rep"])
    keep_a, give_a = sum_first(keep_a, got_a, at)
    got_a = send_all(give_a, wires["z"])
    owned_i = sum_z(keep_i, got_i)
    got_i = send_all([owned_i] * 3, wires["rep"])
    owned_a = sum_z(keep_a, got_a)
    got_a = send_all([owned_a] * 3, wires["rep"])
    o_down, o_in, o_attn = blocks_of(owned_d, got_d, at), blocks_of(owned_i, got_i, at), blocks_of(owned_a, got_a, at)

    halves = [jnp.where(c == h, bias_sums[0], bias_sums[1]) for h in (0, 1)]
    grad_b_q = jnp.concatenate([half[:split] for half in halves])
    grad_b_v = jnp.concatenate([half[2 * split :] for half in halves])
    small = (grad_b_q, grad_b_v, sums[5], sums[3], sums[4], flag_sums[0], flag_sums[1], sums[2], sums[0], sums[1], in_sums[0])
    packed = jnp.concatenate([value.reshape(n_fsdp, -1) for value in small], axis=1)
    for pairs in wires["rep_bits"] + wires["fsdp_bits"]:
        packed = packed + send(packed, pairs)
    packed = pick(packed, 0, own)
    o_small = [packed[i * step : (i + 1) * step] for i in range(10)]

    def join(blocks, cut=slice(None)):
        return jnp.concatenate([jnp.concatenate([block[:, cut] for block in row], axis=1) for row in blocks])

    o_qkv = jnp.concatenate([join(o_attn, slice(i * split, (i + 1) * split)) for i in (1, 2, 3)], axis=1)
    return (
        out.reshape(layer_input.shape),
        grad_input.reshape(layer_input.shape),
        o_qkv,
        o_small[0],
        o_small[1],
        join(o_attn, slice(0, split)),
        o_small[2],
        o_small[3],
        o_small[4],
        o_small[5],
        o_small[6],
        join(o_in),
        packed[10 * step :],
        join(o_down),
        o_small[7],
        o_small[8],
        o_small[9],
    )


def solution(mesh):
    return jax.shard_map(
        body,
        mesh=mesh,
        in_specs=(
            P(("rep", "fsdp"), None, None),
            P(("rep", "fsdp"), None),
            P(("rep", "fsdp"), None),
            P(("rep", "fsdp")),
            P("fsdp", None),
            P("fsdp"),
            P("fsdp"),
            P("fsdp", None),
            P("fsdp"),
            P("fsdp"),
            P("fsdp"),
            P("fsdp"),
            P("fsdp"),
            P("fsdp", None),
            P("fsdp"),
            P("fsdp", None),
            P("fsdp"),
            P("fsdp"),
            P("fsdp"),
            P(("rep", "fsdp"), None, None),
        ),
        out_specs=(
            P(("rep", "fsdp"), None, None),
            P(("rep", "fsdp"), None, None),
            P("fsdp", None),
            P("fsdp"),
            P("fsdp"),
            P("fsdp", None),
            P("fsdp"),
            P("fsdp"),
            P("fsdp"),
            P("fsdp"),
            P("fsdp"),
            P("fsdp", None),
            P("fsdp"),
            P("fsdp", None),
            P("fsdp"),
            P("fsdp"),
            P("fsdp"),
        ),
        check_vma=False,
    )
```

```python
import functools

import jax
import jax.numpy as jnp
from jax import lax
from jax.experimental import pallas as pl
from jax.experimental.pallas import tpu as pltpu
from jax.sharding import PartitionSpec as P

HEADS = 12
AXES = ("rep", "fsdp")
EPSILON = 1e-05
TILE = 256
VMEM_BYTES = 60 * 1024 * 1024
STEEP = 0.28
TAIL = (0.11652066258099363, 0.06749752053058514, 0.2689081593014359, -0.23699088133158833, 0.38987234732742354, -0.10580781763400933)


def wiring(n_fsdp):
    n_z = n_fsdp // 2

    def pairs(move):
        out = []
        for i in range(4 * n_fsdp):
            y, c, z, x = i // (2 * n_fsdp), i // n_fsdp % 2, i % n_fsdp // 2, i % 2
            y2, c2, z2, x2 = move(y, c, z, x)
            out.append((i, ((y2 * 2 + c2) * n_z + z2) * 2 + x2))
        return out

    return {
        "core": pairs(lambda y, c, z, x: (y, 1 - c, z, x)),
        "first": pairs(lambda y, c, z, x: (1 - y, c, z, x) if c == 0 else (y, c, z, 1 - x)),
        "second": pairs(lambda y, c, z, x: (y, c, z, 1 - x) if c == 0 else (1 - y, c, z, x)),
        "z": [pairs(lambda y, c, z, x, m=m: (y, c, z ^ m, x)) for m in range(1, n_z)],
        "rep": [pairs(lambda y, c, z, x, m=m: (y ^ (m // 2), c ^ (m % 2), z, x)) for m in (1, 2, 3)],
        "x": pairs(lambda y, c, z, x: (y, c, z, 1 - x)),
    }


def send(value, pairs):
    return lax.ppermute(value, AXES, pairs)


def tie(*values):
    return lax.optimization_barrier(values)


def pick(value, axis, index):
    return lax.dynamic_index_in_dim(value, index, axis, keepdims=False)


def add_low(left, right):
    return (left.astype(jnp.float32) + right.astype(jnp.float32)).astype(jnp.bfloat16)


def flip_by(value, axis, mask):
    for bit in range(value.shape[axis].bit_length() - 1):
        shape = value.shape
        cut = value.reshape(shape[:axis] + (-1, 2, 1 << bit) + shape[axis + 1 :])
        value = jnp.where(mask >> bit & 1 == 1, jnp.flip(cut, axis + 1), cut).reshape(shape)
    return value


def gather_z(piece, wires):
    return jnp.concatenate([piece] + [send(piece, pairs) for pairs in wires["z"]])


def grow(value, got):
    return jnp.concatenate([value, got])


def pieces_of(eight, got, other_eight, other_got, at, n_z):
    rows = eight.shape[0] // (2 * n_z)
    if in_blocks(rows):
        return (eight, got), (other_eight, other_got)
    y, z, x = at[0], at[2], at[3]
    out = []
    for side, source in ((0, grow(eight, got)), (1, grow(other_eight, other_got))):
        blocks = source.reshape(2, 2, n_z, rows, -1)
        blocks = jnp.where(at[1] ^ side == 0, blocks, blocks.swapaxes(0, 1))
        blocks = flip_by(flip_by(flip_by(blocks, 0, x), 1, y), 2, z)
        out.append((blocks.transpose(2, 0, 1, 3, 4).reshape(source.shape),))
    return tuple(out)


def in_blocks(rows):
    return rows % 16 == 0


def sum_core(keep, got, at, n_z):
    y, c, x = at[0], at[1], at[3]
    summed = add_low(keep, got).reshape(n_z, 2, 2, -1, keep.shape[1])
    away = jnp.where(c == 0, pick(summed, 1, 1 - x), pick(summed, 2, 1 - y))
    return jnp.where(c == 0, pick(summed, 1, x), pick(summed, 2, y)), away


def sum_second(keep, got, at):
    spot = jnp.where(at[1] == 0, at[0], at[3])
    return tuple(add_low(pick(keep, 1, which), pick(got, 1, which)) for which in (spot, 1 - spot))


def sum_first(keep, got, at):
    z = at[2]
    sums = [add_low(pick(keep, 0, z ^ m), pick(got, 0, z ^ m)) for m in range(keep.shape[0])]
    return sums[0], sums[1:]


def sum_z(keep, gots):
    total = keep.astype(jnp.float32)
    for got in gots:
        total = total + got.astype(jnp.float32)
    return total.astype(jnp.bfloat16)


def blocks_of(owned, gots, at):
    quarters = jnp.stack([owned] + list(gots))
    return [
        [pick(quarters, 0, (at[0] ^ row) * 2 + (at[1] ^ col)).astype(jnp.float32) for col in (0, 1)] for row in (0, 1)
    ]


def blocks_of_pairs(pair, got, at):
    halves = jnp.stack([pair, got])
    return [
        [pick(pick(halves, 0, at[1] ^ col), 0, at[0] ^ row).astype(jnp.float32) for col in (0, 1)] for row in (0, 1)
    ]


def send_all(values, wires):
    return [send(value, pairs) for value, pairs in zip(values, wires, strict=True)]


def dot(left, right):
    return lax.dot_general(left, right, (((1,), (0,)), ((), ())), preferred_element_type=jnp.float32)


def dot_cols(left, right):
    return lax.dot_general(left, right, (((1,), (1,)), ((), ())), preferred_element_type=jnp.float32)


def dot_rows(left, right):
    return lax.dot_general(left, right, (((0,), (0,)), ((), ())), preferred_element_type=jnp.float32)


def call(kernel, grid, in_specs, out_specs, out_shape, scratch=(), flops=0, prefetch=0, aliases=None, name=None):
    sizes = [s.size * s.dtype.itemsize for s in jax.tree.leaves(out_shape)]
    return pl.pallas_call(
        kernel,
        grid_spec=pltpu.PrefetchScalarGridSpec(
            num_scalar_prefetch=prefetch, grid=grid, in_specs=in_specs, out_specs=out_specs, scratch_shapes=scratch
        ),
        out_shape=out_shape,
        compiler_params=pltpu.CompilerParams(
            dimension_semantics=("arbitrary",) * len(grid), vmem_limit_bytes=VMEM_BYTES
        ),
        cost_estimate=pl.CostEstimate(flops=flops, bytes_accessed=2 * sum(sizes), transcendentals=0),
        input_output_aliases=aliases or {},
        name=name,
    )


def whole(shape):
    return pl.BlockSpec(shape, lambda i, *_: (0,) * len(shape))


def tiles(width):
    return pl.BlockSpec((TILE, width), lambda i, *_: (i, 0))


ANY = pl.BlockSpec(memory_space=pl.ANY)


def load(at_ref, refs, n_z, targets, relative=False):
    y, c, z, x = at_ref[0], at_ref[1], at_ref[2], at_ref[3]
    per_side = len(refs) // 2
    for side in (0, 1):
        core = jnp.bitwise_xor(c, side)
        half = side if relative else core
        pieces = refs[side * per_side : (side + 1) * per_side]
        rows = pieces[0].shape[0] // (2 * n_z)
        for first, cols, into, sem in targets:
            lanes = pl.ds(pl.multiple_of(half * cols, 128), cols)
            if per_side == 1:
                pltpu.make_async_copy(pieces[0].at[:, pl.ds(first, cols)], into.at[:, lanes], sem).start()
                continue
            for late, ref in enumerate(pieces):
                for b in (0, 1):
                    by_x = jnp.bitwise_xor(x, jnp.where(core == 0, late, b))
                    by_y = jnp.bitwise_xor(y, jnp.where(core == 0, b, late))
                    for m in range(n_z):
                        slot = (jnp.bitwise_xor(z, m) * 2 + by_x) * 2 + by_y
                        pltpu.make_async_copy(
                            ref.at[pl.ds((b * n_z + m) * rows, rows), pl.ds(first, cols)],
                            into.at[pl.ds(pl.multiple_of(slot * rows, rows), rows), lanes],
                            sem,
                        ).start()


def loaded(array, sem):
    pltpu.make_async_copy(array, array, sem).wait()


def qkv_kernel(n_z, at_ref, flag_ref, x_ref, row_ref, bias_ref, *refs):
    pieces, (qkv_ref, low_ref, w_ref, sem) = refs[:-4], refs[-4:]

    @pl.when(pl.program_id(0) == 0)
    def _():
        load(at_ref, pieces, n_z, [(0, w_ref.shape[1] // 2, w_ref, sem)])
        loaded(w_ref, sem)

    embed_low = (x_ref[...].astype(jnp.float32) + dot_rows(flag_ref[...], row_ref[...])).astype(jnp.bfloat16)
    low_ref[...] = embed_low
    out = dot(embed_low, w_ref[...]) + bias_ref[...]
    third = out.shape[1] // 6
    for half in (0, 1):
        at = half * 3 * third
        qkv_ref[half, :, :third] = (out[:, at : at + third] * 0.125).astype(jnp.bfloat16)
        qkv_ref[half, :, third:] = out[:, at + third : at + 3 * third].astype(jnp.bfloat16)


FLAGS = pl.BlockSpec((16, TILE), lambda i, *_: (0, i))


def project(at, flags, x, rows, bias, pieces, n_z):
    count, width = x.shape
    cols = bias.shape[1] // 2
    return call(
        functools.partial(qkv_kernel, n_z),
        (count // TILE,),
        [FLAGS, tiles(width), whole((16, width)), whole((1, 2 * cols))] + [ANY] * len(pieces),
        [pl.BlockSpec((2, TILE, cols), lambda i, *_: (0, i, 0)), tiles(width)],
        [jax.ShapeDtypeStruct((2, count, cols), jnp.bfloat16), jax.ShapeDtypeStruct((count, width), jnp.bfloat16)],
        [pltpu.VMEM((width, 2 * cols), jnp.bfloat16), pltpu.SemaphoreType.DMA],
        4 * count * width * cols,
        1,
        name="project",
    )(at, flags, x, rows, bias, *pieces)


def unpack_kernel(at_ref, packed_ref, rows_ref, bias_ref, b_in_ref):
    n_fsdp = packed_ref.shape[0]
    own = at_ref[2] * 2 + at_ref[3]
    shards = [packed_ref[jnp.bitwise_xor(own, f)] for f in range(n_fsdp)]
    rows = jnp.concatenate([shard[:16] for shard in shards], axis=1)
    rows_ref[...] = rows.astype(jnp.bfloat16)
    split = rows.shape[1] // 2
    zero = jnp.zeros((1, split), jnp.float32)
    cut = [rows[i : i + 1, at : at + split] for at in (0, split) for i in (8, 9)]
    bias_ref[...] = jnp.concatenate([cut[0], zero, cut[1], cut[2], zero, cut[3]], axis=1)
    b_in_ref[...] = jnp.concatenate([shard[i : i + 1] for shard in shards for i in range(10, 14)], axis=1)


def unpack(at, packed, own):
    n_fsdp, _, step = packed.shape
    width = n_fsdp * step
    if step % 32:
        packed = flip_by(packed, 0, own)
        rows = packed.transpose(1, 0, 2).reshape(16, width)
        split = width // 2
        zero = jnp.zeros((split,))
        bias = [p for h in (0, split) for p in (rows[8, h : h + split], zero, rows[9, h : h + split])]
        return rows.astype(jnp.bfloat16), jnp.concatenate(bias)[None], packed[:, 10:14].reshape(1, 4 * width)
    return pl.pallas_call(
        unpack_kernel,
        in_specs=[pl.BlockSpec(memory_space=pltpu.SMEM), pl.BlockSpec(memory_space=pltpu.VMEM)],
        out_specs=[pl.BlockSpec(memory_space=pltpu.VMEM)] * 3,
        out_shape=[
            jax.ShapeDtypeStruct((16, width), jnp.bfloat16),
            jax.ShapeDtypeStruct((1, 3 * width), jnp.float32),
            jax.ShapeDtypeStruct((1, 4 * width), jnp.float32),
        ],
        name="unpack",
    )(at, packed)


def attend_kernel(n_pair, len_ref, q_ref, k_ref, v_ref, *refs):
    ctx_ref, inv_ref, p_ref = refs[-3:]
    length = len_ref[pl.program_id(0) // n_pair]
    query, keys, values = q_ref[...], k_ref[...], v_ref[...]
    lane = lax.broadcasted_iota(jnp.int32, query.shape, 1)
    row = lax.broadcasted_iota(jnp.int32, query.shape, 0)
    unused = jnp.where(row >= length, -1e30, 0.0).astype(jnp.bfloat16)
    zero, one = jnp.zeros_like(query), jnp.ones_like(query)
    low = lane < 64
    parts = []
    for head in (0, 1):
        mine = low if head == 0 else ~low
        spare = lane == 64 - 64 * head
        scores = dot_cols(
            jnp.where(mine, query, jnp.where(spare, one, zero)), jnp.where(mine, keys, jnp.where(spare, unused, zero))
        )
        expo = jnp.exp(scores - jnp.max(scores, axis=1, keepdims=True)).astype(jnp.bfloat16)
        p_ref[head] = expo
        parts.append(dot(expo, jnp.where(mine, values, one)))
    inv = 1.0 / pltpu.roll(jnp.where(low, parts[1], parts[0]), 64, axis=1)
    inv_ref[...] = inv
    ctx_ref[...] = (jnp.where(low, parts[0], parts[1]) * inv).astype(jnp.bfloat16)


def attend(half, lengths, qkv, before):
    docs = lengths.shape[0]
    count, cols = qkv.shape[1:]
    seq, n_pair = count // docs, cols // 384

    def part(which):
        return pl.BlockSpec((None, seq, 128), lambda i, *_: (half, i // n_pair, which * n_pair + i % n_pair))

    def out():
        return pl.BlockSpec((seq, 128), lambda i, *_: (i // n_pair, half * n_pair + i % n_pair))

    return call(
        functools.partial(attend_kernel, n_pair),
        (docs * n_pair,),
        [part(0), part(1), part(2)] + [ANY] * len(before),
        [out(), out(), pl.BlockSpec((None, None, 2, seq, seq), lambda i, *_: (half, i, 0, 0, 0))],
        [
            jax.ShapeDtypeStruct((count, 2 * cols // 3), jnp.bfloat16),
            jax.ShapeDtypeStruct((count, 2 * cols // 3), jnp.float32),
            jax.ShapeDtypeStruct((2, docs * n_pair, 2, seq, seq), jnp.bfloat16),
        ],
        flops=docs * n_pair * 2 * seq * seq * 256 * 4,
        prefetch=1,
        aliases={4 + i: i for i in range(len(before))},
        name="attend",
    )(lengths, qkv, qkv, qkv, *before)


def norm(resid):
    center = resid - jnp.mean(resid, axis=1, keepdims=True)
    inv = lax.rsqrt(jnp.mean(center * center, axis=1, keepdims=True) + EPSILON)
    return center * inv, inv


def norm_back(grad, normal, inv, gain):
    scaled = grad * gain
    return inv * (
        scaled
        - jnp.mean(scaled, axis=1, keepdims=True)
        - normal * jnp.mean(scaled * normal, axis=1, keepdims=True)
    )


def gelu_parts(u):
    expo = jnp.exp(u * u * -0.5)
    t = 1.0 / (1.0 + STEEP * jnp.abs(u))
    poly = TAIL[5]
    for coef in TAIL[4::-1]:
        poly = poly * t + coef
    tail = expo * (t * poly)
    phi = jnp.where(u >= 0, 1.0 - tail, tail)
    return phi, phi + u * (expo * 0.3989422804014327)


def sum_rows(value):
    return jnp.sum(value, axis=0, keepdims=True)


def start_sums(*refs):
    @pl.when(pl.program_id(0) == 0)
    def _():
        for ref in refs:
            ref[...] = jnp.zeros_like(ref)


def wide_of(rows, *indices):
    rows = rows.astype(jnp.float32)
    return [rows[i : i + 1] for i in indices]


def ffn_kernel(
    n_z,
    n_mid,
    at_ref,
    flag_ref,
    x_ref,
    ctx_ref,
    cot_ref,
    row_ref,
    b_in_ref,
    *refs,
):
    mid, down = refs[:n_mid], refs[n_mid:-15]
    out_ref, low_ref, act_ref, dbranch_ref, dhidden_ref, dattn_ref, dresid_ref, dctx_ref = refs[-15:-7]
    sums_ref, in_sums_ref, wo_ref, wi_ref, wd_ref, slope_ref, sems = refs[-7:]
    first = pl.program_id(0) == 0
    width = x_ref.shape[1]
    chunks = range(0, wi_ref.shape[1], width)

    start_sums(sums_ref, in_sums_ref)

    @pl.when(first)
    def _():
        half = wi_ref.shape[1] // 2
        load(at_ref, mid, n_z, [(half, width // 2, wo_ref, sems.at[0])])
        load(at_ref, mid, n_z, [(0, half, wi_ref, sems.at[1])])
        load(at_ref, down, n_z, [(0, width // 2, wd_ref, sems.at[2])])
        loaded(wo_ref, sems.at[0])
        loaded(wi_ref, sems.at[1])
        loaded(wd_ref, sems.at[2])

    b_out, gain1, shift1, b_down, gain2, shift2 = wide_of(row_ref[...], 2, 3, 4, 5, 6, 7)
    embed = x_ref[...].astype(jnp.float32) + dot_rows(flag_ref[...], row_ref[...])
    normal1, inv1 = norm(embed + dot(ctx_ref[...], wo_ref[...]) + b_out)
    normed = normal1 * gain1 + shift1
    normed_low = normed.astype(jnp.bfloat16)
    low_ref[...] = normed_low
    branch = normed + b_down
    for at in chunks:
        cols = slice(at, at + width)
        hidden = dot(normed_low, wi_ref[:, cols]) + b_in_ref[:, cols]
        phi, slope = gelu_parts(hidden)
        slope_ref[:, cols] = slope
        activated = (hidden * phi).astype(jnp.bfloat16)
        act_ref[:, cols] = activated
        branch = branch + dot(activated, wd_ref[cols, :])
    normal2, inv2 = norm(branch)
    out_ref[...] = (normal2 * gain2 + shift2).astype(jnp.bfloat16)
    grad = cot_ref[...].astype(jnp.float32)
    dresid2 = norm_back(grad, normal2, inv2, gain2)
    dbranch = dresid2.astype(jnp.bfloat16)
    dbranch_ref[...] = dbranch
    sums_ref[0:1] += sum_rows(grad * normal2)
    sums_ref[1:2] += sum_rows(grad)
    sums_ref[2:3] += sum_rows(dbranch.astype(jnp.float32))
    dnormed = dresid2
    for at in chunks:
        cols = slice(at, at + width)
        dhidden = (dot_cols(dbranch, wd_ref[cols, :]) * slope_ref[:, cols]).astype(jnp.bfloat16)
        dhidden_ref[:, cols] = dhidden
        in_sums_ref[0:1, cols] += sum_rows(dhidden.astype(jnp.float32))
        dnormed = dnormed + dot_cols(dhidden, wi_ref[:, cols])
    dresid1 = norm_back(dnormed, normal1, inv1, gain1)
    dattn = dresid1.astype(jnp.bfloat16)
    dresid_ref[...] = dresid1
    dattn_ref[...] = dattn
    sums_ref[3:4] += sum_rows(dnormed * normal1)
    sums_ref[4:5] += sum_rows(dnormed)
    sums_ref[5:6] += sum_rows(dattn.astype(jnp.float32))
    dctx_ref[...] = dot_cols(dattn, wo_ref[...]).astype(jnp.bfloat16)


def ffn(at, flags, x, ctx, cot, rows, b_in, mid, down, n_z):
    count, width = x.shape
    ff_width = b_in.shape[1]
    low = jax.ShapeDtypeStruct((count, width), jnp.bfloat16)
    wide = jax.ShapeDtypeStruct((count, ff_width), jnp.bfloat16)
    return call(
        functools.partial(ffn_kernel, n_z, len(mid)),
        (count // TILE,),
        [FLAGS]
        + [tiles(width)] * 3
        + [whole((16, width)), whole((1, ff_width))]
        + [ANY] * (len(mid) + len(down)),
        [tiles(width)] * 2
        + [tiles(ff_width), tiles(width), tiles(ff_width)]
        + [tiles(width)] * 3
        + [whole((8, width)), whole((8, ff_width))],
        [low, low, wide, low, wide, low, jax.ShapeDtypeStruct((count, width), jnp.float32), low]
        + [jax.ShapeDtypeStruct((8, width), jnp.float32), jax.ShapeDtypeStruct((8, ff_width), jnp.float32)],
        [
            pltpu.VMEM((width, width), jnp.bfloat16),
            pltpu.VMEM((width, ff_width), jnp.bfloat16),
            pltpu.VMEM((ff_width, width), jnp.bfloat16),
            pltpu.VMEM((TILE, ff_width), jnp.float32),
            pltpu.SemaphoreType.DMA((3,)),
        ],
        4 * count * width * (width + 2 * ff_width),
        1,
        name="ffn",
    )(at, flags, x, ctx, cot, rows, b_in, *mid, *down)


def grad_kernel(n_first, first_z, by_z, at_ref, *refs):
    *lefts, got_ref, away_ref, stay_ref, sum_ref = refs if first_z else (*refs[:-1], None, None, refs[-1], None)
    step = pl.program_id(0)

    def put(left_ref, right_ref):
        grad = dot_rows(left_ref[...], right_ref[...])
        lanes = slice(0, grad.shape[1])
        if not first_z:
            stay_ref[:, lanes] = grad.astype(jnp.bfloat16)
            return
        sum_ref[:, lanes] = (grad + got_ref[:, lanes].astype(jnp.float32)).astype(jnp.bfloat16)
        y, c, x = at_ref[0], at_ref[1], at_ref[3]
        rows = away_ref.shape[2]
        for z in range(by_z):
            for b in (0, 1):
                for ref, this_x, this_y in ((away_ref, 1 - x, 1 - y), (stay_ref, x, y)):
                    block = jnp.where(c == 0, this_x * 2 + b, b * 2 + this_y) + z * 4
                    ref[z, b, :, lanes] = sum_ref[pl.ds(pl.multiple_of(block * rows, rows), rows), lanes]

    if len(lefts) == 2:
        put(*lefts)
        return
    pl.when(step < n_first)(lambda: put(lefts[0], lefts[1]))
    pl.when(step >= n_first)(lambda: put(lefts[2], lefts[3]))


def grads(at, half, parts, got, n_z, tile, name):
    count, rows = parts[0][0].shape
    width = sum(cols for _, _, cols in parts)
    tall = rows > 2 * width
    n_first = (rows if tall else parts[0][2]) // tile
    steps = n_first + len(parts) - 1
    specs, arrays = [], []
    for left, right, cols in parts:
        if tall:
            specs += [pl.BlockSpec((count, tile), lambda i, *_: (0, i))]
            specs += [pl.BlockSpec((count, cols), lambda i, at_ref: (0, at_ref[4]))]
        else:
            n_tile = max(cols // tile, 1)
            start = n_tile if right.shape[1] > cols else 0
            specs += [
                whole((count, rows)),
                pl.BlockSpec(
                    (count, min(tile, cols)),
                    lambda i, at_ref, n=n_tile, start=start: (0, at_ref[4] * start + jnp.minimum(i, n - 1)),
                ),
            ]
        arrays += [left, right]
    at = jnp.concatenate([at, half])
    block = rows // (4 * n_z)
    shape = (tile, width) if tall else (rows, tile)
    spec = pl.BlockSpec(shape, (lambda i, *_: (i, 0)) if tall else (lambda i, *_: (0, i)))
    flops = 2 * count * rows * width
    plain = functools.partial(grad_kernel, n_first, False, 0)
    fused = got is not None and block % 16 == 0
    if not fused:
        grad = call(
            plain, (steps,), specs, spec, jax.ShapeDtypeStruct((rows, width), jnp.bfloat16), flops=flops, prefetch=1, name=name
        )(at, *arrays)
        if got is None:
            return grad
        stay, away = sum_core(grad, got, at, n_z)
        return away, stay
    by_z = shape[0] // (4 * block)
    split = pl.BlockSpec(
        (by_z, 2, block, shape[1]), (lambda i, *_: (i, 0, 0, 0)) if tall else (lambda i, *_: (0, 0, 0, i))
    )
    return call(
        functools.partial(grad_kernel, n_first, True, by_z),
        (steps,),
        specs + [spec],
        [split] * 2,
        [jax.ShapeDtypeStruct((n_z, 2, block, width), jnp.bfloat16)] * 2,
        [pltpu.VMEM(shape, jnp.bfloat16)],
        flops=flops,
        prefetch=1,
        name=name,
    )(at, *arrays, got)


def attend_back_kernel(n_pair, half_ref, q_ref, k_ref, v_ref, ctx_ref, inv_ref, p_ref, dctx_ref, out_ref):
    pair = pl.program_id(0) % n_pair
    query, keys, values = q_ref[...], k_ref[...], v_ref[...]
    lane = lax.broadcasted_iota(jnp.int32, query.shape, 1)
    low = lane < 64
    zero, one = jnp.zeros_like(query), jnp.ones_like(query)
    dctx = (dctx_ref[...].astype(jnp.float32) * inv_ref[...]).astype(jnp.bfloat16)
    product = dctx.astype(jnp.float32) * ctx_ref[...].astype(jnp.float32)
    grads = []
    for head in (0, 1):
        mine = low if head == 0 else ~low
        spare = lane == 64 - 64 * head
        fine = lane == 65 - 64 * head
        delta = jnp.sum(jnp.where(mine, product, 0.0), axis=1, keepdims=True)
        coarse = delta.astype(jnp.bfloat16)
        rest = (delta - coarse.astype(jnp.float32)).astype(jnp.bfloat16)
        left = jnp.where(mine, dctx, jnp.where(spare, -coarse, jnp.where(fine, -rest, zero)))
        expo = p_ref[head]
        dprobs = dot_cols(left, jnp.where(mine, values, jnp.where(spare | fine, one, zero)))
        dscores = (expo.astype(jnp.float32) * dprobs).astype(jnp.bfloat16)
        grads.append((dot(dscores, keys) * 0.125, dot_rows(dscores, query), dot_rows(expo, dctx)))
    third = out_ref.shape[1] // 3
    for which in range(3):
        grad = jnp.where(low, grads[0][which], grads[1][which]).astype(jnp.bfloat16)
        out_ref[:, pl.ds(pl.multiple_of(which * third + pair * 128, 128), 128)] = grad


def attend_back(half, docs, qkv, ctx, inv, expo, dctx):
    count, cols = qkv.shape[1:]
    seq, n_pair = count // docs, cols // 384

    def part(which):
        return pl.BlockSpec((None, seq, 128), lambda i, h: (h[0], i // n_pair, which * n_pair + i % n_pair))

    one = pl.BlockSpec((seq, 128), lambda i, h: (i // n_pair, h[0] * n_pair + i % n_pair))
    return call(
        functools.partial(attend_back_kernel, n_pair),
        (docs * n_pair,),
        [part(0), part(1), part(2), one, one]
        + [pl.BlockSpec((None, None, 2, seq, seq), lambda i, h: (h[0], i, 0, 0, 0)), one],
        pl.BlockSpec((seq, cols), lambda i, h: (i // n_pair, 0)),
        jax.ShapeDtypeStruct((count, cols), jnp.bfloat16),
        flops=docs * n_pair * 2 * seq * seq * 256 * 10,
        prefetch=1,
        name="attend_back",
    )(half, qkv, qkv, qkv, ctx, inv, expo, dctx)


def embed_grad_kernel(n_z, at_ref, flag_ref, dresid_ref, mine_ref, theirs_ref, *refs):
    pieces, (grad_ref, sums_ref, bias_ref, w_ref, sem) = refs[:-5], refs[-5:]
    cols = mine_ref.shape[1]
    start_sums(sums_ref, bias_ref)

    @pl.when(pl.program_id(0) == 0)
    def _():
        load(at_ref, pieces, n_z, [(0, cols, w_ref, sem)], relative=True)
        loaded(w_ref, sem)

    mine, theirs = mine_ref[...], theirs_ref[...]
    dembed = dresid_ref[...] + dot_cols(mine, w_ref[:, :cols]) + dot_cols(theirs, w_ref[:, cols:])
    coarse = dembed.astype(jnp.bfloat16)
    grad_ref[...] = coarse
    rest = (dembed - coarse.astype(jnp.float32)).astype(jnp.bfloat16)
    sums_ref[...] += dot(flag_ref[...], coarse) + dot(flag_ref[...], rest)
    bias_ref[0:1] += sum_rows(mine.astype(jnp.float32))
    bias_ref[1:2] += sum_rows(theirs.astype(jnp.float32))


def embed_grad(at, flags, dresid, mine, theirs, pieces, n_z):
    count, width = dresid.shape
    cols = mine.shape[1]
    return call(
        functools.partial(embed_grad_kernel, n_z),
        (count // TILE,),
        [FLAGS, tiles(width), tiles(cols), tiles(cols)] + [ANY] * len(pieces),
        [tiles(width), whole((16, width)), whole((8, cols))],
        [
            jax.ShapeDtypeStruct((count, width), jnp.bfloat16),
            jax.ShapeDtypeStruct((16, width), jnp.float32),
            jax.ShapeDtypeStruct((8, cols), jnp.float32),
        ],
        [pltpu.VMEM((width, 2 * cols), jnp.bfloat16), pltpu.SemaphoreType.DMA],
        4 * count * width * cols,
        1,
        name="embed_grad",
    )(at, flags, dresid, mine, theirs, *pieces)


def pack_kernel(at_ref, sums_ref, in_ref, flag_ref, bias_ref, out_ref):
    core = at_ref[1]
    width = sums_ref.shape[1]
    split = width // 2
    bias = bias_ref[...]
    mine, theirs = bias[0:1], bias[1:2]
    low, high = jnp.where(core == 0, mine, theirs), jnp.where(core == 0, theirs, mine)
    for row, cols in ((0, slice(0, split)), (1, slice(2 * split, 3 * split))):
        out_ref[row : row + 1, :split] = low[:, cols]
        out_ref[row : row + 1, split:] = high[:, cols]
    for row, (ref, source) in enumerate(
        ((sums_ref, 5), (sums_ref, 3), (sums_ref, 4), (flag_ref, 0), (flag_ref, 1), (sums_ref, 2), (sums_ref, 0), (sums_ref, 1)), 2
    ):
        out_ref[row : row + 1, :] = ref[source : source + 1, :]
    out_ref[10:11, :] = jnp.zeros((1, width), jnp.float32)
    for i in range(4):
        out_ref[11 + i : 12 + i, :] = in_ref[0:1, i * width : (i + 1) * width]
    out_ref[15:16, :] = jnp.zeros((1, width), jnp.float32)


def pack(at, sums, in_sums, flag_sums, bias_sums):
    return pl.pallas_call(
        pack_kernel,
        in_specs=[pl.BlockSpec(memory_space=pltpu.SMEM)] + [pl.BlockSpec(memory_space=pltpu.VMEM)] * 4,
        out_specs=pl.BlockSpec(memory_space=pltpu.VMEM),
        out_shape=jax.ShapeDtypeStruct((16, sums.shape[1]), jnp.float32),
        name="pack",
    )(at, sums, in_sums, flag_sums, bias_sums)


def body(
    layer_input,
    masked,
    replaced,
    lengths,
    w_qkv,
    b_q,
    b_v,
    w_out,
    b_out,
    gain1,
    shift1,
    mask_vec,
    repl_vec,
    w_in,
    b_in,
    w_down,
    b_down,
    gain2,
    shift2,
    cotangent,
):
    doc_count, seq_len, width = layer_input.shape
    tok_count = doc_count * seq_len
    n_fsdp = lax.axis_size("fsdp")
    n_z = n_fsdp // 2
    wires = wiring(n_fsdp)
    rep, own = lax.axis_index("rep"), lax.axis_index("fsdp")
    at = jnp.stack([rep // 2, rep % 2, own // 2, own % 2]).astype(jnp.int32)
    y, c = at[0], at[1]
    ff_width = w_in.shape[1]
    split = width // 2
    step = width // n_fsdp

    def quarter(weight):
        rows, cols = weight.shape[0] // 2, weight.shape[1] // 2
        return lax.dynamic_slice(weight, (y * rows, c * cols), (rows, cols))

    vectors = jnp.stack((mask_vec, repl_vec, b_out, gain1, shift1, b_down, gain2, shift2, b_q, b_v))
    packed = jnp.concatenate([vectors, b_in.reshape(-1, step), jnp.zeros((2, step), b_in.dtype)])
    packed = packed.astype(jnp.float32)[None]
    first_attn = jnp.concatenate([quarter(w_qkv[:, i * width : (i + 1) * width]) for i in range(3)], axis=1)
    first_mid = jnp.concatenate([quarter(w_in), quarter(w_out)], axis=1)
    first_down = quarter(w_down)

    attn = gather_z(first_attn, wires)
    attn, packed = tie(attn, packed)
    got_attn = send(attn, wires["first"])
    packed = gather_z(grow(packed, send(packed, wires["x"])), wires)
    got_attn, first_mid, packed = tie(got_attn, first_mid, packed)
    rows, bias, b_in = unpack(at, packed, own)
    flags = jnp.stack([masked.reshape(tok_count), replaced.reshape(tok_count)]).astype(jnp.bfloat16)
    flags = jnp.concatenate([flags, jnp.zeros((14, tok_count), jnp.bfloat16)])
    x = layer_input.reshape(tok_count, width)
    cot = cotangent.reshape(tok_count, width)
    attn = grow(attn, got_attn)
    got_attn = send(attn, wires["second"])
    mid = gather_z(first_mid, wires)
    mid, got_attn, first_down, rows = tie(mid, got_attn, first_down, rows)
    got_mid = send(mid, wires["first"])
    pieces = (attn, got_attn, send(attn, wires["core"]), send(got_attn, wires["core"]))
    got_down = send_all([first_down] * (n_z - 1), wires["z"])
    got_mid, rows = tie(got_mid, rows)
    mid = grow(mid, got_mid)
    rows, mid = tie(rows, mid)
    got_mid = send(mid, wires["second"])
    w_attn = sum(pieces_of(*pieces, at, n_z), ())

    qkv, embed_low = project(at, flags, x, rows, bias, w_attn, n_z)
    qkv, got_down = tie(qkv, got_down)
    down = jnp.concatenate([first_down] + got_down)
    qkv, down = tie(qkv, down)
    got_down = send(down, wires["first"])
    other_mid = send(mid, wires["core"])
    part = attend(0, lengths, qkv, ())
    part, got_mid, got_down, other_mid = tie(part, got_mid, got_down, other_mid)
    down = grow(down, got_down)
    part, down = tie(part, down)
    got_down = send(down, wires["second"])
    other_down = send(down, wires["core"])
    w_mid = (mid, got_mid, other_mid, send(got_mid, wires["core"]))
    ctx, inv, expo = attend(1, lengths, qkv, part)
    ctx, w_mid, got_down, other_down = tie(ctx, w_mid, got_down, other_down)
    w_mid = sum(pieces_of(*w_mid, at, n_z), ())
    w_back = sum(pieces_of(down, got_down, other_down, send(got_down, wires["core"]), at, n_z), ())
    out, normed_low, activated, dbranch, dhidden, dattn, dresid1, dctx, sums, in_sums = ffn(
        at, flags, x, ctx, cot, rows, b_in, w_mid, w_back, n_z
    )

    mine, theirs = c[None], 1 - c[None]
    part_d = [(activated, dbranch, split)]
    part_m = [(normed_low, dhidden, ff_width // 2), (ctx, dattn, split)]
    give_d = grads(at, theirs, part_d, None, n_z, width, "down_give")
    dattn, give_d = tie(dattn, give_d)
    part_m[1] = (ctx, dattn, split)
    got_d = send(give_d, wires["core"])
    give_m = grads(at, theirs, part_m, None, n_z, width, "mid_give")
    got_d, give_m = tie(got_d, give_m)
    got_m = send(give_m, wires["core"])
    give_d, keep_d = grads(at, mine, part_d, got_d, n_z, width, "down_keep")
    give_d, dctx = tie(give_d, dctx)
    got_d = send(give_d, wires["second"])
    dqkv_theirs = attend_back(theirs, doc_count, qkv, ctx, inv, expo, dctx)
    got_d, got_m, dqkv_theirs = tie(got_d, got_m, dqkv_theirs)
    keep_d, give_d = sum_second(keep_d, got_d, at)
    give_d, got_m = tie(give_d, got_m)
    got_d = send(give_d, wires["first"])
    give_m, keep_m = grads(at, mine, part_m, got_m, n_z, width, "mid_keep")
    got_d, give_m, dqkv_theirs = tie(got_d, give_m, dqkv_theirs)
    got_m = send(give_m, wires["second"])
    keep_d, give_d = sum_first(keep_d, got_d, at)
    give_d, dqkv_theirs = tie(give_d, dqkv_theirs)
    got_d = send_all(give_d, wires["z"])
    give_a = grads(at, theirs, [(embed_low, dqkv_theirs, 3 * split)], None, n_z, 3 * split, "attn_give")
    give_a, dctx = tie(give_a, dctx)
    got_a = send(give_a, wires["core"])
    dqkv_mine = attend_back(mine, doc_count, qkv, ctx, inv, expo, dctx)
    got_d, got_m, got_a, dqkv_mine = tie(got_d, got_m, got_a, dqkv_mine)
    keep_m, give_m = sum_second(keep_m, got_m, at)
    owned_d = sum_z(keep_d, got_d)
    give_m, owned_d, got_a = tie(give_m, owned_d, got_a)
    got_m = send(give_m, wires["first"])
    give_a, keep_a = grads(at, mine, [(embed_low, dqkv_mine, 3 * split)], got_a, n_z, 3 * split, "attn_keep")
    give_a, got_m = tie(give_a, got_m)
    got_a = send(give_a, wires["second"])
    keep_m, give_m = sum_first(keep_m, got_m, at)
    give_m, dqkv_mine, owned_d = tie(give_m, dqkv_mine, owned_d)
    got_m = send_all(give_m, wires["z"])
    got_d = send(owned_d, wires["rep"][1])
    grad_input, flag_sums, bias_sums = embed_grad(at, flags, dresid1, dqkv_mine, dqkv_theirs, w_attn, n_z)
    got_d, got_a, flag_sums = tie(got_d, got_a, flag_sums)
    keep_a, give_a = sum_second(keep_a, got_a, at)
    packed = pack(at, sums, in_sums, flag_sums, bias_sums)
    give_a, packed, got_m = tie(give_a, packed, got_m)
    got_a = send(give_a, wires["first"])
    got = send(packed, wires["x"])
    pair_d = jnp.stack([owned_d, got_d])
    owned_m = sum_z(keep_m, got_m)
    got_a, got, pair_d, owned_m = tie(got_a, got, pair_d, owned_m)
    packed = packed + got
    keep_a, give_a = sum_first(keep_a, got_a, at)
    give_a, packed, pair_d, owned_m = tie(give_a, packed, pair_d, owned_m)
    got_a = send_all(give_a, wires["z"])
    got = send_all([packed] * (n_z - 1), wires["z"])
    got_d = send(pair_d, wires["core"])
    got_m = send(owned_m, wires["rep"][1])
    got_a, got, got_d, got_m = tie(got_a, got, got_d, got_m)
    owned_a = sum_z(keep_a, got_a)
    terms = jnp.stack([packed] + got)
    packed = sum((pick(terms, 0, own // 2 ^ z) for z in range(1, n_z)), pick(terms, 0, own // 2))
    pair_m = jnp.stack([owned_m, got_m])
    owned_a, packed, pair_m = tie(owned_a, packed, pair_m)
    got_a = send_all([owned_a] * 3, wires["rep"])
    got = send_all([packed] * 3, wires["rep"])
    got_m = send(pair_m, wires["core"])
    terms = jnp.stack([packed] + got)
    packed = sum((pick(terms, 0, rep ^ r) for r in range(1, 4)), pick(terms, 0, rep))
    o_small = lax.dynamic_slice(packed, (0, own * step), (16, step))
    o_b_in = lax.dynamic_slice(packed[11:15].reshape(ff_width), (own * (ff_width // n_fsdp),), (ff_width // n_fsdp,))
    o_down, o_mid = blocks_of_pairs(pair_d, got_d, at), blocks_of_pairs(pair_m, got_m, at)
    o_attn = blocks_of(owned_a, got_a, at)

    def join(blocks, cut=slice(None)):
        return jnp.concatenate([jnp.concatenate([block[:, cut] for block in row], axis=1) for row in blocks])

    o_qkv = jnp.concatenate([join(o_attn, slice(i * split, (i + 1) * split)) for i in (0, 1, 2)], axis=1)
    return (
        out.reshape(layer_input.shape),
        grad_input.reshape(layer_input.shape),
        o_qkv,
        o_small[0],
        o_small[1],
        join(o_mid, slice(ff_width // 2, None)),
        o_small[2],
        o_small[3],
        o_small[4],
        o_small[5],
        o_small[6],
        join(o_mid, slice(0, ff_width // 2)),
        o_b_in,
        join(o_down),
        o_small[7],
        o_small[8],
        o_small[9],
    )


def solution(mesh):
    return jax.shard_map(
        body,
        mesh=mesh,
        in_specs=(
            P(("rep", "fsdp"), None, None),
            P(("rep", "fsdp"), None),
            P(("rep", "fsdp"), None),
            P(("rep", "fsdp")),
            P("fsdp", None),
            P("fsdp"),
            P("fsdp"),
            P("fsdp", None),
            P("fsdp"),
            P("fsdp"),
            P("fsdp"),
            P("fsdp"),
            P("fsdp"),
            P("fsdp", None),
            P("fsdp"),
            P("fsdp", None),
            P("fsdp"),
            P("fsdp"),
            P("fsdp"),
            P(("rep", "fsdp"), None, None),
        ),
        out_specs=(
            P(("rep", "fsdp"), None, None),
            P(("rep", "fsdp"), None, None),
            P("fsdp", None),
            P("fsdp"),
            P("fsdp"),
            P("fsdp", None),
            P("fsdp"),
            P("fsdp"),
            P("fsdp"),
            P("fsdp"),
            P("fsdp"),
            P("fsdp", None),
            P("fsdp"),
            P("fsdp", None),
            P("fsdp"),
            P("fsdp"),
            P("fsdp"),
        ),
        check_vma=False,
    )
```

```python
import functools

import jax
import jax.numpy as jnp
from jax import lax
from jax.experimental import pallas as pl
from jax.experimental.pallas import tpu as pltpu
from jax.sharding import PartitionSpec as P

HEADS = 12
AXES = ("rep", "fsdp")
EPSILON = 1e-05
TILE = 256
FFN_TILE = 512
PART = 256
OFFSET = 1
VMEM_BYTES = 60 * 1024 * 1024
STEEP = 0.28
TAIL = (0.11652066258099363, 0.06749752053058514, 0.2689081593014359, -0.23699088133158833, 0.38987234732742354, -0.10580781763400933)


def wiring(n_fsdp):
    n_z = n_fsdp // 2

    def pairs(move):
        out = []
        for i in range(4 * n_fsdp):
            y, c, z, x = i // (2 * n_fsdp), i // n_fsdp % 2, i % n_fsdp // 2, i % 2
            y2, c2, z2, x2 = move(y, c, z, x)
            out.append((i, ((y2 * 2 + c2) * n_z + z2) * 2 + x2))
        return out

    return {
        "core": pairs(lambda y, c, z, x: (y, 1 - c, z, x)),
        "first": pairs(lambda y, c, z, x: (1 - y, c, z, x) if c == 0 else (y, c, z, 1 - x)),
        "second": pairs(lambda y, c, z, x: (y, c, z, 1 - x) if c == 0 else (1 - y, c, z, x)),
        "z": [pairs(lambda y, c, z, x, m=m: (y, c, z ^ m, x)) for m in range(1, n_z)],
        "rep": [pairs(lambda y, c, z, x, m=m: (y ^ (m // 2), c ^ (m % 2), z, x)) for m in (1, 2, 3)],
        "x": pairs(lambda y, c, z, x: (y, c, z, 1 - x)),
        "z_bits": [pairs(lambda y, c, z, x, b=b: (y, c, z ^ (1 << b), x)) for b in range(n_z.bit_length() - 1)],
    }


def send(value, pairs):
    return lax.ppermute(value, AXES, pairs)


def tie(*values):
    return lax.optimization_barrier(values)


def pick(value, axis, index):
    return lax.dynamic_index_in_dim(value, index, axis, keepdims=False)


def add_low(left, right):
    return (left.astype(jnp.float32) + right.astype(jnp.float32)).astype(jnp.bfloat16)


def flip_by(value, axis, mask):
    for bit in range(value.shape[axis].bit_length() - 1):
        shape = value.shape
        cut = value.reshape(shape[:axis] + (-1, 2, 1 << bit) + shape[axis + 1 :])
        value = jnp.where(mask >> bit & 1 == 1, jnp.flip(cut, axis + 1), cut).reshape(shape)
    return value


def gather_z(piece, wires):
    return jnp.concatenate([piece] + [send(piece, pairs) for pairs in wires["z"]])


def grow(value, got):
    return jnp.concatenate([value, got])


def pieces_of(eight, got, other_eight, other_got, at, n_z):
    rows = eight.shape[0] // (2 * n_z)
    if in_blocks(rows):
        return (eight, got), (other_eight, other_got)
    y, z, x = at[0], at[2], at[3]
    out = []
    for side, source in ((0, grow(eight, got)), (1, grow(other_eight, other_got))):
        blocks = source.reshape(2, 2, n_z, rows, -1)
        blocks = jnp.where(at[1] ^ side == 0, blocks, blocks.swapaxes(0, 1))
        blocks = flip_by(flip_by(flip_by(blocks, 0, x), 1, y), 2, z)
        out.append((blocks.transpose(2, 0, 1, 3, 4).reshape(source.shape),))
    return tuple(out)


def in_blocks(rows):
    return rows % 16 == 0


def sum_core(keep, got, at, n_z):
    y, c, x = at[0], at[1], at[3]
    summed = add_low(keep, got).reshape(n_z, 2, 2, -1, keep.shape[1])
    away = jnp.where(c == 0, pick(summed, 1, 1 - x), pick(summed, 2, 1 - y))
    return jnp.where(c == 0, pick(summed, 1, x), pick(summed, 2, y)), away


def sum_second(keep, got, at):
    spot = jnp.where(at[1] == 0, at[0], at[3])
    return tuple(add_low(pick(keep, 1, which), pick(got, 1, which)) for which in (spot, 1 - spot))


def sum_first(keep, got, at):
    z = at[2]
    sums = [add_low(pick(keep, 0, z ^ m), pick(got, 0, z ^ m)) for m in range(keep.shape[0])]
    return sums[0], sums[1:]


def sum_z(keep, gots):
    total = keep.astype(jnp.float32)
    for got in gots:
        total = total + got.astype(jnp.float32)
    return total.astype(jnp.bfloat16)


def blocks_of(owned, gots, at):
    quarters = jnp.stack([owned] + list(gots))
    return [
        [pick(quarters, 0, (at[0] ^ row) * 2 + (at[1] ^ col)).astype(jnp.float32) for col in (0, 1)] for row in (0, 1)
    ]


def blocks_of_pairs(pair, got, at):
    halves = jnp.stack([pair, got])
    return [
        [pick(pick(halves, 0, at[1] ^ col), 0, at[0] ^ row).astype(jnp.float32) for col in (0, 1)] for row in (0, 1)
    ]


def send_all(values, wires):
    return [send(value, pairs) for value, pairs in zip(values, wires, strict=True)]


def dot(left, right):
    return lax.dot_general(left, right, (((1,), (0,)), ((), ())), preferred_element_type=jnp.float32)


def dot_cols(left, right):
    return lax.dot_general(left, right, (((1,), (1,)), ((), ())), preferred_element_type=jnp.float32)


def dot_rows(left, right):
    return lax.dot_general(left, right, (((0,), (0,)), ((), ())), preferred_element_type=jnp.float32)


def call(kernel, grid, in_specs, out_specs, out_shape, scratch=(), flops=0, prefetch=0, aliases=None, name=None):
    sizes = [s.size * s.dtype.itemsize for s in jax.tree.leaves(out_shape)]
    return pl.pallas_call(
        kernel,
        grid_spec=pltpu.PrefetchScalarGridSpec(
            num_scalar_prefetch=prefetch, grid=grid, in_specs=in_specs, out_specs=out_specs, scratch_shapes=scratch
        ),
        out_shape=out_shape,
        compiler_params=pltpu.CompilerParams(
            dimension_semantics=("arbitrary",) * len(grid), vmem_limit_bytes=VMEM_BYTES
        ),
        cost_estimate=pl.CostEstimate(flops=flops, bytes_accessed=2 * sum(sizes), transcendentals=0),
        input_output_aliases=aliases or {},
        name=name,
    )


def whole(shape):
    return pl.BlockSpec(shape, lambda i, *_: (0,) * len(shape))


def tiles(width):
    return pl.BlockSpec((TILE, width), lambda i, *_: (i, 0))


ANY = pl.BlockSpec(memory_space=pl.ANY)


def load(at_ref, refs, n_z, targets, sides=(0, 1)):
    y, c, z, x = at_ref[0], at_ref[1], at_ref[2], at_ref[3]
    per_side = len(refs) // len(sides)
    for number, side in enumerate(sides):
        core = jnp.bitwise_xor(c, side)
        half = core if len(sides) > 1 else 0
        pieces = refs[number * per_side : (number + 1) * per_side]
        rows = pieces[0].shape[0] // (2 * n_z)
        for first, cols, into, sem in targets:
            lanes = pl.ds(pl.multiple_of(half * cols, 128) if len(sides) > 1 else 0, cols)
            if per_side == 1:
                pltpu.make_async_copy(pieces[0].at[:, pl.ds(first, cols)], into.at[:, lanes], sem).start()
                continue
            for late, ref in enumerate(pieces):
                for b in (0, 1):
                    by_x = jnp.bitwise_xor(x, jnp.where(core == 0, late, b))
                    by_y = jnp.bitwise_xor(y, jnp.where(core == 0, b, late))
                    for m in range(n_z):
                        slot = (jnp.bitwise_xor(z, m) * 2 + by_x) * 2 + by_y
                        pltpu.make_async_copy(
                            ref.at[pl.ds((b * n_z + m) * rows, rows), pl.ds(first, cols)],
                            into.at[pl.ds(pl.multiple_of(slot * rows, rows), rows), lanes],
                            sem,
                        ).start()


def loaded(array, sem):
    pltpu.make_async_copy(array, array, sem).wait()


def qkv_kernel(n_z, at_ref, flag_ref, x_ref, row_ref, bias_ref, *refs):
    pieces, (qkv_ref, low_ref, w_ref, sem) = refs[:-4], refs[-4:]

    @pl.when(pl.program_id(0) == 0)
    def _():
        load(at_ref, pieces, n_z, [(0, w_ref.shape[1] // 2, w_ref, sem)])
        loaded(w_ref, sem)

    embed_low = (x_ref[...].astype(jnp.float32) + dot_rows(flag_ref[...], row_ref[...])).astype(jnp.bfloat16)
    low_ref[...] = embed_low
    out = dot(embed_low, w_ref[...]) + bias_ref[...]
    third = out.shape[1] // 6
    for half in (0, 1):
        at = half * 3 * third
        qkv_ref[half, :, :third] = (out[:, at : at + third] * 0.125).astype(jnp.bfloat16)
        qkv_ref[half, :, third:] = out[:, at + third : at + 3 * third].astype(jnp.bfloat16)


FLAGS = pl.BlockSpec((16, TILE), lambda i, *_: (0, i))


def project(at, flags, x, rows, bias, pieces, n_z):
    count, width = x.shape
    cols = bias.shape[1] // 2
    return call(
        functools.partial(qkv_kernel, n_z),
        (count // TILE,),
        [FLAGS, tiles(width), whole((16, width)), whole((1, 2 * cols))] + [ANY] * len(pieces),
        [pl.BlockSpec((2, TILE, cols), lambda i, *_: (0, i, 0)), tiles(width)],
        [jax.ShapeDtypeStruct((2, count, cols), jnp.bfloat16), jax.ShapeDtypeStruct((count, width), jnp.bfloat16)],
        [pltpu.VMEM((width, 2 * cols), jnp.bfloat16), pltpu.SemaphoreType.DMA],
        4 * count * width * cols,
        1,
        name="project",
    )(at, flags, x, rows, bias, *pieces)


def unpack_kernel(at_ref, packed_ref, rows_ref, bias_ref, b_in_ref):
    n_fsdp = packed_ref.shape[0]
    own = at_ref[2] * 2 + at_ref[3]
    shards = [packed_ref[jnp.bitwise_xor(own, f)] for f in range(n_fsdp)]
    rows = jnp.concatenate([shard[:16] for shard in shards], axis=1)
    rows_ref[...] = rows.astype(jnp.bfloat16)
    split = rows.shape[1] // 2
    zero = jnp.zeros((1, split), jnp.float32)
    cut = [rows[i : i + 1, at : at + split] for at in (0, split) for i in (8, 9)]
    bias_ref[...] = jnp.concatenate([cut[0], zero, cut[1], cut[2], zero, cut[3]], axis=1)
    b_in_ref[...] = jnp.concatenate([shard[i : i + 1] for shard in shards for i in range(10, 14)], axis=1)


def unpack(at, packed, own):
    n_fsdp, _, step = packed.shape
    width = n_fsdp * step
    if step % 32:
        packed = flip_by(packed, 0, own)
        rows = packed.transpose(1, 0, 2).reshape(16, width)
        split = width // 2
        zero = jnp.zeros((split,))
        bias = [p for h in (0, split) for p in (rows[8, h : h + split], zero, rows[9, h : h + split])]
        return rows.astype(jnp.bfloat16), jnp.concatenate(bias)[None], packed[:, 10:14].reshape(1, 4 * width)
    return pl.pallas_call(
        unpack_kernel,
        in_specs=[pl.BlockSpec(memory_space=pltpu.SMEM), pl.BlockSpec(memory_space=pltpu.VMEM)],
        out_specs=[pl.BlockSpec(memory_space=pltpu.VMEM)] * 3,
        out_shape=[
            jax.ShapeDtypeStruct((16, width), jnp.bfloat16),
            jax.ShapeDtypeStruct((1, 3 * width), jnp.float32),
            jax.ShapeDtypeStruct((1, 4 * width), jnp.float32),
        ],
        name="unpack",
    )(at, packed)


def attend_kernel(docs, len_ref, q_ref, k_ref, v_ref, ctx_ref, inv_ref, p_ref):
    seq = q_ref.shape[0] // docs
    lane = lax.broadcasted_iota(jnp.int32, (seq, 128), 1)
    row = lax.broadcasted_iota(jnp.int32, (seq, 128), 0)
    low = lane < 64
    zero, one = jnp.zeros((seq, 128), jnp.bfloat16), jnp.ones((seq, 128), jnp.bfloat16)
    heads = []
    for doc in range(docs):
        here = slice(doc * seq, (doc + 1) * seq)
        query, keys, values = q_ref[here], k_ref[here], v_ref[here]
        unused = jnp.where(row >= len_ref[doc], -1e30, 0.0).astype(jnp.bfloat16)
        for head in (0, 1):
            mine = low if head == 0 else ~low
            spare = lane == 64 - 64 * head
            left = jnp.where(mine, query, jnp.where(spare, one, zero))
            heads.append((left, jnp.where(mine, keys, jnp.where(spare, unused, zero)), jnp.where(mine, values, one)))
    later = dot_cols(*heads[0][:2])
    parts = []
    for i, (_, _, values) in enumerate(heads):
        scores = later
        if i + 1 < len(heads):
            later = dot_cols(*heads[i + 1][:2])
        doc, head = i // 2, i % 2
        expo = jnp.exp(scores - jnp.max(scores, axis=1, keepdims=True)).astype(jnp.bfloat16)
        p_ref[doc, head] = expo
        parts.append(dot(expo, values))
        if head == 1:
            here = slice(doc * seq, (doc + 1) * seq)
            inv = 1.0 / pltpu.roll(jnp.where(low, parts[i], parts[i - 1]), 64, axis=1)
            inv_ref[here] = inv
            ctx_ref[here] = (jnp.where(low, parts[i - 1], parts[i]) * inv).astype(jnp.bfloat16)


def attend(lengths, qkv):
    docs = lengths.shape[0]
    count, cols = qkv.shape[1:]
    seq, n_pair = count // docs, cols // 384

    def part(which):
        return pl.BlockSpec((None, count, 128), lambda i, *_: (i // n_pair, 0, which * n_pair + i % n_pair))

    out = pl.BlockSpec((count, 128), lambda i, *_: (0, i))
    return call(
        functools.partial(attend_kernel, docs),
        (2 * n_pair,),
        [part(0), part(1), part(2)],
        [out, out, pl.BlockSpec((None, None, docs, 2, seq, seq), lambda i, *_: (i // n_pair, i % n_pair, 0, 0, 0, 0))],
        [
            jax.ShapeDtypeStruct((count, 2 * cols // 3), jnp.bfloat16),
            jax.ShapeDtypeStruct((count, 2 * cols // 3), jnp.float32),
            jax.ShapeDtypeStruct((2, n_pair, docs, 2, seq, seq), jnp.bfloat16),
        ],
        flops=2 * docs * n_pair * 2 * seq * seq * 256 * 4,
        prefetch=1,
        name="attend",
    )(lengths, qkv, qkv, qkv)


def norm(resid):
    center = resid - jnp.mean(resid, axis=1, keepdims=True)
    inv = lax.rsqrt(jnp.mean(center * center, axis=1, keepdims=True) + EPSILON)
    return center * inv, inv


def norm_back(grad, normal, inv, gain):
    scaled = grad * gain
    return inv * (
        scaled
        - jnp.mean(scaled, axis=1, keepdims=True)
        - normal * jnp.mean(scaled * normal, axis=1, keepdims=True)
    )


def gelu_parts(u):
    expo = jnp.exp(u * u * -0.5)
    t = 1.0 / (1.0 + STEEP * jnp.abs(u))
    poly = TAIL[5]
    for coef in TAIL[4::-1]:
        poly = poly * t + coef
    tail = expo * (t * poly)
    phi = jnp.where(u >= 0, 1.0 - tail, tail)
    return phi, phi + u * (expo * 0.3989422804014327)


def sum_rows(value):
    return jnp.sum(value, axis=0, keepdims=True)


def start_sums(*refs):
    @pl.when(pl.program_id(0) == 0)
    def _():
        for ref in refs:
            ref[...] = jnp.zeros_like(ref)


def wide_of(rows, *indices):
    rows = rows.astype(jnp.float32)
    return [rows[i : i + 1] for i in indices]


def ffn_kernel(
    n_z,
    n_mid,
    at_ref,
    flag_ref,
    x_ref,
    ctx_ref,
    cot_ref,
    row_ref,
    b_in_ref,
    *refs,
):
    mid, down = refs[:n_mid], refs[n_mid:-15]
    out_ref, low_ref, act_ref, dbranch_ref, dhidden_ref, dattn_ref, dresid_ref, dctx_ref = refs[-15:-7]
    sums_ref, in_sums_ref, wo_ref, wi_ref, wd_ref, slope_ref, sems = refs[-7:]
    first = pl.program_id(0) == 0
    width = x_ref.shape[1]
    chunks = range(0, wi_ref.shape[1], width)

    start_sums(sums_ref, in_sums_ref)

    @pl.when(first)
    def _():
        half = wi_ref.shape[1] // 2
        load(at_ref, mid, n_z, [(half, width // 2, wo_ref, sems.at[0])])
        load(at_ref, mid, n_z, [(0, half, wi_ref, sems.at[1])])
        load(at_ref, down, n_z, [(0, width // 2, wd_ref, sems.at[2])])
        loaded(wo_ref, sems.at[0])
        loaded(wi_ref, sems.at[1])
        loaded(wd_ref, sems.at[2])

    b_out, gain1, shift1, b_down, gain2, shift2 = wide_of(row_ref[...], 2, 3, 4, 5, 6, 7)

    def chain(here):
        flags = flag_ref[:, here]
        embed = x_ref[here].astype(jnp.float32) + dot_rows(flags, row_ref[...])
        resid1 = embed + dot(ctx_ref[here], wo_ref[...]) + b_out
        yield
        normal1, inv1 = norm(resid1)
        normed = normal1 * gain1 + shift1
        normed_low = normed.astype(jnp.bfloat16)
        low_ref[here] = normed_low
        branch = normed + b_down
        yield
        for at in chunks:
            cols = slice(at, at + width)
            hidden = dot(normed_low, wi_ref[:, cols]) + b_in_ref[:, cols]
            phi, slope = gelu_parts(hidden)
            slope_ref[here, cols] = slope
            activated = (hidden * phi).astype(jnp.bfloat16)
            act_ref[here, cols] = activated
            branch = branch + dot(activated, wd_ref[cols, :])
            yield
        normal2, inv2 = norm(branch)
        out_ref[here] = (normal2 * gain2 + shift2).astype(jnp.bfloat16)
        grad = cot_ref[here].astype(jnp.float32)
        dresid2 = norm_back(grad, normal2, inv2, gain2)
        dbranch = dresid2.astype(jnp.bfloat16)
        dbranch_ref[here] = dbranch
        sums_ref[0:1] += sum_rows(grad * normal2)
        sums_ref[1:2] += sum_rows(grad)
        sums_ref[2:3] += sum_rows(dbranch.astype(jnp.float32))
        dnormed = dresid2
        yield
        for at in chunks:
            cols = slice(at, at + width)
            dhidden = (dot_cols(dbranch, wd_ref[cols, :]) * slope_ref[here, cols]).astype(jnp.bfloat16)
            dhidden_ref[here, cols] = dhidden
            in_sums_ref[0:1, cols] += sum_rows(dhidden.astype(jnp.float32))
            dnormed = dnormed + dot_cols(dhidden, wi_ref[:, cols])
            yield
        dresid1 = norm_back(dnormed, normal1, inv1, gain1)
        dattn = dresid1.astype(jnp.bfloat16)
        dresid_ref[here] = dresid1
        dattn_ref[here] = dattn
        sums_ref[3:4] += sum_rows(dnormed * normal1)
        sums_ref[4:5] += sum_rows(dnormed)
        sums_ref[5:6] += sum_rows(dattn.astype(jnp.float32))
        rest = (dresid1 - dattn.astype(jnp.float32)).astype(jnp.bfloat16)
        sums_ref[8:24] += dot(flags, dattn) + dot(flags, rest)
        yield
        dctx_ref[here] = dot_cols(dattn, wo_ref[...]).astype(jnp.bfloat16)

    count = x_ref.shape[0] // PART
    running = [chain(slice(i * PART, (i + 1) * PART)) for i in range(count)]
    offset = OFFSET
    step = 0
    while running:
        alive = []
        for number, one in enumerate(running):
            if step >= number * offset and next(one, "end") == "end":
                continue
            alive.append(one)
        running = alive
        step += 1


def ffn(at, flags, x, ctx, cot, rows, b_in, mid, down, n_z):
    count, width = x.shape
    ff_width = b_in.shape[1]
    low = jax.ShapeDtypeStruct((count, width), jnp.bfloat16)

    def rows_of(cols):
        return pl.BlockSpec((FFN_TILE, cols), lambda i, *_: (i, 0))

    wide = jax.ShapeDtypeStruct((count, ff_width), jnp.bfloat16)
    return call(
        functools.partial(ffn_kernel, n_z, len(mid)),
        (count // FFN_TILE,),
        [pl.BlockSpec((16, FFN_TILE), lambda i, *_: (0, i))]
        + [rows_of(width)] * 3
        + [whole((16, width)), whole((1, ff_width))]
        + [ANY] * (len(mid) + len(down)),
        [rows_of(width)] * 2
        + [rows_of(ff_width), rows_of(width), rows_of(ff_width)]
        + [rows_of(width)] * 3
        + [whole((24, width)), whole((8, ff_width))],
        [low, low, wide, low, wide, low, jax.ShapeDtypeStruct((count, width), jnp.float32), low]
        + [jax.ShapeDtypeStruct((24, width), jnp.float32), jax.ShapeDtypeStruct((8, ff_width), jnp.float32)],
        [
            pltpu.VMEM((width, width), jnp.bfloat16),
            pltpu.VMEM((width, ff_width), jnp.bfloat16),
            pltpu.VMEM((ff_width, width), jnp.bfloat16),
            pltpu.VMEM((FFN_TILE, ff_width), jnp.float32),
            pltpu.SemaphoreType.DMA((3,)),
        ],
        4 * count * width * (width + 2 * ff_width),
        1,
        name="ffn",
    )(at, flags, x, ctx, cot, rows, b_in, *mid, *down)


def split_sum(at_ref, grad, got_ref, away_ref, stay_ref, sum_ref, lanes):
    sum_ref[:, lanes] = (grad + got_ref[:, lanes].astype(jnp.float32)).astype(jnp.bfloat16)
    y, c, x = at_ref[0], at_ref[1], at_ref[3]
    rows = away_ref.shape[2]
    for z in range(away_ref.shape[0]):
        for b in (0, 1):
            for ref, this_x, this_y in ((away_ref, 1 - x, 1 - y), (stay_ref, x, y)):
                block = jnp.where(c == 0, this_x * 2 + b, b * 2 + this_y) + z * 4
                ref[z, b, :, lanes] = sum_ref[pl.ds(pl.multiple_of(block * rows, rows), rows), lanes]


def grad_kernel(n_first, first_z, at_ref, *refs):
    *lefts, got_ref, away_ref, stay_ref, sum_ref = refs if first_z else (*refs[:-1], None, None, refs[-1], None)
    step = pl.program_id(0)

    def put(left_ref, right_ref):
        grad = dot_rows(left_ref[...], right_ref[...])
        lanes = slice(0, grad.shape[1])
        if not first_z:
            stay_ref[:, lanes] = grad.astype(jnp.bfloat16)
            return
        split_sum(at_ref, grad, got_ref, away_ref, stay_ref, sum_ref, lanes)

    if len(lefts) == 2:
        put(*lefts)
        return
    pl.when(step < n_first)(lambda: put(lefts[0], lefts[1]))
    pl.when(step >= n_first)(lambda: put(lefts[2], lefts[3]))


def grads(at, half, parts, got, n_z, tile, name):
    count, rows = parts[0][0].shape
    width = sum(cols for _, _, cols in parts)
    tall = rows > 2 * width
    n_first = (rows if tall else parts[0][2]) // tile
    steps = n_first + len(parts) - 1
    specs, arrays = [], []
    for left, right, cols in parts:
        if tall:
            specs += [pl.BlockSpec((count, tile), lambda i, *_: (0, i))]
            specs += [pl.BlockSpec((count, cols), lambda i, at_ref: (0, at_ref[4]))]
        else:
            n_tile = max(cols // tile, 1)
            start = n_tile if right.shape[1] > cols else 0
            specs += [
                whole((count, rows)),
                pl.BlockSpec(
                    (count, min(tile, cols)),
                    lambda i, at_ref, n=n_tile, start=start: (0, at_ref[4] * start + jnp.minimum(i, n - 1)),
                ),
            ]
        arrays += [left, right]
    at = jnp.concatenate([at, half])
    block = rows // (4 * n_z)
    shape = (tile, width) if tall else (rows, tile)
    spec = pl.BlockSpec(shape, (lambda i, *_: (i, 0)) if tall else (lambda i, *_: (0, i)))
    flops = 2 * count * rows * width
    plain = functools.partial(grad_kernel, n_first, False)
    fused = got is not None and block % 16 == 0
    if not fused:
        grad = call(
            plain, (steps,), specs, spec, jax.ShapeDtypeStruct((rows, width), jnp.bfloat16), flops=flops, prefetch=1, name=name
        )(at, *arrays)
        if got is None:
            return grad
        stay, away = sum_core(grad, got, at, n_z)
        return away, stay
    by_z = shape[0] // (4 * block)
    split = pl.BlockSpec(
        (by_z, 2, block, shape[1]), (lambda i, *_: (i, 0, 0, 0)) if tall else (lambda i, *_: (0, 0, 0, i))
    )
    return call(
        functools.partial(grad_kernel, n_first, True),
        (steps,),
        specs + [spec],
        [split] * 2,
        [jax.ShapeDtypeStruct((n_z, 2, block, width), jnp.bfloat16)] * 2,
        [pltpu.VMEM(shape, jnp.bfloat16)],
        flops=flops,
        prefetch=1,
        name=name,
    )(at, *arrays, got)


def attend_back_kernel(
    docs, fused, at_ref, q_ref, k_ref, v_ref, ctx_ref, inv_ref, p_ref, dctx_ref, low_ref, flag_ref, *refs
):
    got_ref, out_ref, sums_ref, *grads_ref = refs if fused else (None, *refs)
    pair = pl.program_id(0)
    seq = q_ref.shape[0] // docs
    third = out_ref.shape[1] // 3
    lane = lax.broadcasted_iota(jnp.int32, (seq, 128), 1)
    low = lane < 64
    zero, one = jnp.zeros((seq, 128), jnp.bfloat16), jnp.ones((seq, 128), jnp.bfloat16)
    for doc in range(docs):
        here = slice(doc * seq, (doc + 1) * seq)
        query, keys, values = q_ref[here], k_ref[here], v_ref[here]
        dctx = (dctx_ref[here].astype(jnp.float32) * inv_ref[here]).astype(jnp.bfloat16)
        product = dctx.astype(jnp.float32) * ctx_ref[here].astype(jnp.float32)
        grads = []
        for head in (0, 1):
            mine = low if head == 0 else ~low
            spare = lane == 64 - 64 * head
            fine = lane == 65 - 64 * head
            delta = jnp.sum(jnp.where(mine, product, 0.0), axis=1, keepdims=True)
            coarse = delta.astype(jnp.bfloat16)
            rest = (delta - coarse.astype(jnp.float32)).astype(jnp.bfloat16)
            left = jnp.where(mine, dctx, jnp.where(spare, -coarse, jnp.where(fine, -rest, zero)))
            expo = p_ref[doc, head]
            dprobs = dot_cols(left, jnp.where(mine, values, jnp.where(spare | fine, one, zero)))
            dscores = (expo.astype(jnp.float32) * dprobs).astype(jnp.bfloat16)
            grads.append((dot(dscores, keys) * 0.125, dot_rows(dscores, query), dot_rows(expo, dctx)))
        for which in range(3):
            grad = jnp.where(low, grads[0][which], grads[1][which]).astype(jnp.bfloat16)
            out_ref[here, pl.ds(pl.multiple_of(which * third + pair * 128, 128), 128)] = grad

    @pl.when(pair == pl.num_programs(0) - 1)
    def _():
        sums_ref[...] = dot(flag_ref[...], out_ref[...])
        grad = dot_rows(low_ref[...], out_ref[...])
        if fused:
            split_sum(at_ref, grad, got_ref, *grads_ref, slice(0, 3 * third))
        else:
            grads_ref[0][...] = grad.astype(jnp.bfloat16)


def attend_back(at, half, docs, qkv, ctx, inv, expo, dctx, low, flags, got, n_z):
    count, cols = qkv.shape[1:]
    seq, n_pair = count // docs, cols // 384
    rows = low.shape[1]

    def part(which):
        return pl.BlockSpec((None, count, 128), lambda i, at_ref: (at_ref[4], 0, which * n_pair + i))

    one = pl.BlockSpec((count, 128), lambda i, at_ref: (0, at_ref[4] * n_pair + i))
    block = rows // (4 * n_z)
    fused = got is not None and block % 16 == 0
    shape = (n_z, 2, block, cols) if fused else (rows, cols)
    more = [whole((rows, cols))] if fused else []
    dqkv, sums, *out = call(
        functools.partial(attend_back_kernel, docs, fused),
        (n_pair,),
        [part(0), part(1), part(2), one, one]
        + [pl.BlockSpec((None, None, docs, 2, seq, seq), lambda i, at_ref: (at_ref[4], i, 0, 0, 0, 0)), one]
        + [whole((count, rows)), whole((16, count))]
        + more,
        [whole((count, cols)), whole((16, cols))] + [whole(shape)] * (2 if fused else 1),
        [jax.ShapeDtypeStruct((count, cols), jnp.bfloat16), jax.ShapeDtypeStruct((16, cols), jnp.float32)]
        + [jax.ShapeDtypeStruct(shape, jnp.bfloat16)] * (2 if fused else 1),
        [pltpu.VMEM((rows, cols), jnp.bfloat16)] if fused else (),
        flops=docs * n_pair * 2 * seq * seq * 256 * 10 + 2 * count * rows * cols,
        prefetch=1,
        name="attend_back",
    )(jnp.concatenate([at, half]), qkv, qkv, qkv, ctx, inv, expo, dctx, low, flags, *([got] if fused else []))
    if got is None or fused:
        return dqkv, sums, *out
    stay, away = sum_core(out[0], got, at, n_z)
    return dqkv, sums, away, stay


def embed_grad_kernel(n_z, side, at_ref, before_ref, dqkv_ref, *refs):
    pieces, (out_ref, w_ref, sem) = refs[:-3], refs[-3:]

    @pl.when(pl.program_id(0) == 0)
    def _():
        load(at_ref, pieces, n_z, [(0, w_ref.shape[1], w_ref, sem)], (side,))
        loaded(w_ref, sem)

    out_ref[...] = (before_ref[...] + dot_cols(dqkv_ref[...], w_ref[...])).astype(out_ref.dtype)


def embed_grad(at, before, dqkv, side, pieces, n_z, dtype):
    count, width = before.shape
    cols = dqkv.shape[1]
    return call(
        functools.partial(embed_grad_kernel, n_z, side),
        (count // TILE,),
        [tiles(width), tiles(cols)] + [ANY] * len(pieces),
        tiles(width),
        jax.ShapeDtypeStruct((count, width), dtype),
        [pltpu.VMEM((width, cols), jnp.bfloat16), pltpu.SemaphoreType.DMA],
        2 * count * width * cols,
        1,
        name="embed_grad",
    )(at, before, dqkv, *pieces)


def pack_kernel(at_ref, sums_ref, in_ref, mine_ref, theirs_ref, out_ref):
    core = at_ref[1]
    width = sums_ref.shape[1]
    split = width // 2
    mine, theirs = mine_ref[...], theirs_ref[...]
    low, high = jnp.where(core == 0, mine, theirs), jnp.where(core == 0, theirs, mine)
    out_ref[...] = jnp.zeros_like(out_ref)
    places = [(0, 15, 0), (1, 15, 2)] + [(16 + 3 * flag + part, flag, part) for flag in (0, 1) for part in range(3)]
    for row, flag, part in places:
        cols = slice(part * split, (part + 1) * split)
        out_ref[row : row + 1, :split] = low[flag : flag + 1, cols]
        out_ref[row : row + 1, split:] = high[flag : flag + 1, cols]
    for row, source in enumerate((5, 3, 4, 8, 9, 2, 0, 1), 2):
        out_ref[row : row + 1, :] = sums_ref[source : source + 1, :]
    for i in range(4):
        out_ref[11 + i : 12 + i, :] = in_ref[0:1, i * width : (i + 1) * width]


def pack(at, sums, in_sums, mine, theirs):
    return pl.pallas_call(
        pack_kernel,
        in_specs=[pl.BlockSpec(memory_space=pltpu.SMEM)] + [pl.BlockSpec(memory_space=pltpu.VMEM)] * 4,
        out_specs=pl.BlockSpec(memory_space=pltpu.VMEM),
        out_shape=jax.ShapeDtypeStruct((24, sums.shape[1]), jnp.float32),
        name="pack",
    )(at, sums, in_sums, mine, theirs)


def body(
    layer_input,
    masked,
    replaced,
    lengths,
    w_qkv,
    b_q,
    b_v,
    w_out,
    b_out,
    gain1,
    shift1,
    mask_vec,
    repl_vec,
    w_in,
    b_in,
    w_down,
    b_down,
    gain2,
    shift2,
    cotangent,
):
    doc_count, seq_len, width = layer_input.shape
    tok_count = doc_count * seq_len
    n_fsdp = lax.axis_size("fsdp")
    n_z = n_fsdp // 2
    wires = wiring(n_fsdp)
    rep, own = lax.axis_index("rep"), lax.axis_index("fsdp")
    at = jnp.stack([rep // 2, rep % 2, own // 2, own % 2]).astype(jnp.int32)
    y, c = at[0], at[1]
    ff_width = w_in.shape[1]
    split = width // 2
    step = width // n_fsdp

    def quarter(weight):
        rows, cols = weight.shape[0] // 2, weight.shape[1] // 2
        return lax.dynamic_slice(weight, (y * rows, c * cols), (rows, cols))

    vectors = jnp.stack((mask_vec, repl_vec, b_out, gain1, shift1, b_down, gain2, shift2, b_q, b_v))
    packed = jnp.concatenate([vectors, b_in.reshape(-1, step), jnp.zeros((2, step), b_in.dtype)])
    packed = packed.astype(jnp.float32)[None]
    first_attn = jnp.concatenate([quarter(w_qkv[:, i * width : (i + 1) * width]) for i in range(3)], axis=1)
    first_mid = jnp.concatenate([quarter(w_in), quarter(w_out)], axis=1)
    first_down = quarter(w_down)

    attn = gather_z(first_attn, wires)
    attn, packed = tie(attn, packed)
    got_attn = send(attn, wires["first"])
    packed = gather_z(grow(packed, send(packed, wires["x"])), wires)
    got_attn, first_mid, packed = tie(got_attn, first_mid, packed)
    rows, bias, b_in = unpack(at, packed, own)
    flags = jnp.stack([masked.reshape(tok_count), replaced.reshape(tok_count)]).astype(jnp.bfloat16)
    flags = jnp.concatenate([flags, jnp.zeros((13, tok_count), jnp.bfloat16), jnp.ones((1, tok_count), jnp.bfloat16)])
    x = layer_input.reshape(tok_count, width)
    cot = cotangent.reshape(tok_count, width)
    attn = grow(attn, got_attn)
    got_attn = send(attn, wires["second"])
    mid = gather_z(first_mid, wires)
    mid, got_attn, first_down, rows = tie(mid, got_attn, first_down, rows)
    got_mid = send(mid, wires["first"])
    pieces = (attn, got_attn, send(attn, wires["core"]), send(got_attn, wires["core"]))
    got_down = send_all([first_down] * (n_z - 1), wires["z"])
    got_mid, got_down, rows = tie(got_mid, got_down, rows)
    mid = grow(mid, got_mid)
    down = jnp.concatenate([first_down] + got_down)
    rows, mid, down = tie(rows, mid, down)
    got_mid = send(mid, wires["second"])
    got_down = send(down, wires["first"])
    own_attn, other_attn = pieces_of(*pieces, at, n_z)
    w_attn = own_attn + other_attn

    qkv, embed_low = project(at, flags, x, rows, bias, w_attn, n_z)
    qkv, got_down = tie(qkv, got_down)
    down = grow(down, got_down)
    qkv, down = tie(qkv, down)
    got_down = send(down, wires["second"])
    other_mid = send(mid, wires["core"])
    other_down = send(down, wires["core"])
    ctx, inv, expo = attend(lengths, qkv)
    ctx, got_mid, got_down, other_mid, other_down = tie(ctx, got_mid, got_down, other_mid, other_down)
    w_mid = sum(pieces_of(mid, got_mid, other_mid, send(got_mid, wires["core"]), at, n_z), ())
    w_back = sum(pieces_of(down, got_down, other_down, send(got_down, wires["core"]), at, n_z), ())
    out, normed_low, activated, dbranch, dhidden, dattn, dresid1, dctx, sums, in_sums = ffn(
        at, flags, x, ctx, cot, rows, b_in, w_mid, w_back, n_z
    )

    mine, theirs = c[None], 1 - c[None]
    part_d = [(activated, dbranch, split)]
    part_m = [(normed_low, dhidden, ff_width // 2), (ctx, dattn, split)]
    give_m = grads(at, theirs, part_m, None, n_z, width, "mid_give")
    activated, give_m = tie(activated, give_m)
    part_d = [(activated, dbranch, split)]
    got_m = send(give_m, wires["core"])
    give_d = grads(at, theirs, part_d, None, n_z, width, "down_give")
    got_m, give_d = tie(got_m, give_d)
    got_d = send(give_d, wires["core"])
    give_m, keep_m = grads(at, mine, part_m, got_m, n_z, width, "mid_keep")
    give_m, got_d = tie(give_m, got_d)
    got_m = send(give_m, wires["second"])
    give_d, keep_d = grads(at, mine, part_d, got_d, n_z, width, "down_keep")
    give_d, dctx = tie(give_d, dctx)
    got_d = send(give_d, wires["second"])
    dqkv_theirs, sums_theirs, give_a = attend_back(
        at, theirs, doc_count, qkv, ctx, inv, expo, dctx, embed_low, flags, None, n_z
    )
    got_d, got_m, give_a = tie(got_d, got_m, give_a)
    keep_m, give_m = sum_second(keep_m, got_m, at)
    keep_d, give_d = sum_second(keep_d, got_d, at)
    give_m, give_d, give_a, dqkv_theirs = tie(give_m, give_d, give_a, dqkv_theirs)
    got_m = send(give_m, wires["first"])
    got_a = send(give_a, wires["core"])
    dembed = embed_grad(at, dresid1, dqkv_theirs, 1, other_attn, n_z, jnp.float32)
    got_m, got_a, dembed = tie(got_m, got_a, dembed)
    keep_m, give_m = sum_first(keep_m, got_m, at)
    give_m, give_d, got_a = tie(give_m, give_d, got_a)
    got_m = send_all(give_m, wires["z"])
    got_d = send(give_d, wires["first"])
    dqkv_mine, sums_mine, give_a, keep_a = attend_back(
        at, mine, doc_count, qkv, ctx, inv, expo, dctx, embed_low, flags, got_a, n_z
    )
    got_d, got_m, give_a = tie(got_d, got_m, give_a)
    got_a = send(give_a, wires["second"])
    keep_d, give_d = sum_first(keep_d, got_d, at)
    packed = pack(at, sums, in_sums, sums_mine, sums_theirs)
    give_d, packed, dqkv_mine = tie(give_d, packed, dqkv_mine)
    got_d = send_all(give_d, wires["z"])
    got = send(packed, wires["x"])
    grad_input = embed_grad(at, dembed, dqkv_mine, 0, own_attn, n_z, jnp.bfloat16)
    owned_m = sum_z(keep_m, got_m)
    got_a, got_d, got, grad_input, owned_m = tie(got_a, got_d, got, grad_input, owned_m)
    keep_a, give_a = sum_second(keep_a, got_a, at)
    packed = packed + got
    give_a, packed, got_d = tie(give_a, packed, got_d)
    got_a = send(give_a, wires["first"])
    got_m = send(owned_m, wires["rep"][1])
    for pairs in wires["z_bits"]:
        packed = packed + send(packed, pairs)
    owned_d = sum_z(keep_d, got_d)
    got_a, got_m, packed, owned_d = tie(got_a, got_m, packed, owned_d)
    keep_a, give_a = sum_first(keep_a, got_a, at)
    give_a, packed, owned_d = tie(give_a, packed, owned_d)
    got_a = send_all(give_a, wires["z"])
    got_d = send(owned_d, wires["rep"][1])
    pair_m = jnp.stack([owned_m, got_m])
    for pairs in (wires["rep"][1], wires["core"]):
        packed = packed + send(packed, pairs)
    got_a, got_d, packed, pair_m = tie(got_a, got_d, packed, pair_m)
    owned_a = sum_z(keep_a, got_a)
    owned_a, packed, got_d, pair_m = tie(owned_a, packed, got_d, pair_m)
    got_a = send_all([owned_a] * 3, wires["rep"])
    pair_d = jnp.stack([owned_d, got_d])
    got_m = send(pair_m, wires["core"])
    got_d = send(pair_d, wires["core"])
    o_small = lax.dynamic_slice(packed, (0, own * step), (16, step))
    o_b_in = lax.dynamic_slice(packed[11:15].reshape(ff_width), (own * (ff_width // n_fsdp),), (ff_width // n_fsdp,))
    through = packed[16:22].reshape(2, 3 * width)
    coarse = through.astype(jnp.bfloat16)
    rest = (through - coarse.astype(jnp.float32)).astype(jnp.bfloat16)
    through = dot_cols(coarse, w_qkv) + dot_cols(rest, w_qkv)
    o_mask, o_repl = o_small[5] + through[0], o_small[6] + through[1]
    o_mid, o_down = blocks_of_pairs(pair_m, got_m, at), blocks_of_pairs(pair_d, got_d, at)
    o_attn = blocks_of(owned_a, got_a, at)

    def join(blocks, cut=slice(None)):
        return jnp.concatenate([jnp.concatenate([block[:, cut] for block in row], axis=1) for row in blocks])

    o_qkv = jnp.concatenate([join(o_attn, slice(i * split, (i + 1) * split)) for i in (0, 1, 2)], axis=1)
    return (
        out.reshape(layer_input.shape),
        grad_input.reshape(layer_input.shape),
        o_qkv,
        o_small[0],
        o_small[1],
        join(o_mid, slice(ff_width // 2, None)),
        o_small[2],
        o_small[3],
        o_small[4],
        o_mask,
        o_repl,
        join(o_mid, slice(0, ff_width // 2)),
        o_b_in,
        join(o_down),
        o_small[7],
        o_small[8],
        o_small[9],
    )


def solution(mesh):
    return jax.shard_map(
        body,
        mesh=mesh,
        in_specs=(
            P(("rep", "fsdp"), None, None),
            P(("rep", "fsdp"), None),
            P(("rep", "fsdp"), None),
            P(("rep", "fsdp")),
            P("fsdp", None),
            P("fsdp"),
            P("fsdp"),
            P("fsdp", None),
            P("fsdp"),
            P("fsdp"),
            P("fsdp"),
            P("fsdp"),
            P("fsdp"),
            P("fsdp", None),
            P("fsdp"),
            P("fsdp", None),
            P("fsdp"),
            P("fsdp"),
            P("fsdp"),
            P(("rep", "fsdp"), None, None),
        ),
        out_specs=(
            P(("rep", "fsdp"), None, None),
            P(("rep", "fsdp"), None, None),
            P("fsdp", None),
            P("fsdp"),
            P("fsdp"),
            P("fsdp", None),
            P("fsdp"),
            P("fsdp"),
            P("fsdp"),
            P("fsdp"),
            P("fsdp"),
            P("fsdp", None),
            P("fsdp"),
            P("fsdp", None),
            P("fsdp"),
            P("fsdp"),
            P("fsdp"),
        ),
        check_vma=False,
    )
```

```python
import functools
import math

import jax
import jax.numpy as jnp
from jax import lax
from jax.experimental import pallas as pl
from jax.experimental.pallas import tpu as pltpu
from jax.sharding import PartitionSpec as P

HEADS = 12
AXES = ("rep", "fsdp")
EPSILON = 1e-05
TILE = 256
FFN_TILE = 512
PART = 256
OFFSET = 1
VMEM_BYTES = 60 * 1024 * 1024
STEEP = 0.28
TAIL = (0.11652066258099363, 0.06749752053058514, 0.2689081593014359, -0.23699088133158833, 0.38987234732742354, -0.10580781763400933)


def wiring(n_fsdp):
    n_z = n_fsdp // 2

    def pairs(move):
        out = []
        for i in range(4 * n_fsdp):
            y, c, z, x = i // (2 * n_fsdp), i // n_fsdp % 2, i % n_fsdp // 2, i % 2
            y2, c2, z2, x2 = move(y, c, z, x)
            out.append((i, ((y2 * 2 + c2) * n_z + z2) * 2 + x2))
        return out

    return {
        "core": pairs(lambda y, c, z, x: (y, 1 - c, z, x)),
        "first": pairs(lambda y, c, z, x: (1 - y, c, z, x) if c == 0 else (y, c, z, 1 - x)),
        "second": pairs(lambda y, c, z, x: (y, c, z, 1 - x) if c == 0 else (1 - y, c, z, x)),
        "z": [pairs(lambda y, c, z, x, m=m: (y, c, z ^ m, x)) for m in range(1, n_z)],
        "rep": [pairs(lambda y, c, z, x, m=m: (y ^ (m // 2), c ^ (m % 2), z, x)) for m in (1, 2, 3)],
        "x": pairs(lambda y, c, z, x: (y, c, z, 1 - x)),
        "z_bits": [pairs(lambda y, c, z, x, b=b: (y, c, z ^ (1 << b), x)) for b in range(n_z.bit_length() - 1)],
    }


def send(value, pairs):
    return lax.ppermute(value, AXES, pairs)


def tie(*values):
    return lax.optimization_barrier(values)


def pick(value, axis, index):
    return lax.dynamic_index_in_dim(value, index, axis, keepdims=False)


def add_low(left, right):
    return (left.astype(jnp.float32) + right.astype(jnp.float32)).astype(jnp.bfloat16)


def flip_by(value, axis, mask):
    for bit in range(value.shape[axis].bit_length() - 1):
        shape = value.shape
        cut = value.reshape(shape[:axis] + (-1, 2, 1 << bit) + shape[axis + 1 :])
        value = jnp.where(mask >> bit & 1 == 1, jnp.flip(cut, axis + 1), cut).reshape(shape)
    return value


def gather_z(piece, wires):
    return jnp.concatenate([piece] + [send(piece, pairs) for pairs in wires["z"]])


def grow(value, got):
    return jnp.concatenate([value, got])


def pieces_of(eight, got, other_eight, other_got, at, n_z):
    rows = eight.shape[0] // (2 * n_z)
    if in_blocks(rows):
        return (eight, got), (other_eight, other_got)
    y, z, x = at[0], at[2], at[3]
    out = []
    for side, source in ((0, grow(eight, got)), (1, grow(other_eight, other_got))):
        blocks = source.reshape(2, 2, n_z, rows, -1)
        blocks = jnp.where(at[1] ^ side == 0, blocks, blocks.swapaxes(0, 1))
        blocks = flip_by(flip_by(flip_by(blocks, 0, x), 1, y), 2, z)
        out.append((blocks.transpose(2, 0, 1, 3, 4).reshape(source.shape),))
    return tuple(out)


def in_blocks(rows):
    return rows % 16 == 0


def sum_core(keep, got, at, n_z):
    y, c, x = at[0], at[1], at[3]
    summed = add_low(keep, got).reshape(n_z, 2, 2, -1, keep.shape[1])
    away = jnp.where(c == 0, pick(summed, 1, 1 - x), pick(summed, 2, 1 - y))
    return jnp.where(c == 0, pick(summed, 1, x), pick(summed, 2, y)), away


def sum_second(keep, got, at):
    spot = jnp.where(at[1] == 0, at[0], at[3])
    return tuple(add_low(pick(keep, 1, which), pick(got, 1, which)) for which in (spot, 1 - spot))


def sum_first(keep, got, at):
    z = at[2]
    sums = [add_low(pick(keep, 0, z ^ m), pick(got, 0, z ^ m)) for m in range(keep.shape[0])]
    return sums[0], sums[1:]


def sum_z(keep, gots):
    total = keep.astype(jnp.float32)
    for got in gots:
        total = total + got.astype(jnp.float32)
    return total.astype(jnp.bfloat16)


def blocks_of(owned, gots, at):
    quarters = jnp.stack([owned] + list(gots))
    return [
        [pick(quarters, 0, (at[0] ^ row) * 2 + (at[1] ^ col)).astype(jnp.float32) for col in (0, 1)] for row in (0, 1)
    ]


def blocks_of_pairs(pair, got, at):
    halves = jnp.stack([pair, got])
    return [
        [pick(pick(halves, 0, at[1] ^ col), 0, at[0] ^ row).astype(jnp.float32) for col in (0, 1)] for row in (0, 1)
    ]


def send_all(values, wires):
    return [send(value, pairs) for value, pairs in zip(values, wires, strict=True)]


def dot(left, right):
    return lax.dot_general(left, right, (((1,), (0,)), ((), ())), preferred_element_type=jnp.float32)


def dot_cols(left, right):
    return lax.dot_general(left, right, (((1,), (1,)), ((), ())), preferred_element_type=jnp.float32)


def dot_rows(left, right):
    return lax.dot_general(left, right, (((0,), (0,)), ((), ())), preferred_element_type=jnp.float32)


def call(kernel, grid, in_specs, out_specs, out_shape, scratch=(), flops=0, prefetch=0, aliases=None, name=None, grant=VMEM_BYTES):
    shapes = out_shape if isinstance(out_shape, list) else [out_shape]
    sizes = [math.prod(s.shape) * jnp.dtype(s.dtype).itemsize for s in shapes]
    return pl.pallas_call(
        kernel,
        grid_spec=pltpu.PrefetchScalarGridSpec(
            num_scalar_prefetch=prefetch, grid=grid, in_specs=in_specs, out_specs=out_specs, scratch_shapes=scratch
        ),
        out_shape=out_shape,
        compiler_params=pltpu.CompilerParams(
            dimension_semantics=("arbitrary",) * len(grid), vmem_limit_bytes=grant
        ),
        cost_estimate=pl.CostEstimate(flops=flops, bytes_accessed=2 * sum(sizes), transcendentals=0),
        input_output_aliases=aliases or {},
        name=name,
    )


def whole(shape):
    return pl.BlockSpec(shape, lambda i, *_: (0,) * len(shape))


def tiles(width):
    return pl.BlockSpec((TILE, width), lambda i, *_: (i, 0))


ANY = pl.BlockSpec(memory_space=pl.ANY)


def load(at_ref, refs, n_z, targets, sides=(0, 1)):
    y, c, z, x = at_ref[0], at_ref[1], at_ref[2], at_ref[3]
    per_side = len(refs) // len(sides)
    for number, side in enumerate(sides):
        core = jnp.bitwise_xor(c, side)
        half = core if len(sides) > 1 else 0
        pieces = refs[number * per_side : (number + 1) * per_side]
        rows = pieces[0].shape[0] // (2 * n_z)
        for first, cols, into, sem in targets:
            lanes = pl.ds(pl.multiple_of(half * cols, 128) if len(sides) > 1 else 0, cols)
            if per_side == 1:
                pltpu.make_async_copy(pieces[0].at[:, pl.ds(first, cols)], into.at[:, lanes], sem).start()
                continue
            for late, ref in enumerate(pieces):
                for b in (0, 1):
                    by_x = jnp.bitwise_xor(x, jnp.where(core == 0, late, b))
                    by_y = jnp.bitwise_xor(y, jnp.where(core == 0, b, late))
                    for m in range(n_z):
                        slot = (jnp.bitwise_xor(z, m) * 2 + by_x) * 2 + by_y
                        pltpu.make_async_copy(
                            ref.at[pl.ds((b * n_z + m) * rows, rows), pl.ds(first, cols)],
                            into.at[pl.ds(pl.multiple_of(slot * rows, rows), rows), lanes],
                            sem,
                        ).start()


def loaded(array, sem):
    pltpu.make_async_copy(array, array, sem).wait()


def qkv_kernel(n_z, at_ref, flag_ref, x_ref, row_ref, bias_ref, *refs):
    pieces, (qkv_ref, low_ref, w_ref, sem) = refs[:-4], refs[-4:]

    @pl.when(pl.program_id(0) == 0)
    def _():
        load(at_ref, pieces, n_z, [(0, w_ref.shape[1] // 2, w_ref, sem)])
        loaded(w_ref, sem)

    embed_low = (x_ref[...].astype(jnp.float32) + dot_rows(flag_ref[...], row_ref[...])).astype(jnp.bfloat16)
    low_ref[...] = embed_low
    out = dot(embed_low, w_ref[...]) + bias_ref[...]
    third = out.shape[1] // 6
    for half in (0, 1):
        at = half * 3 * third
        qkv_ref[half, :, :third] = (out[:, at : at + third] * 0.125).astype(jnp.bfloat16)
        qkv_ref[half, :, third:] = out[:, at + third : at + 3 * third].astype(jnp.bfloat16)


FLAGS = pl.BlockSpec((16, TILE), lambda i, *_: (0, i))


def project(at, flags, x, rows, bias, pieces, n_z):
    count, width = x.shape
    cols = bias.shape[1] // 2
    return call(
        functools.partial(qkv_kernel, n_z),
        (count // TILE,),
        [FLAGS, tiles(width), whole((16, width)), whole((1, 2 * cols))] + [ANY] * len(pieces),
        [pl.BlockSpec((2, TILE, cols), lambda i, *_: (0, i, 0)), tiles(width)],
        [pltpu.HBM((2, count, cols), jnp.bfloat16), pltpu.HBM((count, width), jnp.bfloat16)],
        [pltpu.VMEM((width, 2 * cols), jnp.bfloat16), pltpu.SemaphoreType.DMA],
        4 * count * width * cols,
        1,
        name="project",
        grant=24 << 20,
    )(at, flags, x, rows, bias, *pieces)


def unpack_kernel(at_ref, packed_ref, rows_ref, bias_ref, b_in_ref):
    n_fsdp = packed_ref.shape[0]
    own = at_ref[2] * 2 + at_ref[3]
    shards = [packed_ref[jnp.bitwise_xor(own, f)] for f in range(n_fsdp)]
    rows = jnp.concatenate([shard[:16] for shard in shards], axis=1)
    rows_ref[...] = rows.astype(jnp.bfloat16)
    split = rows.shape[1] // 2
    zero = jnp.zeros((1, split), jnp.float32)
    cut = [rows[i : i + 1, at : at + split] for at in (0, split) for i in (8, 9)]
    bias_ref[...] = jnp.concatenate([cut[0], zero, cut[1], cut[2], zero, cut[3]], axis=1)
    b_in_ref[...] = jnp.concatenate([shard[i : i + 1] for shard in shards for i in range(10, 14)], axis=1)


def unpack(at, packed, own):
    n_fsdp, _, step = packed.shape
    width = n_fsdp * step
    if step % 32:
        packed = flip_by(packed, 0, own)
        rows = packed.transpose(1, 0, 2).reshape(16, width)
        split = width // 2
        zero = jnp.zeros((split,))
        bias = [p for h in (0, split) for p in (rows[8, h : h + split], zero, rows[9, h : h + split])]
        return rows.astype(jnp.bfloat16), jnp.concatenate(bias)[None], packed[:, 10:14].reshape(1, 4 * width)
    return pl.pallas_call(
        unpack_kernel,
        in_specs=[pl.BlockSpec(memory_space=pltpu.SMEM), pl.BlockSpec(memory_space=pltpu.VMEM)],
        out_specs=[pl.BlockSpec(memory_space=pltpu.VMEM)] * 3,
        out_shape=[
            jax.ShapeDtypeStruct((16, width), jnp.bfloat16),
            jax.ShapeDtypeStruct((1, 3 * width), jnp.float32),
            jax.ShapeDtypeStruct((1, 4 * width), jnp.float32),
        ],
        name="unpack",
    )(at, packed)


def attend_kernel(docs, len_ref, q_ref, k_ref, v_ref, ctx_ref, inv_ref, p_ref):
    seq = q_ref.shape[0] // docs
    lane = lax.broadcasted_iota(jnp.int32, (seq, 128), 1)
    row = lax.broadcasted_iota(jnp.int32, (seq, 128), 0)
    low = lane < 64
    zero, one = jnp.zeros((seq, 128), jnp.bfloat16), jnp.ones((seq, 128), jnp.bfloat16)
    heads = []
    for doc in range(docs):
        here = slice(doc * seq, (doc + 1) * seq)
        query, keys, values = q_ref[here], k_ref[here], v_ref[here]
        unused = jnp.where(row >= len_ref[doc], -1e30, 0.0).astype(jnp.bfloat16)
        for head in (0, 1):
            mine = low if head == 0 else ~low
            spare = lane == 64 - 64 * head
            left = jnp.where(mine, query, jnp.where(spare, one, zero))
            heads.append((left, jnp.where(mine, keys, jnp.where(spare, unused, zero)), jnp.where(mine, values, one)))
    later = dot_cols(*heads[0][:2])
    parts = []
    for i, (_, _, values) in enumerate(heads):
        scores = later
        if i + 1 < len(heads):
            later = dot_cols(*heads[i + 1][:2])
        doc, head = i // 2, i % 2
        expo = jnp.exp(scores - jnp.max(scores, axis=1, keepdims=True)).astype(jnp.bfloat16)
        p_ref[doc, head] = expo
        parts.append(dot(expo, values))
        if head == 1:
            here = slice(doc * seq, (doc + 1) * seq)
            inv = 1.0 / pltpu.roll(jnp.where(low, parts[i], parts[i - 1]), 64, axis=1)
            inv_ref[here] = inv
            ctx_ref[here] = (jnp.where(low, parts[i - 1], parts[i]) * inv).astype(jnp.bfloat16)


def attend(lengths, qkv):
    docs = lengths.shape[0]
    count, cols = qkv.shape[1:]
    seq, n_pair = count // docs, cols // 384

    def part(which):
        return pl.BlockSpec((None, count, 128), lambda i, *_: (i // n_pair, 0, which * n_pair + i % n_pair))

    out = pl.BlockSpec((count, 128), lambda i, *_: (0, i))
    return call(
        functools.partial(attend_kernel, docs),
        (2 * n_pair,),
        [part(0), part(1), part(2)],
        [out, out, pl.BlockSpec((None, None, docs, 2, seq, seq), lambda i, *_: (i // n_pair, i % n_pair, 0, 0, 0, 0))],
        [
            jax.ShapeDtypeStruct((count, 2 * cols // 3), jnp.bfloat16),
            jax.ShapeDtypeStruct((count, 2 * cols // 3), jnp.float32),
            jax.ShapeDtypeStruct((2, n_pair, docs, 2, seq, seq), jnp.bfloat16),
        ],
        flops=2 * docs * n_pair * 2 * seq * seq * 256 * 4,
        prefetch=1,
        name="attend",
    )(lengths, qkv, qkv, qkv)


def norm(resid):
    center = resid - jnp.mean(resid, axis=1, keepdims=True)
    inv = lax.rsqrt(jnp.mean(center * center, axis=1, keepdims=True) + EPSILON)
    return center * inv, inv


def norm_back(grad, normal, inv, gain):
    scaled = grad * gain
    return inv * (
        scaled
        - jnp.mean(scaled, axis=1, keepdims=True)
        - normal * jnp.mean(scaled * normal, axis=1, keepdims=True)
    )


def gelu_parts(u):
    expo = jnp.exp(u * u * -0.5)
    t = 1.0 / (1.0 + STEEP * jnp.abs(u))
    poly = TAIL[5]
    for coef in TAIL[4::-1]:
        poly = poly * t + coef
    tail = expo * (t * poly)
    phi = jnp.where(u >= 0, 1.0 - tail, tail)
    return phi, phi + u * (expo * 0.3989422804014327)


def sum_rows(value):
    return jnp.sum(value, axis=0, keepdims=True)


def start_sums(*refs):
    @pl.when(pl.program_id(0) == 0)
    def _():
        for ref in refs:
            ref[...] = jnp.zeros_like(ref)


def wide_of(rows, *indices):
    rows = rows.astype(jnp.float32)
    return [rows[i : i + 1] for i in indices]


def ffn_kernel(
    n_z,
    n_mid,
    at_ref,
    flag_ref,
    x_ref,
    ctx_ref,
    cot_ref,
    row_ref,
    b_in_ref,
    *refs,
):
    mid, down = refs[:n_mid], refs[n_mid:-15]
    out_ref, low_ref, act_ref, dbranch_ref, dhidden_ref, dattn_ref, dresid_ref, dctx_ref = refs[-15:-7]
    sums_ref, in_sums_ref, wo_ref, wi_ref, wd_ref, slope_ref, sems = refs[-7:]
    first = pl.program_id(0) == 0
    width = x_ref.shape[1]
    chunks = range(0, wi_ref.shape[1], width)

    start_sums(sums_ref, in_sums_ref)

    @pl.when(first)
    def _():
        half = wi_ref.shape[1] // 2
        load(at_ref, mid, n_z, [(half, width // 2, wo_ref, sems.at[0])])
        load(at_ref, mid, n_z, [(0, half, wi_ref, sems.at[1])])
        load(at_ref, down, n_z, [(0, width // 2, wd_ref, sems.at[2])])
        loaded(wo_ref, sems.at[0])
        loaded(wi_ref, sems.at[1])
        loaded(wd_ref, sems.at[2])

    b_out, gain1, shift1, b_down, gain2, shift2 = wide_of(row_ref[...], 2, 3, 4, 5, 6, 7)

    def chain(here):
        flags = flag_ref[:, here]
        embed = x_ref[here].astype(jnp.float32) + dot_rows(flags, row_ref[...])
        resid1 = embed + dot(ctx_ref[here], wo_ref[...]) + b_out
        yield
        normal1, inv1 = norm(resid1)
        normed = normal1 * gain1 + shift1
        normed_low = normed.astype(jnp.bfloat16)
        low_ref[here] = normed_low
        branch = normed + b_down
        yield
        for at in chunks:
            cols = slice(at, at + width)
            hidden = dot(normed_low, wi_ref[:, cols]) + b_in_ref[:, cols]
            phi, slope = gelu_parts(hidden)
            slope_ref[here, cols] = slope
            activated = (hidden * phi).astype(jnp.bfloat16)
            act_ref[here, cols] = activated
            branch = branch + dot(activated, wd_ref[cols, :])
            yield
        normal2, inv2 = norm(branch)
        out_ref[here] = (normal2 * gain2 + shift2).astype(jnp.bfloat16)
        grad = cot_ref[here].astype(jnp.float32)
        dresid2 = norm_back(grad, normal2, inv2, gain2)
        dbranch = dresid2.astype(jnp.bfloat16)
        dbranch_ref[here] = dbranch
        sums_ref[0:1] += sum_rows(grad * normal2)
        sums_ref[1:2] += sum_rows(grad)
        sums_ref[2:3] += sum_rows(dbranch.astype(jnp.float32))
        dnormed = dresid2
        yield
        for at in chunks:
            cols = slice(at, at + width)
            dhidden = (dot_cols(dbranch, wd_ref[cols, :]) * slope_ref[here, cols]).astype(jnp.bfloat16)
            dhidden_ref[here, cols] = dhidden
            in_sums_ref[0:1, cols] += sum_rows(dhidden.astype(jnp.float32))
            dnormed = dnormed + dot_cols(dhidden, wi_ref[:, cols])
            yield
        dresid1 = norm_back(dnormed, normal1, inv1, gain1)
        dattn = dresid1.astype(jnp.bfloat16)
        dresid_ref[here] = dresid1
        dattn_ref[here] = dattn
        sums_ref[3:4] += sum_rows(dnormed * normal1)
        sums_ref[4:5] += sum_rows(dnormed)
        sums_ref[5:6] += sum_rows(dattn.astype(jnp.float32))
        rest = (dresid1 - dattn.astype(jnp.float32)).astype(jnp.bfloat16)
        sums_ref[8:24] += dot(flags, dattn) + dot(flags, rest)
        yield
        dctx_ref[here] = dot_cols(dattn, wo_ref[...]).astype(jnp.bfloat16)

    count = x_ref.shape[0] // PART
    running = [chain(slice(i * PART, (i + 1) * PART)) for i in range(count)]
    offset = OFFSET
    step = 0
    while running:
        alive = []
        for number, one in enumerate(running):
            if step >= number * offset and next(one, "end") == "end":
                continue
            alive.append(one)
        running = alive
        step += 1


def ffn(at, flags, x, ctx, cot, rows, b_in, mid, down, n_z):
    count, width = x.shape
    ff_width = b_in.shape[1]
    low = jax.ShapeDtypeStruct((count, width), jnp.bfloat16)

    def rows_of(cols):
        return pl.BlockSpec((FFN_TILE, cols), lambda i, *_: (i, 0))

    wide = jax.ShapeDtypeStruct((count, ff_width), jnp.bfloat16)
    return call(
        functools.partial(ffn_kernel, n_z, len(mid)),
        (count // FFN_TILE,),
        [pl.BlockSpec((16, FFN_TILE), lambda i, *_: (0, i))]
        + [rows_of(width)] * 3
        + [whole((16, width)), whole((1, ff_width))]
        + [ANY] * (len(mid) + len(down)),
        [rows_of(width)] * 2
        + [rows_of(ff_width), rows_of(width), rows_of(ff_width)]
        + [rows_of(width)] * 3
        + [whole((24, width)), whole((8, ff_width))],
        [low, low, wide, low, wide, low, jax.ShapeDtypeStruct((count, width), jnp.float32), low]
        + [jax.ShapeDtypeStruct((24, width), jnp.float32), jax.ShapeDtypeStruct((8, ff_width), jnp.float32)],
        [
            pltpu.VMEM((width, width), jnp.bfloat16),
            pltpu.VMEM((width, ff_width), jnp.bfloat16),
            pltpu.VMEM((ff_width, width), jnp.bfloat16),
            pltpu.VMEM((FFN_TILE, ff_width), jnp.float32),
            pltpu.SemaphoreType.DMA((3,)),
        ],
        4 * count * width * (width + 2 * ff_width),
        1,
        name="ffn",
    )(at, flags, x, ctx, cot, rows, b_in, *mid, *down)


def split_sum(at_ref, grad, got_ref, away_ref, stay_ref, sum_ref, lanes):
    sum_ref[:, lanes] = (grad + got_ref[:, lanes].astype(jnp.float32)).astype(jnp.bfloat16)
    y, c, x = at_ref[0], at_ref[1], at_ref[3]
    rows = away_ref.shape[2]
    for z in range(away_ref.shape[0]):
        for b in (0, 1):
            for ref, this_x, this_y in ((away_ref, 1 - x, 1 - y), (stay_ref, x, y)):
                block = jnp.where(c == 0, this_x * 2 + b, b * 2 + this_y) + z * 4
                ref[z, b, :, lanes] = sum_ref[pl.ds(pl.multiple_of(block * rows, rows), rows), lanes]


def grad_kernel(n_first, first_z, at_ref, *refs):
    *lefts, got_ref, away_ref, stay_ref, sum_ref = refs if first_z else (*refs[:-1], None, None, refs[-1], None)
    step = pl.program_id(0)

    def put(left_ref, right_ref):
        grad = dot_rows(left_ref[...], right_ref[...])
        lanes = slice(0, grad.shape[1])
        if not first_z:
            stay_ref[:, lanes] = grad.astype(jnp.bfloat16)
            return
        split_sum(at_ref, grad, got_ref, away_ref, stay_ref, sum_ref, lanes)

    if len(lefts) == 2:
        put(*lefts)
        return
    pl.when(step < n_first)(lambda: put(lefts[0], lefts[1]))
    pl.when(step >= n_first)(lambda: put(lefts[2], lefts[3]))


def grads(at, parts, got, n_z, tile, name):
    count, rows = parts[0][0].shape
    width = sum(cols for _, _, cols in parts)
    tall = rows > 2 * width
    n_first = (rows if tall else parts[0][2]) // tile
    steps = n_first + len(parts) - 1
    specs, arrays = [], []
    for left, right, cols in parts:
        if tall:
            specs += [pl.BlockSpec((count, tile), lambda i, *_: (0, i))]
            specs += [pl.BlockSpec((count, cols), lambda i, at_ref: (0, at_ref[4]))]
        else:
            n_tile = max(cols // tile, 1)
            start = n_tile if right.shape[1] > cols else 0
            specs += [
                whole((count, rows)),
                pl.BlockSpec(
                    (count, min(tile, cols)),
                    lambda i, at_ref, n=n_tile, start=start: (0, at_ref[4] * start + jnp.minimum(i, n - 1)),
                ),
            ]
        arrays += [left, right]
    block = rows // (4 * n_z)
    shape = (tile, width) if tall else (rows, tile)
    spec = pl.BlockSpec(shape, (lambda i, *_: (i, 0)) if tall else (lambda i, *_: (0, i)))
    flops = 2 * count * rows * width
    plain = functools.partial(grad_kernel, n_first, False)
    fused = got is not None and block % 16 == 0
    if not fused:
        grad = call(
            plain, (steps,), specs, spec, jax.ShapeDtypeStruct((rows, width), jnp.bfloat16), flops=flops, prefetch=1, name=name
        )(at, *arrays)
        if got is None:
            return grad
        stay, away = sum_core(grad, got, at, n_z)
        return away, stay
    by_z = shape[0] // (4 * block)
    split = pl.BlockSpec(
        (by_z, 2, block, shape[1]), (lambda i, *_: (i, 0, 0, 0)) if tall else (lambda i, *_: (0, 0, 0, i))
    )
    return call(
        functools.partial(grad_kernel, n_first, True),
        (steps,),
        specs + [spec],
        [split] * 2,
        [jax.ShapeDtypeStruct((n_z, 2, block, width), jnp.bfloat16)] * 2,
        [pltpu.VMEM(shape, jnp.bfloat16)],
        flops=flops,
        prefetch=1,
        name=name,
    )(at, *arrays, got)


def attend_back_kernel(
    docs, fused, at_ref, q_ref, k_ref, v_ref, ctx_ref, inv_ref, p_ref, dctx_ref, low_ref, flag_ref, *refs
):
    got_ref, out_ref, sums_ref, *grads_ref = refs if fused else (None, *refs)
    pair = pl.program_id(0)
    seq = q_ref.shape[0] // docs
    third = out_ref.shape[1] // 3
    lane = lax.broadcasted_iota(jnp.int32, (seq, 128), 1)
    low = lane < 64
    zero, one = jnp.zeros((seq, 128), jnp.bfloat16), jnp.ones((seq, 128), jnp.bfloat16)
    for doc in range(docs):
        here = slice(doc * seq, (doc + 1) * seq)
        query, keys, values = q_ref[here], k_ref[here], v_ref[here]
        dctx = (dctx_ref[here].astype(jnp.float32) * inv_ref[here]).astype(jnp.bfloat16)
        product = dctx.astype(jnp.float32) * ctx_ref[here].astype(jnp.float32)
        grads = []
        for head in (0, 1):
            mine = low if head == 0 else ~low
            spare = lane == 64 - 64 * head
            fine = lane == 65 - 64 * head
            delta = jnp.sum(jnp.where(mine, product, 0.0), axis=1, keepdims=True)
            coarse = delta.astype(jnp.bfloat16)
            rest = (delta - coarse.astype(jnp.float32)).astype(jnp.bfloat16)
            left = jnp.where(mine, dctx, jnp.where(spare, -coarse, jnp.where(fine, -rest, zero)))
            expo = p_ref[doc, head]
            dprobs = dot_cols(left, jnp.where(mine, values, jnp.where(spare | fine, one, zero)))
            dscores = (expo.astype(jnp.float32) * dprobs).astype(jnp.bfloat16)
            grads.append((dot(dscores, keys) * 0.125, dot_rows(dscores, query), dot_rows(expo, dctx)))
        for which in range(3):
            grad = jnp.where(low, grads[0][which], grads[1][which]).astype(jnp.bfloat16)
            out_ref[here, pl.ds(pl.multiple_of(which * third + pair * 128, 128), 128)] = grad

    @pl.when(pair == pl.num_programs(0) - 1)
    def _():
        sums_ref[...] = dot(flag_ref[...], out_ref[...])
        grad = dot_rows(low_ref[...], out_ref[...])
        if fused:
            split_sum(at_ref, grad, got_ref, *grads_ref, slice(0, 3 * third))
        else:
            grads_ref[0][...] = grad.astype(jnp.bfloat16)


def attend_back(at, docs, qkv, ctx, inv, expo, dctx, low, flags, got, n_z):
    count, cols = qkv.shape[1:]
    seq, n_pair = count // docs, cols // 384
    rows = low.shape[1]

    def part(which):
        return pl.BlockSpec((None, count, 128), lambda i, at_ref: (at_ref[4], 0, which * n_pair + i))

    one = pl.BlockSpec((count, 128), lambda i, at_ref: (0, at_ref[4] * n_pair + i))
    block = rows // (4 * n_z)
    fused = got is not None and block % 16 == 0
    shape = (n_z, 2, block, cols) if fused else (rows, cols)
    more = [whole((rows, cols))] if fused else []
    dqkv, sums, *out = call(
        functools.partial(attend_back_kernel, docs, fused),
        (n_pair,),
        [part(0), part(1), part(2), one, one]
        + [pl.BlockSpec((None, None, docs, 2, seq, seq), lambda i, at_ref: (at_ref[4], i, 0, 0, 0, 0)), one]
        + [whole((count, rows)), whole((16, count))]
        + more,
        [whole((count, cols)), whole((16, cols))] + [whole(shape)] * (2 if fused else 1),
        [jax.ShapeDtypeStruct((count, cols), jnp.bfloat16), jax.ShapeDtypeStruct((16, cols), jnp.float32)]
        + [jax.ShapeDtypeStruct(shape, jnp.bfloat16)] * (2 if fused else 1),
        [pltpu.VMEM((rows, cols), jnp.bfloat16)] if fused else (),
        flops=docs * n_pair * 2 * seq * seq * 256 * 10 + 2 * count * rows * cols,
        prefetch=1,
        name="attend_back",
    )(at, qkv, qkv, qkv, ctx, inv, expo, dctx, low, flags, *([got] if fused else []))
    if got is None or fused:
        return dqkv, sums, *out
    stay, away = sum_core(out[0], got, at, n_z)
    return dqkv, sums, away, stay


def embed_grad_kernel(n_z, side, at_ref, before_ref, dqkv_ref, *refs):
    pieces, (out_ref, w_ref, sem) = refs[:-3], refs[-3:]

    @pl.when(pl.program_id(0) == 0)
    def _():
        load(at_ref, pieces, n_z, [(0, w_ref.shape[1], w_ref, sem)], (side,))
        loaded(w_ref, sem)

    out_ref[...] = (before_ref[...] + dot_cols(dqkv_ref[...], w_ref[...])).astype(out_ref.dtype)


def embed_grad(at, before, dqkv, side, pieces, n_z, dtype):
    count, width = before.shape
    cols = dqkv.shape[1]

    def rows_of(cols):
        return pl.BlockSpec((FFN_TILE, cols), lambda i, *_: (i, 0))

    return call(
        functools.partial(embed_grad_kernel, n_z, side),
        (count // FFN_TILE,),
        [rows_of(width), rows_of(cols)] + [ANY] * len(pieces),
        rows_of(width),
        jax.ShapeDtypeStruct((count, width), dtype),
        [pltpu.VMEM((width, cols), jnp.bfloat16), pltpu.SemaphoreType.DMA],
        2 * count * width * cols,
        1,
        name="embed_grad",
    )(at, before, dqkv, *pieces)


def pack_kernel(at_ref, sums_ref, in_ref, mine_ref, theirs_ref, out_ref):
    core = at_ref[1]
    width = sums_ref.shape[1]
    split = width // 2
    mine, theirs = mine_ref[...], theirs_ref[...]
    low, high = jnp.where(core == 0, mine, theirs), jnp.where(core == 0, theirs, mine)
    out_ref[...] = jnp.zeros_like(out_ref)
    places = [(0, 15, 0), (1, 15, 2)] + [(16 + 3 * flag + part, flag, part) for flag in (0, 1) for part in range(3)]
    for row, flag, part in places:
        cols = slice(part * split, (part + 1) * split)
        out_ref[row : row + 1, :split] = low[flag : flag + 1, cols]
        out_ref[row : row + 1, split:] = high[flag : flag + 1, cols]
    for row, source in enumerate((5, 3, 4, 8, 9, 2, 0, 1), 2):
        out_ref[row : row + 1, :] = sums_ref[source : source + 1, :]
    for i in range(4):
        out_ref[11 + i : 12 + i, :] = in_ref[0:1, i * width : (i + 1) * width]


def pack(at, sums, in_sums, mine, theirs):
    return pl.pallas_call(
        pack_kernel,
        in_specs=[pl.BlockSpec(memory_space=pltpu.SMEM)] + [pl.BlockSpec(memory_space=pltpu.VMEM)] * 4,
        out_specs=pl.BlockSpec(memory_space=pltpu.VMEM),
        out_shape=jax.ShapeDtypeStruct((24, sums.shape[1]), jnp.float32),
        name="pack",
    )(at, sums, in_sums, mine, theirs)


def body(
    layer_input,
    masked,
    replaced,
    lengths,
    w_qkv,
    b_q,
    b_v,
    w_out,
    b_out,
    gain1,
    shift1,
    mask_vec,
    repl_vec,
    w_in,
    b_in,
    w_down,
    b_down,
    gain2,
    shift2,
    cotangent,
):
    doc_count, seq_len, width = layer_input.shape
    tok_count = doc_count * seq_len
    n_fsdp = lax.axis_size("fsdp")
    n_z = n_fsdp // 2
    wires = wiring(n_fsdp)
    rep, own = lax.axis_index("rep"), lax.axis_index("fsdp")
    at = jnp.stack([rep // 2, rep % 2, own // 2, own % 2]).astype(jnp.int32)
    y, c = at[0], at[1]
    ff_width = w_in.shape[1]
    split = width // 2
    step = width // n_fsdp

    def quarter(weight):
        rows, cols = weight.shape[0] // 2, weight.shape[1] // 2
        return lax.dynamic_slice(weight, (y * rows, c * cols), (rows, cols))

    vectors = jnp.stack((mask_vec, repl_vec, b_out, gain1, shift1, b_down, gain2, shift2, b_q, b_v))
    packed = jnp.concatenate([vectors, b_in.reshape(-1, step), jnp.zeros((2, step), b_in.dtype)])
    packed = packed.astype(jnp.float32)[None]
    first_attn = jnp.concatenate([quarter(w_qkv[:, i * width : (i + 1) * width]) for i in range(3)], axis=1)
    first_mid = jnp.concatenate([quarter(w_in), quarter(w_out)], axis=1)
    first_down = quarter(w_down)

    flags = jnp.stack([masked.reshape(tok_count), replaced.reshape(tok_count)]).astype(jnp.bfloat16)
    flags = jnp.concatenate([flags, jnp.zeros((13, tok_count), jnp.bfloat16), jnp.ones((1, tok_count), jnp.bfloat16)])
    attn = gather_z(first_attn, wires)
    mine, theirs = jnp.concatenate([at, c[None]]), jnp.concatenate([at, 1 - c[None]])
    attn, packed, flags, mine, theirs = tie(attn, packed, flags, mine, theirs)
    got_attn = send(attn, wires["first"])
    packed = gather_z(grow(packed, send(packed, wires["x"])), wires)
    got_attn, first_mid, packed = tie(got_attn, first_mid, packed)
    rows, bias, b_in = unpack(at, packed, own)
    x = layer_input.reshape(tok_count, width)
    cot = cotangent.reshape(tok_count, width)
    attn = grow(attn, got_attn)
    got_attn = send(attn, wires["second"])
    mid = gather_z(first_mid, wires)
    mid, got_attn, first_down, rows = tie(mid, got_attn, first_down, rows)
    got_mid = send(mid, wires["first"])
    pieces = (attn, got_attn, send(attn, wires["core"]), send(got_attn, wires["core"]))
    got_down = send_all([first_down] * (n_z - 1), wires["z"])
    got_mid, got_down, rows = tie(got_mid, got_down, rows)
    mid = grow(mid, got_mid)
    down = jnp.concatenate([first_down] + got_down)
    rows, mid, down = tie(rows, mid, down)
    got_mid = send(mid, wires["second"])
    got_down = send(down, wires["first"])
    own_attn, other_attn = pieces_of(*pieces, at, n_z)
    w_attn = own_attn + other_attn

    qkv, embed_low = project(at, flags, x, rows, bias, w_attn, n_z)
    qkv, got_down = tie(qkv, got_down)
    down = grow(down, got_down)
    qkv, down = tie(qkv, down)
    got_down = send(down, wires["second"])
    other_mid = send(mid, wires["core"])
    other_down = send(down, wires["core"])
    ctx, inv, expo = attend(lengths, qkv)
    ctx, got_mid, got_down, other_mid, other_down = tie(ctx, got_mid, got_down, other_mid, other_down)
    w_mid = sum(pieces_of(mid, got_mid, other_mid, send(got_mid, wires["core"]), at, n_z), ())
    w_back = sum(pieces_of(down, got_down, other_down, send(got_down, wires["core"]), at, n_z), ())
    out, normed_low, activated, dbranch, dhidden, dattn, dresid1, dctx, sums, in_sums = ffn(
        at, flags, x, ctx, cot, rows, b_in, w_mid, w_back, n_z
    )

    part_d = [(activated, dbranch, split)]
    part_m = [(normed_low, dhidden, ff_width // 2), (ctx, dattn, split)]
    give_m = grads(theirs, part_m, None, n_z, width, "mid_give")
    activated, give_m = tie(activated, give_m)
    part_d = [(activated, dbranch, split)]
    got_m = send(give_m, wires["core"])
    give_d = grads(theirs, part_d, None, n_z, 2 * width, "down_give")
    got_m, give_d = tie(got_m, give_d)
    got_d = send(give_d, wires["core"])
    give_m, keep_m = grads(mine, part_m, got_m, n_z, width, "mid_keep")
    give_m, got_d = tie(give_m, got_d)
    got_m = send(give_m, wires["second"])
    give_d, keep_d = grads(mine, part_d, got_d, n_z, 2 * width, "down_keep")
    give_d, dctx = tie(give_d, dctx)
    got_d = send(give_d, wires["second"])
    dqkv_theirs, sums_theirs, give_a = attend_back(
        theirs, doc_count, qkv, ctx, inv, expo, dctx, embed_low, flags, None, n_z
    )
    got_d, got_m, give_a = tie(got_d, got_m, give_a)
    keep_m, give_m = sum_second(keep_m, got_m, at)
    keep_d, give_d = sum_second(keep_d, got_d, at)
    give_m, give_d, give_a, dqkv_theirs = tie(give_m, give_d, give_a, dqkv_theirs)
    got_m = send(give_m, wires["first"])
    got_a = send(give_a, wires["core"])
    dembed = embed_grad(at, dresid1, dqkv_theirs, 1, other_attn, n_z, jnp.float32)
    got_m, got_a, dembed = tie(got_m, got_a, dembed)
    keep_m, give_m = sum_first(keep_m, got_m, at)
    give_m, give_d, got_a = tie(give_m, give_d, got_a)
    got_m = send_all(give_m, wires["z"])
    got_d = send(give_d, wires["first"])
    dqkv_mine, sums_mine, give_a, keep_a = attend_back(
        mine, doc_count, qkv, ctx, inv, expo, dctx, embed_low, flags, got_a, n_z
    )
    got_d, got_m, give_a = tie(got_d, got_m, give_a)
    got_a = send(give_a, wires["second"])
    keep_d, give_d = sum_first(keep_d, got_d, at)
    packed = pack(at, sums, in_sums, sums_mine, sums_theirs)
    give_d, packed, dqkv_mine = tie(give_d, packed, dqkv_mine)
    got_d = send_all(give_d, wires["z"])
    got = send(packed, wires["x"])
    grad_input = embed_grad(at, dembed, dqkv_mine, 0, own_attn, n_z, jnp.bfloat16)
    owned_m = sum_z(keep_m, got_m)
    got_a, got_d, got, grad_input, owned_m = tie(got_a, got_d, got, grad_input, owned_m)
    keep_a, give_a = sum_second(keep_a, got_a, at)
    packed = packed + got
    give_a, packed, got_d = tie(give_a, packed, got_d)
    got_a = send(give_a, wires["first"])
    for pairs in wires["z_bits"]:
        packed = packed + send(packed, pairs)
    owned_d = sum_z(keep_d, got_d)
    got_a, packed, owned_d, owned_m = tie(got_a, packed, owned_d, owned_m)
    keep_a, give_a = sum_first(keep_a, got_a, at)
    give_a, packed, owned_d, owned_m = tie(give_a, packed, owned_d, owned_m)
    got_a = send_all(give_a, wires["z"])
    got_m = send(owned_m, wires["rep"][1])
    got_d = send(owned_d, wires["rep"][1])
    got_a, got_d, got_m, packed = tie(got_a, got_d, got_m, packed)
    owned_a = sum_z(keep_a, got_a)
    pair_m, pair_d = jnp.stack([owned_m, got_m]), jnp.stack([owned_d, got_d])
    owned_a, packed, pair_d, pair_m = tie(owned_a, packed, pair_d, pair_m)
    got_a = send_all([owned_a] * 3, wires["rep"])
    got_m = send(pair_m, wires["core"])
    got_d = send(pair_d, wires["core"])
    for pairs in (wires["core"], wires["rep"][1]):
        packed = packed + send(packed, pairs)
    o_small = lax.dynamic_slice(packed, (0, own * step), (16, step))
    o_b_in = lax.dynamic_slice(packed[11:15].reshape(ff_width), (own * (ff_width // n_fsdp),), (ff_width // n_fsdp,))
    through = packed[16:22].reshape(2, 3 * width)
    coarse = through.astype(jnp.bfloat16)
    rest = (through - coarse.astype(jnp.float32)).astype(jnp.bfloat16)
    through = dot_cols(coarse, w_qkv) + dot_cols(rest, w_qkv)
    o_mask, o_repl = o_small[5] + through[0], o_small[6] + through[1]
    o_mid, o_down = blocks_of_pairs(pair_m, got_m, at), blocks_of_pairs(pair_d, got_d, at)
    o_attn = blocks_of(owned_a, got_a, at)

    def join(blocks, cut=slice(None)):
        return jnp.concatenate([jnp.concatenate([block[:, cut] for block in row], axis=1) for row in blocks])

    o_qkv = jnp.concatenate([join(o_attn, slice(i * split, (i + 1) * split)) for i in (0, 1, 2)], axis=1)
    return (
        out.reshape(layer_input.shape),
        grad_input.reshape(layer_input.shape),
        o_qkv,
        o_small[0],
        o_small[1],
        join(o_mid, slice(ff_width // 2, None)),
        o_small[2],
        o_small[3],
        o_small[4],
        o_mask,
        o_repl,
        join(o_mid, slice(0, ff_width // 2)),
        o_b_in,
        join(o_down),
        o_small[7],
        o_small[8],
        o_small[9],
    )


def solution(mesh):
    return jax.shard_map(
        body,
        mesh=mesh,
        in_specs=(
            P(("rep", "fsdp"), None, None),
            P(("rep", "fsdp"), None),
            P(("rep", "fsdp"), None),
            P(("rep", "fsdp")),
            P("fsdp", None),
            P("fsdp"),
            P("fsdp"),
            P("fsdp", None),
            P("fsdp"),
            P("fsdp"),
            P("fsdp"),
            P("fsdp"),
            P("fsdp"),
            P("fsdp", None),
            P("fsdp"),
            P("fsdp", None),
            P("fsdp"),
            P("fsdp"),
            P("fsdp"),
            P(("rep", "fsdp"), None, None),
        ),
        out_specs=(
            P(("rep", "fsdp"), None, None),
            P(("rep", "fsdp"), None, None),
            P("fsdp", None),
            P("fsdp"),
            P("fsdp"),
            P("fsdp", None),
            P("fsdp"),
            P("fsdp"),
            P("fsdp"),
            P("fsdp"),
            P("fsdp"),
            P("fsdp", None),
            P("fsdp"),
            P("fsdp", None),
            P("fsdp"),
            P("fsdp"),
            P("fsdp"),
        ),
        check_vma=False,
    )
```

```python
import functools

import jax
import jax.numpy as jnp
from jax import lax
from jax.experimental import pallas as pl
from jax.experimental.pallas import tpu as pltpu
from jax.sharding import PartitionSpec as P

HEADS = 12
AXES = ("rep", "fsdp")
EPSILON = 1e-05
TILE = 256
FFN_TILE = 512
PART = 256
OFFSET = 1
VMEM_BYTES = 60 * 1024 * 1024
STEEP = 0.28
TAIL = (0.11652066258099363, 0.06749752053058514, 0.2689081593014359, -0.23699088133158833, 0.38987234732742354, -0.10580781763400933)


def wiring(n_fsdp):
    n_z = n_fsdp // 2

    def pairs(move):
        out = []
        for i in range(4 * n_fsdp):
            y, c, z, x = i // (2 * n_fsdp), i // n_fsdp % 2, i % n_fsdp // 2, i % 2
            y2, c2, z2, x2 = move(y, c, z, x)
            out.append((i, ((y2 * 2 + c2) * n_z + z2) * 2 + x2))
        return out

    return {
        "core": pairs(lambda y, c, z, x: (y, 1 - c, z, x)),
        "first": pairs(lambda y, c, z, x: (1 - y, c, z, x) if c == z % 2 else (y, c, z, 1 - x)),
        "second": pairs(lambda y, c, z, x: (y, c, z, 1 - x) if c == z % 2 else (1 - y, c, z, x)),
        "z": [pairs(lambda y, c, z, x, m=m: (y, c, z ^ m, x)) for m in range(1, n_z)],
        "rep": [pairs(lambda y, c, z, x, m=m: (y ^ (m // 2), c ^ (m % 2), z, x)) for m in (1, 2, 3)],
        "x": pairs(lambda y, c, z, x: (y, c, z, 1 - x)),
        "z_bits": [pairs(lambda y, c, z, x, b=b: (y, c, z ^ (1 << b), x)) for b in range(n_z.bit_length() - 1)],
    }


def send(value, pairs):
    return lax.ppermute(value, AXES, pairs)


def tie(*values):
    return lax.optimization_barrier(values)


def pick(value, axis, index):
    return lax.dynamic_index_in_dim(value, index, axis, keepdims=False)


def add_low(left, right):
    return (left.astype(jnp.float32) + right.astype(jnp.float32)).astype(jnp.bfloat16)


def flip_by(value, axis, mask):
    for bit in range(value.shape[axis].bit_length() - 1):
        shape = value.shape
        cut = value.reshape(shape[:axis] + (-1, 2, 1 << bit) + shape[axis + 1 :])
        value = jnp.where(mask >> bit & 1 == 1, jnp.flip(cut, axis + 1), cut).reshape(shape)
    return value


def gather_z(piece, wires):
    return jnp.concatenate([piece] + [send(piece, pairs) for pairs in wires["z"]])


def grow(value, got):
    return jnp.concatenate([value, got])


def pieces_of(eight, got, other_eight, other_got, at, n_z):
    rows = eight.shape[0] // (2 * n_z)
    if in_blocks(rows):
        return (eight, got), (other_eight, other_got)
    y, z, x = at[0], at[2], at[3]
    out = []
    for side, source in ((0, grow(eight, got)), (1, grow(other_eight, other_got))):
        blocks = source.reshape(2, 2, n_z, rows, -1)
        blocks = jnp.where(at[1] ^ side == z % 2, blocks, blocks.swapaxes(0, 1))
        blocks = flip_by(flip_by(flip_by(blocks, 0, x), 1, y), 2, z)
        out.append((blocks.transpose(2, 0, 1, 3, 4).reshape(source.shape),))
    return tuple(out)


def in_blocks(rows):
    return rows % 16 == 0


def sum_core(keep, got, at, n_z):
    y, c, x = at[0], at[1] ^ at[2] % 2, at[3]
    summed = add_low(keep, got).reshape(n_z, 2, 2, -1, keep.shape[1])
    away = jnp.where(c == 0, pick(summed, 1, 1 - x), pick(summed, 2, 1 - y))
    return jnp.where(c == 0, pick(summed, 1, x), pick(summed, 2, y)), away


def sum_second(keep, got, at):
    spot = jnp.where(at[1] == at[2] % 2, at[0], at[3])
    return tuple(add_low(pick(keep, 1, which), pick(got, 1, which)) for which in (spot, 1 - spot))


def sum_first(keep, got, at):
    z = at[2]
    sums = [add_low(pick(keep, 0, z ^ m), pick(got, 0, z ^ m)) for m in range(keep.shape[0])]
    return sums[0], sums[1:]


def sum_z(keep, gots):
    total = keep.astype(jnp.float32)
    for got in gots:
        total = total + got.astype(jnp.float32)
    return total.astype(jnp.bfloat16)


def blocks_of(owned, gots, at):
    quarters = jnp.stack([owned] + list(gots))
    return [
        [pick(quarters, 0, (at[0] ^ row) * 2 + (at[1] ^ col)).astype(jnp.float32) for col in (0, 1)] for row in (0, 1)
    ]


def blocks_of_pairs(pair, got, at):
    halves = jnp.stack([pair, got])
    return [
        [pick(pick(halves, 0, at[1] ^ col), 0, at[0] ^ row).astype(jnp.float32) for col in (0, 1)] for row in (0, 1)
    ]


def send_all(values, wires):
    return [send(value, pairs) for value, pairs in zip(values, wires, strict=True)]


def dot(left, right):
    return lax.dot_general(left, right, (((1,), (0,)), ((), ())), preferred_element_type=jnp.float32)


def dot_cols(left, right):
    return lax.dot_general(left, right, (((1,), (1,)), ((), ())), preferred_element_type=jnp.float32)


def dot_rows(left, right):
    return lax.dot_general(left, right, (((0,), (0,)), ((), ())), preferred_element_type=jnp.float32)


def call(kernel, grid, in_specs, out_specs, out_shape, scratch=(), flops=0, prefetch=0, aliases=None, name=None):
    sizes = [s.size * s.dtype.itemsize for s in jax.tree.leaves(out_shape)]
    return pl.pallas_call(
        kernel,
        grid_spec=pltpu.PrefetchScalarGridSpec(
            num_scalar_prefetch=prefetch, grid=grid, in_specs=in_specs, out_specs=out_specs, scratch_shapes=scratch
        ),
        out_shape=out_shape,
        compiler_params=pltpu.CompilerParams(
            dimension_semantics=("arbitrary",) * len(grid), vmem_limit_bytes=VMEM_BYTES
        ),
        cost_estimate=pl.CostEstimate(flops=flops, bytes_accessed=2 * sum(sizes), transcendentals=0),
        input_output_aliases=aliases or {},
        name=name,
    )


def whole(shape):
    return pl.BlockSpec(shape, lambda i, *_: (0,) * len(shape))


def tiles(width):
    return pl.BlockSpec((TILE, width), lambda i, *_: (i, 0))


ANY = pl.BlockSpec(memory_space=pl.ANY)


def load(at_ref, refs, n_z, targets, sides=(0, 1)):
    y, c, z, x = at_ref[0], at_ref[1], at_ref[2], at_ref[3]
    per_side = len(refs) // len(sides)
    for number, side in enumerate(sides):
        core = jnp.bitwise_xor(c, side)
        half = core if len(sides) > 1 else 0
        pieces = refs[number * per_side : (number + 1) * per_side]
        rows = pieces[0].shape[0] // (2 * n_z)
        for first, cols, into, sem in targets:
            lanes = pl.ds(pl.multiple_of(half * cols, 128) if len(sides) > 1 else 0, cols)
            if per_side == 1:
                pltpu.make_async_copy(pieces[0].at[:, pl.ds(first, cols)], into.at[:, lanes], sem).start()
                continue
            for late, ref in enumerate(pieces):
                for b in (0, 1):
                    by_x = jnp.bitwise_xor(x, jnp.where(core == z % 2, late, b))
                    by_y = jnp.bitwise_xor(y, jnp.where(core == z % 2, b, late))
                    for m in range(n_z):
                        slot = (jnp.bitwise_xor(z, m) * 2 + by_x) * 2 + by_y
                        pltpu.make_async_copy(
                            ref.at[pl.ds((b * n_z + m) * rows, rows), pl.ds(first, cols)],
                            into.at[pl.ds(pl.multiple_of(slot * rows, rows), rows), lanes],
                            sem,
                        ).start()


def loaded(array, sem):
    pltpu.make_async_copy(array, array, sem).wait()


def qkv_kernel(n_z, at_ref, flag_ref, x_ref, row_ref, bias_ref, *refs):
    pieces, (qkv_ref, low_ref, w_ref, sem) = refs[:-4], refs[-4:]

    @pl.when(pl.program_id(0) == 0)
    def _():
        load(at_ref, pieces, n_z, [(0, w_ref.shape[1] // 2, w_ref, sem)])
        loaded(w_ref, sem)

    embed_low = (x_ref[...].astype(jnp.float32) + dot_rows(flag_ref[...], row_ref[...])).astype(jnp.bfloat16)
    low_ref[...] = embed_low
    out = dot(embed_low, w_ref[...]) + bias_ref[...]
    third = out.shape[1] // 6
    for half in (0, 1):
        at = half * 3 * third
        qkv_ref[half, :, :third] = (out[:, at : at + third] * 0.125).astype(jnp.bfloat16)
        qkv_ref[half, :, third:] = out[:, at + third : at + 3 * third].astype(jnp.bfloat16)


FLAGS = pl.BlockSpec((16, TILE), lambda i, *_: (0, i))


def project(at, flags, x, rows, bias, pieces, n_z):
    count, width = x.shape
    cols = bias.shape[1] // 2
    return call(
        functools.partial(qkv_kernel, n_z),
        (count // TILE,),
        [FLAGS, tiles(width), whole((16, width)), whole((1, 2 * cols))] + [ANY] * len(pieces),
        [pl.BlockSpec((2, TILE, cols), lambda i, *_: (0, i, 0)), tiles(width)],
        [jax.ShapeDtypeStruct((2, count, cols), jnp.bfloat16), jax.ShapeDtypeStruct((count, width), jnp.bfloat16)],
        [pltpu.VMEM((width, 2 * cols), jnp.bfloat16), pltpu.SemaphoreType.DMA],
        4 * count * width * cols,
        1,
        name="project",
    )(at, flags, x, rows, bias, *pieces)


def unpack_kernel(at_ref, packed_ref, rows_ref, bias_ref, b_in_ref):
    n_fsdp = packed_ref.shape[0]
    own = at_ref[2] * 2 + at_ref[3]
    shards = [packed_ref[jnp.bitwise_xor(own, f)] for f in range(n_fsdp)]
    rows = jnp.concatenate([shard[:16] for shard in shards], axis=1)
    rows_ref[...] = rows.astype(jnp.bfloat16)
    split = rows.shape[1] // 2
    zero = jnp.zeros((1, split), jnp.float32)
    cut = [rows[i : i + 1, at : at + split] for at in (0, split) for i in (8, 9)]
    bias_ref[...] = jnp.concatenate([cut[0], zero, cut[1], cut[2], zero, cut[3]], axis=1)
    b_in_ref[...] = jnp.concatenate([shard[i : i + 1] for shard in shards for i in range(10, 14)], axis=1)


def unpack(at, packed, own):
    n_fsdp, _, step = packed.shape
    width = n_fsdp * step
    if step % 32:
        packed = flip_by(packed, 0, own)
        rows = packed.transpose(1, 0, 2).reshape(16, width)
        split = width // 2
        zero = jnp.zeros((split,))
        bias = [p for h in (0, split) for p in (rows[8, h : h + split], zero, rows[9, h : h + split])]
        return rows.astype(jnp.bfloat16), jnp.concatenate(bias)[None], packed[:, 10:14].reshape(1, 4 * width)
    return pl.pallas_call(
        unpack_kernel,
        in_specs=[pl.BlockSpec(memory_space=pltpu.SMEM), pl.BlockSpec(memory_space=pltpu.VMEM)],
        out_specs=[pl.BlockSpec(memory_space=pltpu.VMEM)] * 3,
        out_shape=[
            jax.ShapeDtypeStruct((16, width), jnp.bfloat16),
            jax.ShapeDtypeStruct((1, 3 * width), jnp.float32),
            jax.ShapeDtypeStruct((1, 4 * width), jnp.float32),
        ],
        name="unpack",
    )(at, packed)


def attend_kernel(docs, len_ref, q_ref, k_ref, v_ref, ctx_ref, inv_ref, p_ref):
    seq = q_ref.shape[0] // docs
    lane = lax.broadcasted_iota(jnp.int32, (seq, 128), 1)
    row = lax.broadcasted_iota(jnp.int32, (seq, 128), 0)
    low = lane < 64
    zero, one = jnp.zeros((seq, 128), jnp.bfloat16), jnp.ones((seq, 128), jnp.bfloat16)
    heads = []
    for doc in range(docs):
        here = slice(doc * seq, (doc + 1) * seq)
        query, keys, values = q_ref[here], k_ref[here], v_ref[here]
        unused = jnp.where(row >= len_ref[doc], -1e30, 0.0).astype(jnp.bfloat16)
        for head in (0, 1):
            mine = low if head == 0 else ~low
            spare = lane == 64 - 64 * head
            left = jnp.where(mine, query, jnp.where(spare, one, zero))
            heads.append((left, jnp.where(mine, keys, jnp.where(spare, unused, zero)), jnp.where(mine, values, one)))
    later = dot_cols(*heads[0][:2])
    parts = []
    for i, (_, _, values) in enumerate(heads):
        scores = later
        if i + 1 < len(heads):
            later = dot_cols(*heads[i + 1][:2])
        doc, head = i // 2, i % 2
        expo = jnp.exp(scores - jnp.max(scores, axis=1, keepdims=True)).astype(jnp.bfloat16)
        p_ref[doc, head] = expo
        parts.append(dot(expo, values))
        if head == 1:
            here = slice(doc * seq, (doc + 1) * seq)
            inv = 1.0 / pltpu.roll(jnp.where(low, parts[i], parts[i - 1]), 64, axis=1)
            inv_ref[here] = inv
            ctx_ref[here] = (jnp.where(low, parts[i - 1], parts[i]) * inv).astype(jnp.bfloat16)


def attend(lengths, qkv):
    docs = lengths.shape[0]
    count, cols = qkv.shape[1:]
    seq, n_pair = count // docs, cols // 384

    def part(which):
        return pl.BlockSpec((None, count, 128), lambda i, *_: (i // n_pair, 0, which * n_pair + i % n_pair))

    out = pl.BlockSpec((count, 128), lambda i, *_: (0, i))
    return call(
        functools.partial(attend_kernel, docs),
        (2 * n_pair,),
        [part(0), part(1), part(2)],
        [out, out, pl.BlockSpec((None, None, docs, 2, seq, seq), lambda i, *_: (i // n_pair, i % n_pair, 0, 0, 0, 0))],
        [
            jax.ShapeDtypeStruct((count, 2 * cols // 3), jnp.bfloat16),
            jax.ShapeDtypeStruct((count, 2 * cols // 3), jnp.float32),
            jax.ShapeDtypeStruct((2, n_pair, docs, 2, seq, seq), jnp.bfloat16),
        ],
        flops=2 * docs * n_pair * 2 * seq * seq * 256 * 4,
        prefetch=1,
        name="attend",
    )(lengths, qkv, qkv, qkv)


def norm(resid):
    center = resid - jnp.mean(resid, axis=1, keepdims=True)
    inv = lax.rsqrt(jnp.mean(center * center, axis=1, keepdims=True) + EPSILON)
    return center * inv, inv


def norm_back(grad, normal, inv, gain):
    scaled = grad * gain
    return inv * (
        scaled
        - jnp.mean(scaled, axis=1, keepdims=True)
        - normal * jnp.mean(scaled * normal, axis=1, keepdims=True)
    )


def gelu_parts(u):
    expo = jnp.exp(u * u * -0.5)
    t = 1.0 / (1.0 + STEEP * jnp.abs(u))
    poly = TAIL[5]
    for coef in TAIL[4::-1]:
        poly = poly * t + coef
    tail = expo * (t * poly)
    phi = jnp.where(u >= 0, 1.0 - tail, tail)
    return phi, phi + u * (expo * 0.3989422804014327)


def sum_rows(value):
    return jnp.sum(value, axis=0, keepdims=True)


def start_sums(*refs):
    @pl.when(pl.program_id(0) == 0)
    def _():
        for ref in refs:
            ref[...] = jnp.zeros_like(ref)


def wide_of(rows, *indices):
    rows = rows.astype(jnp.float32)
    return [rows[i : i + 1] for i in indices]


def ffn_kernel(
    n_z,
    n_mid,
    at_ref,
    flag_ref,
    x_ref,
    ctx_ref,
    cot_ref,
    row_ref,
    b_in_ref,
    *refs,
):
    mid, down = refs[:n_mid], refs[n_mid:-15]
    out_ref, low_ref, act_ref, dbranch_ref, dhidden_ref, dattn_ref, dresid_ref, dctx_ref = refs[-15:-7]
    sums_ref, in_sums_ref, wo_ref, wi_ref, wd_ref, slope_ref, sems = refs[-7:]
    first = pl.program_id(0) == 0
    width = x_ref.shape[1]
    chunks = range(0, wi_ref.shape[1], width)

    start_sums(sums_ref, in_sums_ref)

    @pl.when(first)
    def _():
        half = wi_ref.shape[1] // 2
        load(at_ref, mid, n_z, [(half, width // 2, wo_ref, sems.at[0])])
        load(at_ref, mid, n_z, [(0, half, wi_ref, sems.at[1])])
        load(at_ref, down, n_z, [(0, width // 2, wd_ref, sems.at[2])])
        loaded(wo_ref, sems.at[0])
        loaded(wi_ref, sems.at[1])
        loaded(wd_ref, sems.at[2])

    b_out, gain1, shift1, b_down, gain2, shift2 = wide_of(row_ref[...], 2, 3, 4, 5, 6, 7)

    def chain(here):
        flags = flag_ref[:, here]
        embed = x_ref[here].astype(jnp.float32) + dot_rows(flags, row_ref[...])
        resid1 = embed + dot(ctx_ref[here], wo_ref[...]) + b_out
        yield
        normal1, inv1 = norm(resid1)
        normed = normal1 * gain1 + shift1
        normed_low = normed.astype(jnp.bfloat16)
        low_ref[here] = normed_low
        branch = normed + b_down
        yield
        for at in chunks:
            cols = slice(at, at + width)
            hidden = dot(normed_low, wi_ref[:, cols]) + b_in_ref[:, cols]
            phi, slope = gelu_parts(hidden)
            slope_ref[here, cols] = slope
            activated = (hidden * phi).astype(jnp.bfloat16)
            act_ref[here, cols] = activated
            branch = branch + dot(activated, wd_ref[cols, :])
            yield
        normal2, inv2 = norm(branch)
        out_ref[here] = (normal2 * gain2 + shift2).astype(jnp.bfloat16)
        grad = cot_ref[here].astype(jnp.float32)
        dresid2 = norm_back(grad, normal2, inv2, gain2)
        dbranch = dresid2.astype(jnp.bfloat16)
        dbranch_ref[here] = dbranch
        sums_ref[0:1] += sum_rows(grad * normal2)
        sums_ref[1:2] += sum_rows(grad)
        sums_ref[2:3] += sum_rows(dbranch.astype(jnp.float32))
        dnormed = dresid2
        yield
        for at in chunks:
            cols = slice(at, at + width)
            dhidden = (dot_cols(dbranch, wd_ref[cols, :]) * slope_ref[here, cols]).astype(jnp.bfloat16)
            dhidden_ref[here, cols] = dhidden
            in_sums_ref[0:1, cols] += sum_rows(dhidden.astype(jnp.float32))
            dnormed = dnormed + dot_cols(dhidden, wi_ref[:, cols])
            yield
        dresid1 = norm_back(dnormed, normal1, inv1, gain1)
        dattn = dresid1.astype(jnp.bfloat16)
        dresid_ref[here] = dresid1
        dattn_ref[here] = dattn
        sums_ref[3:4] += sum_rows(dnormed * normal1)
        sums_ref[4:5] += sum_rows(dnormed)
        sums_ref[5:6] += sum_rows(dattn.astype(jnp.float32))
        rest = (dresid1 - dattn.astype(jnp.float32)).astype(jnp.bfloat16)
        sums_ref[8:24] += dot(flags, dattn) + dot(flags, rest)
        yield
        dctx_ref[here] = dot_cols(dattn, wo_ref[...]).astype(jnp.bfloat16)

    count = x_ref.shape[0] // PART
    running = [chain(slice(i * PART, (i + 1) * PART)) for i in range(count)]
    offset = OFFSET
    step = 0
    while running:
        alive = []
        for number, one in enumerate(running):
            if step >= number * offset and next(one, "end") == "end":
                continue
            alive.append(one)
        running = alive
        step += 1


def ffn(at, flags, x, ctx, cot, rows, b_in, mid, down, n_z):
    count, width = x.shape
    ff_width = b_in.shape[1]
    low = jax.ShapeDtypeStruct((count, width), jnp.bfloat16)

    def rows_of(cols):
        return pl.BlockSpec((FFN_TILE, cols), lambda i, *_: (i, 0))

    wide = jax.ShapeDtypeStruct((count, ff_width), jnp.bfloat16)
    return call(
        functools.partial(ffn_kernel, n_z, len(mid)),
        (count // FFN_TILE,),
        [pl.BlockSpec((16, FFN_TILE), lambda i, *_: (0, i))]
        + [rows_of(width)] * 3
        + [whole((16, width)), whole((1, ff_width))]
        + [ANY] * (len(mid) + len(down)),
        [rows_of(width)] * 2
        + [rows_of(ff_width), rows_of(width), rows_of(ff_width)]
        + [rows_of(width)] * 3
        + [whole((24, width)), whole((8, ff_width))],
        [low, low, wide, low, wide, low, jax.ShapeDtypeStruct((count, width), jnp.float32), low]
        + [jax.ShapeDtypeStruct((24, width), jnp.float32), jax.ShapeDtypeStruct((8, ff_width), jnp.float32)],
        [
            pltpu.VMEM((width, width), jnp.bfloat16),
            pltpu.VMEM((width, ff_width), jnp.bfloat16),
            pltpu.VMEM((ff_width, width), jnp.bfloat16),
            pltpu.VMEM((FFN_TILE, ff_width), jnp.float32),
            pltpu.SemaphoreType.DMA((3,)),
        ],
        4 * count * width * (width + 2 * ff_width),
        1,
        name="ffn",
    )(at, flags, x, ctx, cot, rows, b_in, *mid, *down)


def split_sum(at_ref, grad, got_ref, away_ref, stay_ref, sum_ref, lanes):
    sum_ref[:, lanes] = (grad + got_ref[:, lanes].astype(jnp.float32)).astype(jnp.bfloat16)
    y, c, x = at_ref[0], jnp.bitwise_xor(at_ref[1], at_ref[2] % 2), at_ref[3]
    rows = away_ref.shape[2]
    for z in range(away_ref.shape[0]):
        for b in (0, 1):
            for ref, this_x, this_y in ((away_ref, 1 - x, 1 - y), (stay_ref, x, y)):
                block = jnp.where(c == 0, this_x * 2 + b, b * 2 + this_y) + z * 4
                ref[z, b, :, lanes] = sum_ref[pl.ds(pl.multiple_of(block * rows, rows), rows), lanes]


def grad_kernel(n_first, first_z, at_ref, *refs):
    *lefts, got_ref, away_ref, stay_ref, sum_ref = refs if first_z else (*refs[:-1], None, None, refs[-1], None)
    step = pl.program_id(0)

    def put(left_ref, right_ref):
        grad = dot_rows(left_ref[...], right_ref[...])
        lanes = slice(0, grad.shape[1])
        if not first_z:
            stay_ref[:, lanes] = grad.astype(jnp.bfloat16)
            return
        split_sum(at_ref, grad, got_ref, away_ref, stay_ref, sum_ref, lanes)

    if len(lefts) == 2:
        put(*lefts)
        return
    pl.when(step < n_first)(lambda: put(lefts[0], lefts[1]))
    pl.when(step >= n_first)(lambda: put(lefts[2], lefts[3]))


def grads(at, half, parts, got, n_z, tile, name):
    count, rows = parts[0][0].shape
    width = sum(cols for _, _, cols in parts)
    tall = rows > 2 * width
    n_first = (rows if tall else parts[0][2]) // tile
    steps = n_first + len(parts) - 1
    specs, arrays = [], []
    for left, right, cols in parts:
        if tall:
            specs += [pl.BlockSpec((count, tile), lambda i, *_: (0, i))]
            specs += [pl.BlockSpec((count, cols), lambda i, at_ref: (0, at_ref[4]))]
        else:
            n_tile = max(cols // tile, 1)
            start = n_tile if right.shape[1] > cols else 0
            specs += [
                whole((count, rows)),
                pl.BlockSpec(
                    (count, min(tile, cols)),
                    lambda i, at_ref, n=n_tile, start=start: (0, at_ref[4] * start + jnp.minimum(i, n - 1)),
                ),
            ]
        arrays += [left, right]
    at = jnp.concatenate([at, half])
    block = rows // (4 * n_z)
    shape = (tile, width) if tall else (rows, tile)
    spec = pl.BlockSpec(shape, (lambda i, *_: (i, 0)) if tall else (lambda i, *_: (0, i)))
    flops = 2 * count * rows * width
    plain = functools.partial(grad_kernel, n_first, False)
    fused = got is not None and block % 16 == 0
    if not fused:
        grad = call(
            plain, (steps,), specs, spec, jax.ShapeDtypeStruct((rows, width), jnp.bfloat16), flops=flops, prefetch=1, name=name
        )(at, *arrays)
        if got is None:
            return grad
        stay, away = sum_core(grad, got, at, n_z)
        return away, stay
    by_z = shape[0] // (4 * block)
    split = pl.BlockSpec(
        (by_z, 2, block, shape[1]), (lambda i, *_: (i, 0, 0, 0)) if tall else (lambda i, *_: (0, 0, 0, i))
    )
    return call(
        functools.partial(grad_kernel, n_first, True),
        (steps,),
        specs + [spec],
        [split] * 2,
        [jax.ShapeDtypeStruct((n_z, 2, block, width), jnp.bfloat16)] * 2,
        [pltpu.VMEM(shape, jnp.bfloat16)],
        flops=flops,
        prefetch=1,
        name=name,
    )(at, *arrays, got)


def attend_back_kernel(
    docs, fused, at_ref, q_ref, k_ref, v_ref, ctx_ref, inv_ref, p_ref, dctx_ref, low_ref, flag_ref, *refs
):
    got_ref, out_ref, sums_ref, *grads_ref = refs if fused else (None, *refs)
    pair = pl.program_id(0)
    seq = q_ref.shape[0] // docs
    third = out_ref.shape[1] // 3
    lane = lax.broadcasted_iota(jnp.int32, (seq, 128), 1)
    low = lane < 64
    zero, one = jnp.zeros((seq, 128), jnp.bfloat16), jnp.ones((seq, 128), jnp.bfloat16)
    for doc in range(docs):
        here = slice(doc * seq, (doc + 1) * seq)
        query, keys, values = q_ref[here], k_ref[here], v_ref[here]
        dctx = (dctx_ref[here].astype(jnp.float32) * inv_ref[here]).astype(jnp.bfloat16)
        product = dctx.astype(jnp.float32) * ctx_ref[here].astype(jnp.float32)
        grads = []
        for head in (0, 1):
            mine = low if head == 0 else ~low
            spare = lane == 64 - 64 * head
            fine = lane == 65 - 64 * head
            delta = jnp.sum(jnp.where(mine, product, 0.0), axis=1, keepdims=True)
            coarse = delta.astype(jnp.bfloat16)
            rest = (delta - coarse.astype(jnp.float32)).astype(jnp.bfloat16)
            left = jnp.where(mine, dctx, jnp.where(spare, -coarse, jnp.where(fine, -rest, zero)))
            expo = p_ref[doc, head]
            dprobs = dot_cols(left, jnp.where(mine, values, jnp.where(spare | fine, one, zero)))
            dscores = (expo.astype(jnp.float32) * dprobs).astype(jnp.bfloat16)
            grads.append((dot(dscores, keys) * 0.125, dot_rows(dscores, query), dot_rows(expo, dctx)))
        for which in range(3):
            grad = jnp.where(low, grads[0][which], grads[1][which]).astype(jnp.bfloat16)
            out_ref[here, pl.ds(pl.multiple_of(which * third + pair * 128, 128), 128)] = grad

    @pl.when(pair == pl.num_programs(0) - 1)
    def _():
        sums_ref[...] = dot(flag_ref[...], out_ref[...])
        grad = dot_rows(low_ref[...], out_ref[...])
        if fused:
            split_sum(at_ref, grad, got_ref, *grads_ref, slice(0, 3 * third))
        else:
            grads_ref[0][...] = grad.astype(jnp.bfloat16)


def attend_back(at, half, docs, qkv, ctx, inv, expo, dctx, low, flags, got, n_z):
    count, cols = qkv.shape[1:]
    seq, n_pair = count // docs, cols // 384
    rows = low.shape[1]

    def part(which):
        return pl.BlockSpec((None, count, 128), lambda i, at_ref: (at_ref[4], 0, which * n_pair + i))

    one = pl.BlockSpec((count, 128), lambda i, at_ref: (0, at_ref[4] * n_pair + i))
    block = rows // (4 * n_z)
    fused = got is not None and block % 16 == 0
    shape = (n_z, 2, block, cols) if fused else (rows, cols)
    more = [whole((rows, cols))] if fused else []
    dqkv, sums, *out = call(
        functools.partial(attend_back_kernel, docs, fused),
        (n_pair,),
        [part(0), part(1), part(2), one, one]
        + [pl.BlockSpec((None, None, docs, 2, seq, seq), lambda i, at_ref: (at_ref[4], i, 0, 0, 0, 0)), one]
        + [whole((count, rows)), whole((16, count))]
        + more,
        [whole((count, cols)), whole((16, cols))] + [whole(shape)] * (2 if fused else 1),
        [jax.ShapeDtypeStruct((count, cols), jnp.bfloat16), jax.ShapeDtypeStruct((16, cols), jnp.float32)]
        + [jax.ShapeDtypeStruct(shape, jnp.bfloat16)] * (2 if fused else 1),
        [pltpu.VMEM((rows, cols), jnp.bfloat16)] if fused else (),
        flops=docs * n_pair * 2 * seq * seq * 256 * 10 + 2 * count * rows * cols,
        prefetch=1,
        name="attend_back",
    )(jnp.concatenate([at, half]), qkv, qkv, qkv, ctx, inv, expo, dctx, low, flags, *([got] if fused else []))
    if got is None or fused:
        return dqkv, sums, *out
    stay, away = sum_core(out[0], got, at, n_z)
    return dqkv, sums, away, stay


def embed_grad_kernel(n_z, side, at_ref, before_ref, dqkv_ref, *refs):
    pieces, (out_ref, w_ref, sem) = refs[:-3], refs[-3:]

    @pl.when(pl.program_id(0) == 0)
    def _():
        load(at_ref, pieces, n_z, [(0, w_ref.shape[1], w_ref, sem)], (side,))
        loaded(w_ref, sem)

    out_ref[...] = (before_ref[...] + dot_cols(dqkv_ref[...], w_ref[...])).astype(out_ref.dtype)


def embed_grad(at, before, dqkv, side, pieces, n_z, dtype):
    count, width = before.shape
    cols = dqkv.shape[1]
    return call(
        functools.partial(embed_grad_kernel, n_z, side),
        (count // TILE,),
        [tiles(width), tiles(cols)] + [ANY] * len(pieces),
        tiles(width),
        jax.ShapeDtypeStruct((count, width), dtype),
        [pltpu.VMEM((width, cols), jnp.bfloat16), pltpu.SemaphoreType.DMA],
        2 * count * width * cols,
        1,
        name="embed_grad",
    )(at, before, dqkv, *pieces)


def pack_kernel(at_ref, sums_ref, in_ref, mine_ref, theirs_ref, out_ref):
    core = at_ref[1]
    width = sums_ref.shape[1]
    split = width // 2
    mine, theirs = mine_ref[...], theirs_ref[...]
    low, high = jnp.where(core == 0, mine, theirs), jnp.where(core == 0, theirs, mine)
    out_ref[...] = jnp.zeros_like(out_ref)
    places = [(0, 15, 0), (1, 15, 2)] + [(16 + 3 * flag + part, flag, part) for flag in (0, 1) for part in range(3)]
    for row, flag, part in places:
        cols = slice(part * split, (part + 1) * split)
        out_ref[row : row + 1, :split] = low[flag : flag + 1, cols]
        out_ref[row : row + 1, split:] = high[flag : flag + 1, cols]
    for row, source in enumerate((5, 3, 4, 8, 9, 2, 0, 1), 2):
        out_ref[row : row + 1, :] = sums_ref[source : source + 1, :]
    for i in range(4):
        out_ref[11 + i : 12 + i, :] = in_ref[0:1, i * width : (i + 1) * width]


def pack(at, sums, in_sums, mine, theirs):
    return pl.pallas_call(
        pack_kernel,
        in_specs=[pl.BlockSpec(memory_space=pltpu.SMEM)] + [pl.BlockSpec(memory_space=pltpu.VMEM)] * 4,
        out_specs=pl.BlockSpec(memory_space=pltpu.VMEM),
        out_shape=jax.ShapeDtypeStruct((24, sums.shape[1]), jnp.float32),
        name="pack",
    )(at, sums, in_sums, mine, theirs)


def body(
    layer_input,
    masked,
    replaced,
    lengths,
    w_qkv,
    b_q,
    b_v,
    w_out,
    b_out,
    gain1,
    shift1,
    mask_vec,
    repl_vec,
    w_in,
    b_in,
    w_down,
    b_down,
    gain2,
    shift2,
    cotangent,
):
    doc_count, seq_len, width = layer_input.shape
    tok_count = doc_count * seq_len
    n_fsdp = lax.axis_size("fsdp")
    n_z = n_fsdp // 2
    wires = wiring(n_fsdp)
    rep, own = lax.axis_index("rep"), lax.axis_index("fsdp")
    at = jnp.stack([rep // 2, rep % 2, own // 2, own % 2]).astype(jnp.int32)
    y, c = at[0], at[1]
    ff_width = w_in.shape[1]
    split = width // 2
    step = width // n_fsdp

    def quarter(weight):
        rows, cols = weight.shape[0] // 2, weight.shape[1] // 2
        return lax.dynamic_slice(weight, (y * rows, c * cols), (rows, cols))

    vectors = jnp.stack((mask_vec, repl_vec, b_out, gain1, shift1, b_down, gain2, shift2, b_q, b_v))
    packed = jnp.concatenate([vectors, b_in.reshape(-1, step), jnp.zeros((2, step), b_in.dtype)])
    packed = packed.astype(jnp.float32)[None]
    first_attn = jnp.concatenate([quarter(w_qkv[:, i * width : (i + 1) * width]) for i in range(3)], axis=1)
    first_mid = jnp.concatenate([quarter(w_in), quarter(w_out)], axis=1)
    first_down = quarter(w_down)

    attn = gather_z(first_attn, wires)
    attn, packed = tie(attn, packed)
    got_attn = send(attn, wires["first"])
    packed = gather_z(grow(packed, send(packed, wires["x"])), wires)
    got_attn, first_mid, packed = tie(got_attn, first_mid, packed)
    rows, bias, b_in = unpack(at, packed, own)
    flags = jnp.stack([masked.reshape(tok_count), replaced.reshape(tok_count)]).astype(jnp.bfloat16)
    flags = jnp.concatenate([flags, jnp.zeros((13, tok_count), jnp.bfloat16), jnp.ones((1, tok_count), jnp.bfloat16)])
    x = layer_input.reshape(tok_count, width)
    cot = cotangent.reshape(tok_count, width)
    attn = grow(attn, got_attn)
    got_attn = send(attn, wires["second"])
    mid = gather_z(first_mid, wires)
    mid, got_attn, first_down, rows = tie(mid, got_attn, first_down, rows)
    got_mid = send(mid, wires["first"])
    pieces = (attn, got_attn, send(attn, wires["core"]), send(got_attn, wires["core"]))
    got_down = send_all([first_down] * (n_z - 1), wires["z"])
    got_mid, got_down, rows = tie(got_mid, got_down, rows)
    mid = grow(mid, got_mid)
    down = jnp.concatenate([first_down] + got_down)
    rows, mid, down = tie(rows, mid, down)
    got_mid = send(mid, wires["second"])
    got_down = send(down, wires["first"])
    own_attn, other_attn = pieces_of(*pieces, at, n_z)
    w_attn = own_attn + other_attn

    qkv, embed_low = project(at, flags, x, rows, bias, w_attn, n_z)
    qkv, got_down = tie(qkv, got_down)
    down = grow(down, got_down)
    qkv, down = tie(qkv, down)
    got_down = send(down, wires["second"])
    other_mid = send(mid, wires["core"])
    other_down = send(down, wires["core"])
    ctx, inv, expo = attend(lengths, qkv)
    ctx, got_mid, got_down, other_mid, other_down = tie(ctx, got_mid, got_down, other_mid, other_down)
    w_mid = sum(pieces_of(mid, got_mid, other_mid, send(got_mid, wires["core"]), at, n_z), ())
    w_back = sum(pieces_of(down, got_down, other_down, send(got_down, wires["core"]), at, n_z), ())
    out, normed_low, activated, dbranch, dhidden, dattn, dresid1, dctx, sums, in_sums = ffn(
        at, flags, x, ctx, cot, rows, b_in, w_mid, w_back, n_z
    )

    mine, theirs = c[None], 1 - c[None]
    part_d = [(activated, dbranch, split)]
    part_m = [(normed_low, dhidden, ff_width // 2), (ctx, dattn, split)]
    give_m = grads(at, theirs, part_m, None, n_z, width, "mid_give")
    activated, give_m = tie(activated, give_m)
    part_d = [(activated, dbranch, split)]
    got_m = send(give_m, wires["core"])
    give_d = grads(at, theirs, part_d, None, n_z, width, "down_give")
    got_m, give_d = tie(got_m, give_d)
    got_d = send(give_d, wires["core"])
    give_m, keep_m = grads(at, mine, part_m, got_m, n_z, width, "mid_keep")
    give_m, got_d = tie(give_m, got_d)
    got_m = send(give_m, wires["second"])
    give_d, keep_d = grads(at, mine, part_d, got_d, n_z, width, "down_keep")
    give_d, dctx = tie(give_d, dctx)
    got_d = send(give_d, wires["second"])
    dqkv_theirs, sums_theirs, give_a = attend_back(
        at, theirs, doc_count, qkv, ctx, inv, expo, dctx, embed_low, flags, None, n_z
    )
    got_d, got_m, give_a = tie(got_d, got_m, give_a)
    keep_m, give_m = sum_second(keep_m, got_m, at)
    keep_d, give_d = sum_second(keep_d, got_d, at)
    give_m, give_d, give_a, dqkv_theirs = tie(give_m, give_d, give_a, dqkv_theirs)
    got_m = send(give_m, wires["first"])
    got_a = send(give_a, wires["core"])
    dembed = embed_grad(at, dresid1, dqkv_theirs, 1, other_attn, n_z, jnp.float32)
    got_m, got_a, dembed = tie(got_m, got_a, dembed)
    keep_m, give_m = sum_first(keep_m, got_m, at)
    give_m, give_d, got_a = tie(give_m, give_d, got_a)
    got_m = send_all(give_m, wires["z"])
    got_d = send(give_d, wires["first"])
    dqkv_mine, sums_mine, give_a, keep_a = attend_back(
        at, mine, doc_count, qkv, ctx, inv, expo, dctx, embed_low, flags, got_a, n_z
    )
    got_d, got_m, give_a = tie(got_d, got_m, give_a)
    got_a = send(give_a, wires["second"])
    keep_d, give_d = sum_first(keep_d, got_d, at)
    packed = pack(at, sums, in_sums, sums_mine, sums_theirs)
    give_d, packed, dqkv_mine = tie(give_d, packed, dqkv_mine)
    got_d = send_all(give_d, wires["z"])
    got = send(packed, wires["x"])
    grad_input = embed_grad(at, dembed, dqkv_mine, 0, own_attn, n_z, jnp.bfloat16)
    owned_m = sum_z(keep_m, got_m)
    got_a, got_d, got, grad_input, owned_m = tie(got_a, got_d, got, grad_input, owned_m)
    keep_a, give_a = sum_second(keep_a, got_a, at)
    packed = packed + got
    give_a, packed, got_d = tie(give_a, packed, got_d)
    got_a = send(give_a, wires["first"])
    got_m = send(owned_m, wires["rep"][1])
    for pairs in wires["z_bits"]:
        packed = packed + send(packed, pairs)
    owned_d = sum_z(keep_d, got_d)
    got_a, got_m, packed, owned_d = tie(got_a, got_m, packed, owned_d)
    keep_a, give_a = sum_first(keep_a, got_a, at)
    give_a, packed, owned_d = tie(give_a, packed, owned_d)
    got_a = send_all(give_a, wires["z"])
    got_d = send(owned_d, wires["rep"][1])
    pair_m = jnp.stack([owned_m, got_m])
    for pairs in (wires["rep"][1], wires["core"]):
        packed = packed + send(packed, pairs)
    got_a, got_d, packed, pair_m = tie(got_a, got_d, packed, pair_m)
    owned_a = sum_z(keep_a, got_a)
    owned_a, packed, got_d, pair_m = tie(owned_a, packed, got_d, pair_m)
    got_a = send_all([owned_a] * 3, wires["rep"])
    pair_d = jnp.stack([owned_d, got_d])
    got_m = send(pair_m, wires["core"])
    got_d = send(pair_d, wires["core"])
    o_small = lax.dynamic_slice(packed, (0, own * step), (16, step))
    o_b_in = lax.dynamic_slice(packed[11:15].reshape(ff_width), (own * (ff_width // n_fsdp),), (ff_width // n_fsdp,))
    through = packed[16:22].reshape(2, 3 * width)
    coarse = through.astype(jnp.bfloat16)
    rest = (through - coarse.astype(jnp.float32)).astype(jnp.bfloat16)
    through = dot_cols(coarse, w_qkv) + dot_cols(rest, w_qkv)
    o_mask, o_repl = o_small[5] + through[0], o_small[6] + through[1]
    o_mid, o_down = blocks_of_pairs(pair_m, got_m, at), blocks_of_pairs(pair_d, got_d, at)
    o_attn = blocks_of(owned_a, got_a, at)

    def join(blocks, cut=slice(None)):
        return jnp.concatenate([jnp.concatenate([block[:, cut] for block in row], axis=1) for row in blocks])

    o_qkv = jnp.concatenate([join(o_attn, slice(i * split, (i + 1) * split)) for i in (0, 1, 2)], axis=1)
    return (
        out.reshape(layer_input.shape),
        grad_input.reshape(layer_input.shape),
        o_qkv,
        o_small[0],
        o_small[1],
        join(o_mid, slice(ff_width // 2, None)),
        o_small[2],
        o_small[3],
        o_small[4],
        o_mask,
        o_repl,
        join(o_mid, slice(0, ff_width // 2)),
        o_b_in,
        join(o_down),
        o_small[7],
        o_small[8],
        o_small[9],
    )


def solution(mesh):
    return jax.shard_map(
        body,
        mesh=mesh,
        in_specs=(
            P(("rep", "fsdp"), None, None),
            P(("rep", "fsdp"), None),
            P(("rep", "fsdp"), None),
            P(("rep", "fsdp")),
            P("fsdp", None),
            P("fsdp"),
            P("fsdp"),
            P("fsdp", None),
            P("fsdp"),
            P("fsdp"),
            P("fsdp"),
            P("fsdp"),
            P("fsdp"),
            P("fsdp", None),
            P("fsdp"),
            P("fsdp", None),
            P("fsdp"),
            P("fsdp"),
            P("fsdp"),
            P(("rep", "fsdp"), None, None),
        ),
        out_specs=(
            P(("rep", "fsdp"), None, None),
            P(("rep", "fsdp"), None, None),
            P("fsdp", None),
            P("fsdp"),
            P("fsdp"),
            P("fsdp", None),
            P("fsdp"),
            P("fsdp"),
            P("fsdp"),
            P("fsdp"),
            P("fsdp"),
            P("fsdp", None),
            P("fsdp"),
            P("fsdp", None),
            P("fsdp"),
            P("fsdp"),
            P("fsdp"),
        ),
        check_vma=False,
    )
```
